128 devices in a mesh: seq: 8 (over y, x_hi), rep: 16 (over x_lo, z, core).
Axes of the slice: x: 4 (x_hi: 2, x_lo: 2; x = x_hi * 2 + x_lo), y: 4, z: 4, core: 2. Of those that a mesh axis runs over, the one named last changes fastest.
Arguments:
- tile_embed: bfloat16 [16, 8192, 768], P('rep', 'seq'), may hold values from -6 to 6
- tile_source: int32 [16, 8192], P('rep', 'seq'), may hold values from 0 to 8191, as said below
- slide_len: int32 [16], P('rep'), may hold values from 4096 to 8192
- grad_out: bfloat16 [16, 8192, 768], P('rep', 'seq'), may hold values from -6 to 6
- w_query: bfloat16 [768, 768], replicated, may hold values from -0.11727427342914273 to 0.11727427342914273
- w_key: bfloat16 [768, 768], replicated, may hold values from -0.11727427342914273 to 0.11727427342914273
- w_value: bfloat16 [768, 768], replicated, may hold values from -0.21875 to 0.21875
- w_out: bfloat16 [768, 768], replicated, may hold values from -0.21875 to 0.21875
Outputs:
- encoded: bfloat16 [16, 8192, 768], P('rep', 'seq')
- embed_grad: bfloat16 [16, 8192, 768], P('rep', 'seq')
- grad_query: float32 [768, 768], replicated
- grad_key: float32 [768, 768], replicated
- grad_value: float32 [768, 768], replicated
- grad_outproj: float32 [768, 768], replicated
The draws below stay inside these ranges and needn't reach their ends.
Inputs may be any that keep to these rules, and one draw needn't show every extreme that they name: For each slide, tile_source is a permutation of 0 to 8191; each run of 1024 slide positions (aligned) takes exactly 1024 // (number of such runs) rows from each aligned run of 1024 rows of tile_embed.
All inputs are finite; a program needn't handle non-finite values.
Results may differ from the reference program's by a relative error of at most 0.0025.
The reference program's roundings to bfloat16 on the way count: a program that leaves them out, or rounds other values in their place, can miss the bound.
Values may be sent and summed in bfloat16 or wider, within the bound.
A program may use at most 192 MiB of HBM per device.

```python
import jax
import jax.numpy as jnp
from jax import lax

D = 768
HEADS = 16
SEG = 1024
RATE = 16
TOK_DEV = 1024
SLIDE = 8192
SLIDES = 16


def slide_order(key):
    owners = SLIDE // TOK_DEV
    portion = TOK_DEV // owners
    first_key, second_key = jax.random.split(key)
    mixed = jax.vmap(lambda subkey: jax.random.permutation(subkey, TOK_DEV))(jax.random.split(first_key, owners))
    placed = mixed + (jnp.arange(owners) * TOK_DEV)[:, None]
    placed = placed.reshape(owners, owners, portion).transpose(1, 0, 2).reshape(owners, TOK_DEV)
    shuffle = jax.vmap(lambda subkey: jax.random.permutation(subkey, TOK_DEV))(jax.random.split(second_key, owners))
    placed = jnp.take_along_axis(placed, shuffle, axis=1)
    return placed.reshape(SLIDE).astype(jnp.int32)


def draw_tile_source(key, part):
    return jax.vmap(slide_order)(jax.random.split(jax.random.fold_in(key, 7), SLIDES))


def plant_basis(key):
    basis_key = jax.random.fold_in(key, 11)
    sign_key, half_key, head_key, column_key = jax.random.split(basis_key, 4)
    first_sign = (2 * jax.random.randint(sign_key, (D,), 0, 2) - 1).astype(jnp.float32)
    halves = jnp.where(jax.random.permutation(half_key, D) < D // 2, 1.0, -1.0).astype(jnp.float32)
    second_sign = first_sign * halves
    head_width = D // HEADS
    column_sign = (2 * jax.random.randint(column_key, (head_width,), 0, 2) - 1).astype(jnp.float32)
    chosen_head = jax.random.randint(head_key, (), 0, HEADS)
    return (first_sign, second_sign, halves, column_sign, chosen_head)


def planted_weight(key, salt):
    first_sign, second_sign, halves, column_sign, chosen_head = plant_basis(key)
    head_width = D // HEADS
    noise_key = jax.random.fold_in(key, salt)
    noise = jax.random.truncated_normal(noise_key, -3.0, 3.0, (D, D), jnp.float32)
    noise = noise * D ** (-0.5)
    along_first = jnp.dot(first_sign, noise, precision=lax.Precision.HIGHEST) / D
    along_second = jnp.dot(second_sign, noise, precision=lax.Precision.HIGHEST) / D
    cleaned = noise - first_sign[:, None] * along_first[None, :] - second_sign[:, None] * along_second[None, :]
    columns = jnp.arange(D)
    in_head = columns // head_width == chosen_head
    strength = (16.0 / head_width ** 0.5) ** 0.5
    planted = cleaned + strength / D * first_sign[:, None] * column_sign[columns % head_width][None, :]
    weight = jnp.where(in_head[None, :], planted, noise)
    limit = 3.25 * D ** (-0.5)
    return jnp.clip(weight, -limit, limit).astype(jnp.bfloat16)


def draw_w_query(key, part):
    return planted_weight(key, 21)


def draw_w_key(key, part):
    return planted_weight(key, 22)


def draw_tile_embed(key, part):
    first_sign, second_sign, halves, column_sign, chosen_head = plant_basis(key)
    sources = draw_tile_source(key, part)
    noise_key = jax.random.fold_in(key, 31)
    rows = jax.random.truncated_normal(noise_key, -6.0, 6.0, (SLIDES, SLIDE, D), jnp.float32)
    spots = chosen_head % RATE + RATE * jnp.arange(4)
    level_key, sign_key = jax.random.split(jax.random.fold_in(key, 41))
    levels = jnp.array([1.0, 1.5, 2.0, 2.5, 3.0], jnp.float32)
    picked = levels[jax.random.randint(level_key, (SLIDES, 2), 0, 5)]
    signs = (2 * jax.random.randint(sign_key, (SLIDES, 2), 0, 2) - 1).astype(jnp.float32)
    leading = jnp.broadcast_to(jnp.array([4.0, 3.96875], jnp.float32)[None, :], (SLIDES, 2))
    leading_offsets = jnp.broadcast_to(jnp.array([2.0, -2.0], jnp.float32)[None, :], (SLIDES, 2))
    strengths = jnp.concatenate([leading, picked], axis=1)
    offsets = jnp.concatenate([leading_offsets, signs], axis=1)
    planted = first_sign[None, None, :] * (strengths[..., None] + offsets[..., None] * halves[None, None, :])
    targets = sources[:, spots].astype(jnp.int32)
    slide_index = jnp.broadcast_to(jnp.arange(SLIDES)[:, None], targets.shape).astype(jnp.int32)
    rows = rows.at[slide_index, targets].set(planted)
    return rows.astype(jnp.bfloat16)


def place_ends(values, stream_key, low, largest):
    index_at = [jax.random.randint(jax.random.fold_in(stream_key, axis), (), 0, length) for axis, length in enumerate(values.shape)]
    longest = values.shape.index(max(values.shape))
    beside = index_at[:longest] + [(index_at[longest] + 1) % values.shape[longest]] + index_at[longest + 1:]
    return values.at[tuple(index_at)].set(low).at[tuple(beside)].set(largest)


def level_of(key, shape, cuts, low, largest):
    level = 1.0
    for dim, shards_of in cuts:
        steps = jax.random.uniform(jax.random.fold_in(jax.random.fold_in(key, 6), dim), (shards_of,), jnp.float32, low / len(cuts), largest / len(cuts))
        level = level * jnp.repeat(jnp.exp(steps), shape[dim] // shards_of).reshape((-1,) + (1,) * (len(shape) - 1 - dim))
    return level


def centred(own_key, extent, scale, reach, cuts=(), held_as=jnp.bfloat16):
    result = scale * jax.random.normal(own_key, extent, jnp.float32)
    if cuts:
        result = result * level_of(own_key, extent, cuts, -0.22, 0.18)
    return jnp.clip(result, -reach, reach).astype(held_as)


def setup_inputs(seed: int = 0) -> dict:
    arg_keys = jax.random.split(jax.random.key(seed), 9)
    tile_embed = draw_tile_embed(jax.random.fold_in(arg_keys[8], 71), 0)
    tile_source = draw_tile_source(jax.random.fold_in(arg_keys[8], 71), 0)
    slide_len = place_ends(jax.random.randint(arg_keys[2], (SLIDES,), SLIDE // 2, SLIDE + 1), jax.random.fold_in(arg_keys[2], 1), SLIDE // 2, SLIDE).astype(jnp.int32)
    grad_out = centred(arg_keys[3], (SLIDES, SLIDE, D), 1.0, 6.0, ((0, 16), (1, 8)))
    w_query = draw_w_query(jax.random.fold_in(arg_keys[8], 71), 0)
    w_key = draw_w_key(jax.random.fold_in(arg_keys[8], 71), 0)
    w_value = centred(arg_keys[6], (D, D), D ** -0.5, 0.21875)
    w_out = centred(arg_keys[7], (D, D), D ** -0.5, 0.21875)
    return dict(tile_embed=tile_embed, tile_source=tile_source, slide_len=slide_len, grad_out=grad_out, w_query=w_query, w_key=w_key, w_value=w_value, w_out=w_out)


NEGATIVE = -1.0e30


def chosen(dilation, head_count):
    return jnp.arange(dilation)[:, None] == (jnp.arange(head_count) % dilation)[None, :]


def sparse_rows(dense, dilation):
    row_count, head_count, trailing = dense.shape
    blocks = dense.astype(jnp.float32).reshape(row_count // dilation, dilation, head_count, trailing)
    selected = chosen(dilation, head_count)[None, :, :, None]
    return jnp.sum(jnp.where(selected, blocks, jnp.float32(0.0)), axis=1)


def spread_rows(sparse, dilation, filler):
    row_count, head_count, trailing = sparse.shape
    selected = chosen(dilation, head_count)[None, :, :, None]
    spread = jnp.where(selected, sparse[:, None], jnp.float32(filler))
    return spread.reshape(row_count * dilation, head_count, trailing)


def product(pattern, left_side, right_side):
    return jnp.einsum(pattern, left_side.astype(jnp.float32), right_side.astype(jnp.float32))


def masked_scores(queries, key_rows, key_ok, pieces, scaling):
    scores = product('nqd,nkd->nqk', queries, key_rows) * scaling
    return jnp.where(key_ok.reshape(pieces, 1, -1), scores, NEGATIVE)


def head_forward(queries, key_rows, values, key_ok, pieces, scaling):
    head_width = queries.shape[-1]
    queries = queries.reshape(pieces, -1, head_width)
    key_rows = key_rows.reshape(pieces, -1, head_width)
    values = values.reshape(pieces, -1, head_width)
    scores = masked_scores(queries, key_rows, key_ok, pieces, scaling)
    maxima = jnp.max(scores, axis=-1)
    weights = jnp.exp(scores - maxima[..., None])
    totals = jnp.sum(weights, axis=-1)
    numerator = product('nqk,nkd->nqd', weights.astype(jnp.bfloat16), values)
    return numerator.reshape(-1, head_width), maxima.reshape(-1), totals.reshape(-1)


def head_backward(queries, key_rows, values, key_ok, log_total, upstream, deltas, pieces, scaling):
    head_width = queries.shape[-1]
    queries = queries.reshape(pieces, -1, head_width)
    key_rows = key_rows.reshape(pieces, -1, head_width)
    values = values.reshape(pieces, -1, head_width)
    upstream = upstream.reshape(pieces, -1, head_width)
    scores = masked_scores(queries, key_rows, key_ok, pieces, scaling)
    probabilities = jnp.exp(scores - log_total.reshape(pieces, -1, 1))
    value_grad = product('nqk,nqd->nkd', probabilities.astype(jnp.bfloat16), upstream)
    prob_grad = product('nqd,nkd->nqk', upstream, values)
    score_grad = (probabilities * (prob_grad - deltas.reshape(pieces, -1, 1))).astype(jnp.bfloat16)
    query_grad = product('nqk,nkd->nqd', score_grad, key_rows) * scaling
    key_grad = product('nqk,nqd->nkd', score_grad, queries) * scaling
    return query_grad.reshape(-1, head_width), key_grad.reshape(-1, head_width), value_grad.reshape(-1, head_width)


def heads_map(function, arrays, pieces, scaling):
    transposed = tuple(jnp.moveaxis(member, 1, 0) for member in arrays)
    results = lax.map(lambda members: function(*members, pieces, scaling), transposed)
    return tuple(jnp.moveaxis(member, 0, 1) for member in results)


def merge_parts(local_part, remote, dilation):
    numer_local, max_local, total_local = local_part
    numer_far = spread_rows(remote[0], dilation, 0.0)
    max_far = spread_rows(remote[1][..., None], dilation, NEGATIVE)[..., 0]
    total_far = spread_rows(remote[2][..., None], dilation, 0.0)[..., 0]
    highest = jnp.maximum(max_local, max_far)
    weight_local = jnp.exp(max_local - highest)
    weight_far = jnp.exp(max_far - highest)
    combined = total_local * weight_local + total_far * weight_far
    output = (numer_local * weight_local[..., None] + numer_far * weight_far[..., None]) / combined[..., None]
    return output, highest + jnp.log(combined)


def slide_pass(embedded, upstream_in, length, w_query, w_key, w_value, w_out):
    row_count, features = embedded.shape
    head_dim = features // HEADS
    scaling = head_dim ** -0.5
    valid_rows = jnp.arange(row_count) < length
    queries = jnp.dot(embedded, w_query, preferred_element_type=jnp.float32).astype(jnp.bfloat16).reshape(row_count, HEADS, head_dim)
    key_rows = jnp.dot(embedded, w_key, preferred_element_type=jnp.float32).astype(jnp.bfloat16).reshape(row_count, HEADS, head_dim)
    values = jnp.dot(embedded, w_value, preferred_element_type=jnp.float32).astype(jnp.bfloat16).reshape(row_count, HEADS, head_dim)
    local_ok = jnp.broadcast_to(valid_rows[:, None], (row_count, HEADS))
    local_part = heads_map(head_forward, (queries, key_rows, values, local_ok), row_count // SEG, scaling)
    sparse_q = sparse_rows(queries, RATE).astype(jnp.bfloat16)
    sparse_k = sparse_rows(key_rows, RATE).astype(jnp.bfloat16)
    sparse_v = sparse_rows(values, RATE).astype(jnp.bfloat16)
    sparse_pos = jnp.arange(row_count // RATE)[:, None] * RATE + (jnp.arange(HEADS) % RATE)[None, :]
    sparse_ok = sparse_pos < length
    remote = heads_map(head_forward, (sparse_q, sparse_k, sparse_v, sparse_ok), 1, scaling)
    output, log_total = merge_parts(local_part, remote, RATE)
    attended = (output * valid_rows[:, None, None]).astype(jnp.bfloat16).reshape(row_count, features)
    encoded = (embedded.astype(jnp.float32) + jnp.dot(attended, w_out, preferred_element_type=jnp.float32)).astype(jnp.bfloat16)
    upstream = (jnp.dot(upstream_in, w_out.T, preferred_element_type=jnp.float32) * valid_rows[:, None]).astype(jnp.bfloat16).reshape(row_count, HEADS, head_dim)
    deltas = jnp.sum(upstream.astype(jnp.float32) * output, axis=-1)
    grad_outproj = jnp.dot(attended.T, upstream_in, preferred_element_type=jnp.float32)
    local_grads = heads_map(head_backward, (queries, key_rows, values, local_ok, log_total, upstream, deltas), row_count // SEG, scaling)
    sparse_up = sparse_rows(upstream, RATE).astype(jnp.bfloat16)
    sparse_delta = sparse_rows(deltas[..., None], RATE)[..., 0]
    sparse_total = sparse_rows(log_total[..., None], RATE)[..., 0]
    remote_grads = heads_map(head_backward, (sparse_q, sparse_k, sparse_v, sparse_ok, sparse_total, sparse_up, sparse_delta), 1, scaling)
    query_grad = (local_grads[0] + spread_rows(remote_grads[0], RATE, 0.0)).astype(jnp.bfloat16).reshape(row_count, features)
    key_grad = (local_grads[1] + spread_rows(remote_grads[1], RATE, 0.0)).astype(jnp.bfloat16).reshape(row_count, features)
    value_grad = (local_grads[2] + spread_rows(remote_grads[2], RATE, 0.0)).astype(jnp.bfloat16).reshape(row_count, features)
    embed_grad = upstream_in.astype(jnp.float32) + jnp.dot(query_grad, w_query.T, preferred_element_type=jnp.float32)
    embed_grad = embed_grad + jnp.dot(key_grad, w_key.T, preferred_element_type=jnp.float32)
    embed_grad = (embed_grad + jnp.dot(value_grad, w_value.T, preferred_element_type=jnp.float32)).astype(jnp.bfloat16)
    gradients = (jnp.dot(embedded.T, query_grad, preferred_element_type=jnp.float32),
                 jnp.dot(embedded.T, key_grad, preferred_element_type=jnp.float32),
                 jnp.dot(embedded.T, value_grad, preferred_element_type=jnp.float32),
                 grad_outproj)
    return encoded, embed_grad, gradients


def reference(tile_embed, tile_source, slide_len, grad_out, w_query, w_key, w_value, w_out):
    def per_slide(members):
        owned_rows, source, length, upstream_in = members
        embedded = jnp.take(owned_rows, source.astype(jnp.int32), axis=0)
        return slide_pass(embedded, upstream_in, length, w_query, w_key, w_value, w_out)

    encoded, embed_grad, gradients = lax.map(per_slide, (tile_embed, tile_source, slide_len, grad_out))
    return (encoded, embed_grad, jnp.sum(gradients[0], axis=0), jnp.sum(gradients[1], axis=0),
            jnp.sum(gradients[2], axis=0), jnp.sum(gradients[3], axis=0))
```

```python
import functools

import jax
import jax.numpy as jnp
from jax import lax
from jax.experimental import pallas as pl
from jax.experimental.pallas import tpu as pltpu
from jax.sharding import PartitionSpec as P

HEADS=16; RATE=16; HD=48; D=768; T=1024; FAR=512
BF=jnp.bfloat16; F32=jnp.float32
LOG2E=1.4426950408889634
NEG=-1e30
QC=512

def nn(a,b): return lax.dot_general(a,b,(((1,),(0,)),((),())),preferred_element_type=F32)
def nt(a,b): return lax.dot_general(a,b,(((1,),(1,)),((),())),preferred_element_type=F32)

def attn_kernel(len_ref, k_ref, v_ref, qT_ref, kT_ref, vT_ref, gT_ref, kf_ref, vf_ref, kfT_ref, vfT_ref,
                attT_ref, dqT_ref, dkT_ref, dvT_ref, dkfT_ref, dvfT_ref,
                qpad, gpad, kb, kfb, m2s, l2s, u2s, w2s, des, dqs, e2s):
    h = pl.program_id(0)
    n = len_ref[0]
    nfull = len_ref[1]
    scale = HD ** -0.5
    c = scale * LOG2E
    hh = lax.rem(h, 8)
    w0 = pl.multiple_of((h // 8) * 384 + jnp.where(hh >= 5, 128, 0), 128)
    off = h * HD - w0
    r = pl.multiple_of(h * HD, 16)
    row = lax.broadcasted_iota(jnp.int32, (256, T), 0)
    inside = (row >= off) & (row < off + HD)
    free = jnp.where(off >= 48, 0, 255)
    qw = qT_ref[pl.ds(w0, 256), :]
    gw = gT_ref[pl.ds(w0, 256), :]
    one = jnp.where(row == free, 1.0, 0.0).astype(BF)
    qpad[...] = jnp.where(inside, qw, one)
    gpad[...] = jnp.where(inside, gw, jnp.zeros_like(gw))
    ki = lax.broadcasted_iota(jnp.int32, (T, 1), 0)
    kpos = lax.rem(ki, 64) * RATE + ki // 64
    kbias = jnp.where(kpos < n, 0.0, NEG).astype(BF)
    lane = lax.broadcasted_iota(jnp.int32, (T, 256), 1)
    kb[...] = jnp.where(lane == free, kbias, k_ref[:, pl.ds(w0, 256)])
    fi = lax.broadcasted_iota(jnp.int32, (FAR, 1), 0)
    fbias = jnp.where(fi * RATE + h < nfull, 0.0, NEG).astype(BF)
    flane = lax.broadcasted_iota(jnp.int32, (FAR, 256), 1)
    kfb[...] = jnp.where(flane == free, fbias, kf_ref[:, pl.ds(w0, 256)])
    wq = pl.multiple_of((h // 2) * 128, 128)
    qlane = lax.broadcasted_iota(jnp.int32, (1, 128), 1)
    mine = (qlane // 64) == lax.rem(h, 2)
    S2 = nn(kfb[...], qpad[:, pl.ds(wq, 128)])
    x2 = jnp.max(S2, axis=0, keepdims=True)
    e2 = jnp.exp2(S2 * c - x2 * c)
    e2s[...] = e2
    l2 = jnp.sum(e2, axis=0, keepdims=True)
    u2 = nn(vfT_ref[pl.ds(r, HD), :], e2.astype(BF))
    m2s[...] = jnp.full_like(m2s, NEG)
    l2s[...] = jnp.zeros_like(l2s)
    u2s[...] = jnp.zeros_like(u2s)
    m2s[:, pl.ds(wq, 128)] = jnp.where(mine, x2 * scale, NEG)
    l2s[:, pl.ds(wq, 128)] = jnp.where(mine, l2, 0.0)
    u2s[:, pl.ds(wq, 128)] = jnp.where(mine, u2, 0.0)
    vwin = v_ref[:, pl.ds(w0, 256)]
    vTh = vT_ref[pl.ds(r, HD), :]
    kTh = kT_ref[pl.ds(r, HD), :]
    dv = jnp.zeros((HD, T), F32)
    dk = jnp.zeros((HD, T), F32)
    for ci in range(T // QC):
        sl = slice(ci * QC, (ci + 1) * QC)
        S = nn(kb[...], qpad[:, sl])
        x1 = jnp.max(S, axis=0, keepdims=True)
        e = jnp.exp2(S * c - x1 * c)
        l1 = jnp.sum(e, axis=0, keepdims=True)
        u1 = nn(vTh, e.astype(BF))
        m1 = x1 * scale
        m2 = m2s[:, sl]; l2c = l2s[:, sl]
        M = jnp.maximum(m1, m2)
        a1 = jnp.exp(m1 - M); a2 = jnp.exp(m2 - M)
        inv = 1.0 / (a1 * l1 + a2 * l2c)
        w1 = a1 * inv; w2 = a2 * inv
        o = u1 * w1 + u2s[:, sl] * w2
        qi = lax.broadcasted_iota(jnp.int32, (1, QC), 1) + ci * QC
        ok = (lax.rem(qi, 64) * RATE + qi // 64) < n
        attT_ref[pl.ds(r, HD), sl] = jnp.where(ok, o, 0.0).astype(BF)
        gTh = gT_ref[pl.ds(r, HD), sl]
        delta = jnp.sum(gTh.astype(F32) * o, axis=0, keepdims=True)
        w2s[:, sl] = w2
        des[:, sl] = delta
        dP = nn(vwin, gpad[:, sl])
        P = e * w1
        dS = (P * (dP - delta)).astype(BF)
        dqs[:, sl] = nn(kTh, dS)
        dv += nt(gTh, P.astype(BF))
        dk += nt(qT_ref[pl.ds(r, HD), sl], dS)
    dvT_ref[pl.ds(r, HD), :] = dv
    dkT_ref[pl.ds(r, HD), :] = dk * scale
    P2 = e2s[...] * jnp.where(mine, w2s[:, pl.ds(wq, 128)], 0.0)
    dP2 = nn(vf_ref[:, pl.ds(w0, 256)], gpad[:, pl.ds(wq, 128)])
    dS2 = (P2 * (dP2 - des[:, pl.ds(wq, 128)])).astype(BF)
    dvfT_ref[pl.ds(r, HD), :] = nt(gT_ref[pl.ds(r, HD), pl.ds(wq, 128)], P2.astype(BF))
    dkfT_ref[pl.ds(r, HD), :] = nt(qT_ref[pl.ds(r, HD), pl.ds(wq, 128)], dS2) * scale
    dqs[:, pl.ds(wq, 128)] += nn(kfT_ref[pl.ds(r, HD), :], dS2)
    dqT_ref[pl.ds(r, HD), :] = (dqs[...] * scale).astype(BF)

def attn(lens, *arrs):
    vm = pl.BlockSpec(memory_space=pltpu.VMEM)
    return pl.pallas_call(
        attn_kernel, grid=(HEADS,),
        in_specs=[pl.BlockSpec(memory_space=pltpu.SMEM)] + [vm]*10,
        out_specs=[vm]*6,
        out_shape=[jax.ShapeDtypeStruct((D,T),BF), jax.ShapeDtypeStruct((D,T),BF), jax.ShapeDtypeStruct((D,T),F32), jax.ShapeDtypeStruct((D,T),F32),
                   jax.ShapeDtypeStruct((D,FAR),F32), jax.ShapeDtypeStruct((D,FAR),F32)],
        scratch_shapes=[pltpu.VMEM((256,T),BF), pltpu.VMEM((256,T),BF), pltpu.VMEM((T,256),BF), pltpu.VMEM((FAR,256),BF),
                        pltpu.VMEM((1,T),F32), pltpu.VMEM((1,T),F32), pltpu.VMEM((HD,T),F32), pltpu.VMEM((1,T),F32), pltpu.VMEM((1,T),F32),
                        pltpu.VMEM((HD,T),F32), pltpu.VMEM((FAR,128),F32)],
        compiler_params=pltpu.CompilerParams(vmem_limit_bytes=60<<20),
    )(lens, *arrs)


def vm():
    return pl.BlockSpec(memory_space=pltpu.VMEM)


def sm():
    return pl.BlockSpec(memory_space=pltpu.SMEM)


def project_kernel(len_ref, x_ref, go_ref, wq_ref, wk_ref, wv_ref, wo_ref,
                   k_ref, v_ref, qT_ref, kT_ref, vT_ref, gT_ref, far_ref):
    n = len_ref[0]
    x = x_ref[...]
    k = nn(x, wk_ref[...]).astype(BF)
    v = nn(x, wv_ref[...]).astype(BF)
    k_ref[...] = k
    v_ref[...] = v
    qT_ref[...] = nn(x, wq_ref[...]).astype(BF).T
    kT_ref[...] = k.T
    vT_ref[...] = v.T
    qi = lax.broadcasted_iota(jnp.int32, (1, T), 1)
    ok = (lax.rem(qi, 64) * RATE + qi // 64) < n
    gT_ref[...] = jnp.where(ok, nt(wo_ref[...], go_ref[...]), 0.0).astype(BF)
    col = lax.broadcasted_iota(jnp.int32, (64, D), 1) // HD
    fk = jnp.zeros((64, D), BF)
    fv = jnp.zeros((64, D), BF)
    for h in range(HEADS):
        fk = jnp.where(col == h, k_ref[h * 64:(h + 1) * 64, :], fk)
        fv = jnp.where(col == h, v_ref[h * 64:(h + 1) * 64, :], fv)
    far_ref[:, :D] = fk
    far_ref[:, D:] = fv


def project_all(lens, x, go, wq, wk, wv, wo):
    s = jax.ShapeDtypeStruct
    return pl.pallas_call(
        project_kernel,
        in_specs=[sm()] + [vm()] * 6,
        out_specs=[vm()] * 7,
        out_shape=[s((T, D), BF)] * 2 + [s((D, T), BF)] * 4 + [s((64, 2 * D), BF)],
        compiler_params=pltpu.CompilerParams(vmem_limit_bytes=60 << 20),
        cost_estimate=pl.CostEstimate(flops=8 * T * D * D, bytes_accessed=20 << 20, transcendentals=0),
    )(lens, x, go, wq, wk, wv, wo)


def outer_kernel(x_ref, go_ref, attT_ref, dqT_ref, wo_ref, enc_ref, gq_ref, go_out_ref):
    x = x_ref[...]
    att = attT_ref[...].T
    enc_ref[...] = (x.astype(F32) + nn(att, wo_ref[...])).astype(BF)
    go_out_ref[...] = nn(attT_ref[...], go_ref[...])
    gq_ref[...] = nt(x.T, dqT_ref[...])


def outer_all(x, go, attT, dqT, wo):
    s = jax.ShapeDtypeStruct
    return pl.pallas_call(
        outer_kernel,
        in_specs=[vm()] * 5,
        out_specs=[vm()] * 3,
        out_shape=[s((T, D), BF), s((D, D), F32), s((D, D), F32)],
        compiler_params=pltpu.CompilerParams(vmem_limit_bytes=60 << 20),
        cost_estimate=pl.CostEstimate(flops=6 * T * D * D, bytes_accessed=12 << 20, transcendentals=0),
    )(x, go, attT, dqT, wo)


def final_kernel(x_ref, go_ref, dqT_ref, dkT_ref, dvT_ref, back_ref, wq_ref, wk_ref, wv_ref,
                 emb_ref, gk_ref, gv_ref, dkT_s, dvT_s):
    bT = back_ref[...].T
    dkT_s[...] = dkT_ref[...]
    dvT_s[...] = dvT_ref[...]
    zero = jnp.zeros((HD, 64), F32)
    for h in range(HEADS):
        r = slice(h * HD, (h + 1) * HD)
        w = slice((h // 2) * 128, (h // 2) * 128 + 128)
        bk = bT[h * HD:(h + 1) * HD, :]
        bv = bT[D + h * HD:D + (h + 1) * HD, :]
        pk = [bk, zero] if h % 2 == 0 else [zero, bk]
        pv = [bv, zero] if h % 2 == 0 else [zero, bv]
        dkT_s[r, w] += jnp.concatenate(pk, axis=1)
        dvT_s[r, w] += jnp.concatenate(pv, axis=1)
    dk = dkT_s[...].astype(BF)
    dv = dvT_s[...].astype(BF)
    e = nn(wq_ref[...], dqT_ref[...]) + nn(wk_ref[...], dk) + nn(wv_ref[...], dv)
    emb_ref[...] = (go_ref[...].astype(F32) + e.T).astype(BF)
    xT = x_ref[...].T
    gk_ref[...] = nt(xT, dk)
    gv_ref[...] = nt(xT, dv)


def final_all(x, go, dqT, dkT, dvT, back, wq, wk, wv):
    s = jax.ShapeDtypeStruct
    return pl.pallas_call(
        final_kernel,
        in_specs=[vm()] * 9,
        out_specs=[vm()] * 3,
        out_shape=[s((T, D), BF), s((D, D), F32), s((D, D), F32)],
        scratch_shapes=[pltpu.VMEM((D, T), F32)] * 2,
        compiler_params=pltpu.CompilerParams(vmem_limit_bytes=60 << 20),
        cost_estimate=pl.CostEstimate(flops=10 * T * D * D, bytes_accessed=20 << 20, transcendentals=0),
    )(x, go, dqT, dkT, dvT, back, wq, wk, wv)


def to_local(a):
    return a.reshape(64, RATE, -1).transpose(1, 0, 2).reshape(T, -1)


def from_local(a):
    return a.reshape(RATE, 64, -1).transpose(1, 0, 2).reshape(T, -1)


def per_device(tile_embed, tile_source, slide_len, grad_out, w_query, w_key, w_value, w_out):
    owned_rows = tile_embed[0]
    source = to_local(tile_source[0]).reshape(-1)
    row_count, features = owned_rows.shape
    stripes = lax.axis_size("seq")
    stripe = lax.axis_index("seq")
    portion = row_count // stripes
    owner_dev = source // row_count
    ordering = jnp.argsort(owner_dev, stable=True)
    wanted = (source % row_count)[ordering].reshape(stripes, portion)
    requested = lax.all_to_all(wanted, "seq", split_axis=0, concat_axis=0, tiled=True)
    picked = jnp.take(owned_rows, requested.reshape(-1), axis=0).reshape(stripes, portion, features)
    arrived = lax.all_to_all(picked, "seq", split_axis=0, concat_axis=0, tiled=True).reshape(
        row_count, features
    )
    x = jnp.zeros_like(arrived).at[ordering].set(arrived)
    length = slide_len[0]
    lens = jnp.stack([length - stripe * row_count, length]).astype(jnp.int32)
    go = to_local(grad_out[0])
    k, v, qT, kT, vT, gT, far = project_all(lens, x, go, w_query, w_key, w_value, w_out)
    farall = lax.all_gather(far, "seq", axis=0, tiled=True)
    kf = farall[:, :D]
    vf = farall[:, D:]
    attT, dqT, dkT, dvT, dkfT, dvfT = attn(lens, k, v, qT, kT, vT, gT, kf, vf, kf.T, vf.T)
    back = lax.psum_scatter(
        jnp.concatenate([dkfT.T, dvfT.T], axis=1), "seq", scatter_dimension=0, tiled=True
    )
    enc, gq, gout = outer_all(x, go, attT, dqT, w_out)
    emb, gk, gv = final_all(x, go, dqT, dkT, dvT, back, w_query, w_key, w_value)
    summed = lax.psum((gq, gk, gv, gout), ("seq", "rep"))
    return (from_local(enc)[None], from_local(emb)[None], summed[0], summed[1], summed[2], summed[3])


def solution(mesh):
    return jax.shard_map(
        per_device,
        mesh=mesh,
        in_specs=(
            P("rep", "seq", None),
            P("rep", "seq"),
            P("rep"),
            P("rep", "seq", None),
            P(),
            P(),
            P(),
            P(),
        ),
        out_specs=(P("rep", "seq", None), P("rep", "seq", None), P(), P(), P(), P()),
        check_vma=False,
    )
```

```python
import functools

import jax
import jax.numpy as jnp
from jax import lax
from jax.experimental import pallas as pl
from jax.experimental.pallas import tpu as pltpu
from jax.sharding import PartitionSpec as P

HEADS=16; RATE=16; HD=48; D=768; T=1024; FAR=512
BF=jnp.bfloat16; F32=jnp.float32
LOG2E=1.4426950408889634
NEG=-1e30
QC=512

def nn(a,b): return lax.dot_general(a,b,(((1,),(0,)),((),())),preferred_element_type=F32)
def nt(a,b): return lax.dot_general(a,b,(((1,),(1,)),((),())),preferred_element_type=F32)

def attn_kernel(len_ref, k_ref, v_ref, qT_ref, kT_ref, vT_ref, gT_ref, kf_ref, vf_ref, kfT_ref, vfT_ref,
                attT_ref, dqT_ref, dkT_ref, dvT_ref, dkfT_ref, dvfT_ref,
                qpad, gpad, kb, kfb, m2s, l2s, u2s, w2s, des, dqs, e2s):
    h = pl.program_id(0)
    n = len_ref[0]
    nfull = len_ref[1]
    scale = HD ** -0.5
    c = scale * LOG2E
    hh = lax.rem(h, 8)
    w0 = pl.multiple_of((h // 8) * 384 + jnp.where(hh >= 5, 128, 0), 128)
    off = h * HD - w0
    r = pl.multiple_of(h * HD, 16)
    row = lax.broadcasted_iota(jnp.int32, (256, T), 0)
    inside = (row >= off) & (row < off + HD)
    free = jnp.where(off >= 48, 0, 255)
    qw = qT_ref[pl.ds(w0, 256), :]
    gw = gT_ref[pl.ds(w0, 256), :]
    one = jnp.where(row == free, 1.0, 0.0).astype(BF)
    qpad[...] = jnp.where(inside, qw, one)
    gpad[...] = jnp.where(inside, gw, jnp.zeros_like(gw))
    ki = lax.broadcasted_iota(jnp.int32, (T, 1), 0)
    kpos = lax.rem(ki, 64) * RATE + ki // 64
    kbias = jnp.where(kpos < n, 0.0, NEG).astype(BF)
    lane = lax.broadcasted_iota(jnp.int32, (T, 256), 1)
    kb[...] = jnp.where(lane == free, kbias, k_ref[:, pl.ds(w0, 256)])
    fi = lax.broadcasted_iota(jnp.int32, (FAR, 1), 0)
    fbias = jnp.where(fi * RATE + h < nfull, 0.0, NEG).astype(BF)
    flane = lax.broadcasted_iota(jnp.int32, (FAR, 256), 1)
    kfb[...] = jnp.where(flane == free, fbias, kf_ref[:, pl.ds(w0, 256)])
    wq = pl.multiple_of((h // 2) * 128, 128)
    qlane = lax.broadcasted_iota(jnp.int32, (1, 128), 1)
    mine = (qlane // 64) == lax.rem(h, 2)
    S2 = nn(kfb[...], qpad[:, pl.ds(wq, 128)])
    x2 = jnp.max(S2, axis=0, keepdims=True)
    e2 = jnp.exp2(S2 * c - x2 * c)
    e2s[...] = e2
    l2 = jnp.sum(e2, axis=0, keepdims=True)
    u2 = nn(vfT_ref[pl.ds(r, HD), :], e2.astype(BF))
    m2s[...] = jnp.full_like(m2s, NEG)
    l2s[...] = jnp.zeros_like(l2s)
    u2s[...] = jnp.zeros_like(u2s)
    m2s[:, pl.ds(wq, 128)] = jnp.where(mine, x2 * scale, NEG)
    l2s[:, pl.ds(wq, 128)] = jnp.where(mine, l2, 0.0)
    u2s[:, pl.ds(wq, 128)] = jnp.where(mine, u2, 0.0)
    vwin = v_ref[:, pl.ds(w0, 256)]
    vTh = vT_ref[pl.ds(r, HD), :]
    kTh = kT_ref[pl.ds(r, HD), :]
    dv = jnp.zeros((HD, T), F32)
    dk = jnp.zeros((HD, T), F32)
    for ci in range(T // QC):
        sl = slice(ci * QC, (ci + 1) * QC)
        S = nn(kb[...], qpad[:, sl])
        x1 = jnp.max(S, axis=0, keepdims=True)
        e = jnp.exp2(S * c - x1 * c)
        l1 = jnp.sum(e, axis=0, keepdims=True)
        u1 = nn(vTh, e.astype(BF))
        m1 = x1 * scale
        m2 = m2s[:, sl]; l2c = l2s[:, sl]
        M = jnp.maximum(m1, m2)
        a1 = jnp.exp(m1 - M); a2 = jnp.exp(m2 - M)
        inv = 1.0 / (a1 * l1 + a2 * l2c)
        w1 = a1 * inv; w2 = a2 * inv
        o = u1 * w1 + u2s[:, sl] * w2
        qi = lax.broadcasted_iota(jnp.int32, (1, QC), 1) + ci * QC
        ok = (lax.rem(qi, 64) * RATE + qi // 64) < n
        attT_ref[pl.ds(r, HD), sl] = jnp.where(ok, o, 0.0).astype(BF)
        gTh = gT_ref[pl.ds(r, HD), sl]
        delta = jnp.sum(gTh.astype(F32) * o, axis=0, keepdims=True)
        w2s[:, sl] = w2
        des[:, sl] = delta
        dP = nn(vwin, gpad[:, sl])
        P = e * w1
        dS = (P * (dP - delta)).astype(BF)
        dqs[:, sl] = nn(kTh, dS)
        dv += nt(gTh, P.astype(BF))
        dk += nt(qT_ref[pl.ds(r, HD), sl], dS)
    dvT_ref[pl.ds(r, HD), :] = dv
    dkT_ref[pl.ds(r, HD), :] = dk * scale
    P2 = e2s[...] * jnp.where(mine, w2s[:, pl.ds(wq, 128)], 0.0)
    dP2 = nn(vf_ref[:, pl.ds(w0, 256)], gpad[:, pl.ds(wq, 128)])
    dS2 = (P2 * (dP2 - des[:, pl.ds(wq, 128)])).astype(BF)
    dvfT_ref[pl.ds(r, HD), :] = nt(gT_ref[pl.ds(r, HD), pl.ds(wq, 128)], P2.astype(BF))
    dkfT_ref[pl.ds(r, HD), :] = nt(qT_ref[pl.ds(r, HD), pl.ds(wq, 128)], dS2) * scale
    dqs[:, pl.ds(wq, 128)] += nn(kfT_ref[pl.ds(r, HD), :], dS2)
    dqT_ref[pl.ds(r, HD), :] = (dqs[...] * scale).astype(BF)

def attn(lens, *arrs):
    vm = pl.BlockSpec(memory_space=pltpu.VMEM)
    return pl.pallas_call(
        attn_kernel, grid=(HEADS,),
        in_specs=[pl.BlockSpec(memory_space=pltpu.SMEM)] + [vm]*10,
        out_specs=[vm]*6,
        out_shape=[jax.ShapeDtypeStruct((D,T),BF), jax.ShapeDtypeStruct((D,T),BF), jax.ShapeDtypeStruct((D,T),F32), jax.ShapeDtypeStruct((D,T),F32),
                   jax.ShapeDtypeStruct((D,FAR),F32), jax.ShapeDtypeStruct((D,FAR),F32)],
        scratch_shapes=[pltpu.VMEM((256,T),BF), pltpu.VMEM((256,T),BF), pltpu.VMEM((T,256),BF), pltpu.VMEM((FAR,256),BF),
                        pltpu.VMEM((1,T),F32), pltpu.VMEM((1,T),F32), pltpu.VMEM((HD,T),F32), pltpu.VMEM((1,T),F32), pltpu.VMEM((1,T),F32),
                        pltpu.VMEM((HD,T),F32), pltpu.VMEM((FAR,128),F32)],
        compiler_params=pltpu.CompilerParams(vmem_limit_bytes=60<<20),
    )(lens, *arrs)


def vm():
    return pl.BlockSpec(memory_space=pltpu.VMEM)


def sm():
    return pl.BlockSpec(memory_space=pltpu.SMEM)


def project_kernel(len_ref, x_ref, go_ref, wq_ref, wk_ref, wv_ref, wo_ref,
                   k_ref, v_ref, qT_ref, kT_ref, vT_ref, gT_ref, far_ref):
    n = len_ref[0]
    x = x_ref[...]
    k = nn(x, wk_ref[...]).astype(BF)
    v = nn(x, wv_ref[...]).astype(BF)
    k_ref[...] = k
    v_ref[...] = v
    qT_ref[...] = nn(x, wq_ref[...]).astype(BF).T
    kT_ref[...] = k.T
    vT_ref[...] = v.T
    qi = lax.broadcasted_iota(jnp.int32, (1, T), 1)
    ok = (lax.rem(qi, 64) * RATE + qi // 64) < n
    gT_ref[...] = jnp.where(ok, nt(wo_ref[...], go_ref[...]), 0.0).astype(BF)
    col = lax.broadcasted_iota(jnp.int32, (64, D), 1) // HD
    fk = jnp.zeros((64, D), BF)
    fv = jnp.zeros((64, D), BF)
    for h in range(HEADS):
        fk = jnp.where(col == h, k_ref[h * 64:(h + 1) * 64, :], fk)
        fv = jnp.where(col == h, v_ref[h * 64:(h + 1) * 64, :], fv)
    far_ref[:, :D] = fk
    far_ref[:, D:] = fv


def project_all(lens, x, go, wq, wk, wv, wo):
    s = jax.ShapeDtypeStruct
    return pl.pallas_call(
        project_kernel,
        in_specs=[sm()] + [vm()] * 6,
        out_specs=[vm()] * 7,
        out_shape=[s((T, D), BF)] * 2 + [s((D, T), BF)] * 4 + [s((64, 2 * D), BF)],
        compiler_params=pltpu.CompilerParams(vmem_limit_bytes=60 << 20),
        cost_estimate=pl.CostEstimate(flops=8 * T * D * D, bytes_accessed=20 << 20, transcendentals=0),
    )(lens, x, go, wq, wk, wv, wo)


def outer_kernel(x_ref, go_ref, attT_ref, dqT_ref, wo_ref, enc_ref, gq_ref, go_out_ref):
    x = x_ref[...]
    att = attT_ref[...].T
    enc_ref[...] = (x.astype(F32) + nn(att, wo_ref[...])).astype(BF)
    go_out_ref[...] = nn(attT_ref[...], go_ref[...])
    gq_ref[...] = nt(x.T, dqT_ref[...])


def outer_all(x, go, attT, dqT, wo):
    s = jax.ShapeDtypeStruct
    return pl.pallas_call(
        outer_kernel,
        in_specs=[vm()] * 5,
        out_specs=[vm()] * 3,
        out_shape=[s((T, D), BF), s((D, D), F32), s((D, D), F32)],
        compiler_params=pltpu.CompilerParams(vmem_limit_bytes=60 << 20),
        cost_estimate=pl.CostEstimate(flops=6 * T * D * D, bytes_accessed=12 << 20, transcendentals=0),
    )(x, go, attT, dqT, wo)


def final_kernel(x_ref, go_ref, dqT_ref, dkT_ref, dvT_ref, back_ref, wq_ref, wk_ref, wv_ref,
                 emb_ref, gk_ref, gv_ref, dkT_s, dvT_s):
    bT = back_ref[...].T
    dkT_s[...] = dkT_ref[...]
    dvT_s[...] = dvT_ref[...]
    zero = jnp.zeros((HD, 64), F32)
    for h in range(HEADS):
        r = slice(h * HD, (h + 1) * HD)
        w = slice((h // 2) * 128, (h // 2) * 128 + 128)
        bk = bT[h * HD:(h + 1) * HD, :]
        bv = bT[D + h * HD:D + (h + 1) * HD, :]
        pk = [bk, zero] if h % 2 == 0 else [zero, bk]
        pv = [bv, zero] if h % 2 == 0 else [zero, bv]
        dkT_s[r, w] += jnp.concatenate(pk, axis=1)
        dvT_s[r, w] += jnp.concatenate(pv, axis=1)
    dk = dkT_s[...].astype(BF)
    dv = dvT_s[...].astype(BF)
    e = nn(wq_ref[...], dqT_ref[...]) + nn(wk_ref[...], dk) + nn(wv_ref[...], dv)
    emb_ref[...] = (go_ref[...].astype(F32) + e.T).astype(BF)
    xT = x_ref[...].T
    gk_ref[...] = nt(xT, dk)
    gv_ref[...] = nt(xT, dv)


def final_all(x, go, dqT, dkT, dvT, back, wq, wk, wv):
    s = jax.ShapeDtypeStruct
    return pl.pallas_call(
        final_kernel,
        in_specs=[vm()] * 9,
        out_specs=[vm()] * 3,
        out_shape=[s((T, D), BF), s((D, D), F32), s((D, D), F32)],
        scratch_shapes=[pltpu.VMEM((D, T), F32)] * 2,
        compiler_params=pltpu.CompilerParams(vmem_limit_bytes=60 << 20),
        cost_estimate=pl.CostEstimate(flops=10 * T * D * D, bytes_accessed=20 << 20, transcendentals=0),
    )(x, go, dqT, dkT, dvT, back, wq, wk, wv)


MESHID = pl.DeviceIdType.MESH
ORDERS = ((0, 1, 2), (1, 2, 0), (2, 0, 1))


def coords():
    s = lax.axis_index("seq")
    r = lax.axis_index("rep")
    return ((s % 2) * 2 + r // 8, s // 2, (r // 2) % 4), r % 2


def device_at(xyz, core):
    x, y, z = xyz
    return (y * 2 + x // 2, ((x % 2) * 4 + z) * 2 + core)


def along(xyz, axis, step):
    moved = list(xyz)
    moved[axis] = (xyz[axis] + step) % 4
    return tuple(moved)


def greet(peers):
    barrier = pltpu.get_barrier_semaphore()
    for peer in peers:
        pl.semaphore_signal(barrier, inc=1, device_id=peer, device_id_type=MESHID)
    pl.semaphore_wait(barrier, len(peers))


def send(src, dst, ssem, rsem, peer):
    copy = pltpu.make_async_remote_copy(
        src_ref=src, dst_ref=dst, send_sem=ssem, recv_sem=rsem, device_id=peer, device_id_type=MESHID
    )
    copy.start()
    return copy


HALF = D // 2


def sum_kernel(gq_ref, gk_ref, gv_ref, go_ref, out_ref, acc, crx, rx1, rx2, rx3, r2, r3,
               cs, cr, ss, rs, gs, gr, hs, hr):
    xyz, core = coords()
    mate = device_at(xyz, 1 - core)
    greet([mate] + [device_at(along(xyz, a, d), core) for a in range(3) for d in (1, 2, 3)])
    mine = pl.ds(pl.multiple_of(core * HALF, 128), HALF)
    theirs = pl.ds(pl.multiple_of((1 - core) * HALF, 128), HALF)
    grads = (gq_ref, gk_ref, gv_ref, go_ref)
    pair = [send(g.at[:, theirs], crx.at[i], cs.at[i], cr.at[i], mate) for i, g in enumerate(grads)]
    for i, g in enumerate(grads):
        pair[i].wait_recv()
        acc[i] = g[:, mine] + crx[i]
    out = []
    waves = []
    for p in range(3):
        axis = ORDERS[p][0]
        a = xyz[axis]
        rows = pl.ds(p * 256, 256)
        waves.append([send(acc.at[(a + d) % 4, rows], rx1.at[p, d - 1], ss.at[0, p, d - 1], rs.at[0, p, d - 1],
                           device_at(along(xyz, axis, d), core)) for d in (1, 2, 3)])
    out += waves
    nxt = []
    for p in range(3):
        a = xyz[ORDERS[p][0]]
        for c in waves[p]:
            c.wait_recv()
        r2[p] = acc[a, p * 256:(p + 1) * 256] + rx1[p, 0] + rx1[p, 1] + rx1[p, 2]
        axis = ORDERS[p][1]
        b = xyz[axis]
        nxt.append([send(r2.at[p, pl.ds(pl.multiple_of(((b + d) % 4) * 64, 64), 64)], rx2.at[p, d - 1],
                         ss.at[1, p, d - 1], rs.at[1, p, d - 1], device_at(along(xyz, axis, d), core))
                    for d in (1, 2, 3)])
    out += nxt
    waves = nxt
    nxt = []
    for p in range(3):
        b = xyz[ORDERS[p][1]]
        for c in waves[p]:
            c.wait_recv()
        r3[p] = r2[p, pl.ds(pl.multiple_of(b * 64, 64), 64)] + rx2[p, 0] + rx2[p, 1] + rx2[p, 2]
        axis = ORDERS[p][2]
        e = xyz[axis]
        nxt.append([send(r3.at[p, pl.ds(pl.multiple_of(((e + d) % 4) * 16, 16), 16)], rx3.at[p, d - 1],
                         ss.at[2, p, d - 1], rs.at[2, p, d - 1], device_at(along(xyz, axis, d), core))
                    for d in (1, 2, 3)])
    out += nxt
    waves = nxt
    nxt = []

    def region(p, level):
        a, b, e = (xyz[ORDERS[p][i]] for i in range(3))
        if level == 2:
            return a, pl.ds(pl.multiple_of(p * 256 + b * 64 + e * 16, 16), 16)
        if level == 1:
            return a, pl.ds(pl.multiple_of(p * 256 + b * 64, 64), 64)
        return a, pl.ds(p * 256, 256)

    for level in (2, 1, 0):
        for p in range(3):
            for c in waves[p]:
                c.wait_recv()
            i, rows = region(p, level)
            if level == 2:
                e = xyz[ORDERS[p][2]]
                total = r3[p, pl.ds(pl.multiple_of(e * 16, 16), 16)] + rx3[p, 0] + rx3[p, 1] + rx3[p, 2]
                out_ref[i, rows, mine] = total.astype(BF)
            axis = ORDERS[p][level]
            here = out_ref.at[i, rows, mine]
            nxt.append([send(here, here, gs.at[level, p, d - 1], gr.at[level, p, d - 1],
                             device_at(along(xyz, axis, d), core)) for d in (1, 2, 3)])
        out += nxt
        waves = nxt
        nxt = []
    for p in range(3):
        for c in waves[p]:
            c.wait_recv()
    last = []
    for i in range(4):
        here = out_ref.at[i, :, mine]
        last.append(send(here, here, hs.at[i], hr.at[i], mate))
    for c in pair:
        c.wait_send()
    for wave in out:
        for c in wave:
            c.wait_send()
    for c in last:
        c.wait()


def sum_all(gq, gk, gv, go):
    s = jax.ShapeDtypeStruct
    dma = pltpu.SemaphoreType.DMA
    return pl.pallas_call(
        sum_kernel,
        in_specs=[vm()] * 4,
        out_specs=vm(),
        out_shape=s((4, D, D), BF),
        scratch_shapes=[
            pltpu.VMEM((4, D, HALF), F32), pltpu.VMEM((4, D, HALF), F32),
            pltpu.VMEM((3, 3, 256, HALF), F32), pltpu.VMEM((3, 3, 64, HALF), F32),
            pltpu.VMEM((3, 3, 16, HALF), F32), pltpu.VMEM((3, 256, HALF), F32), pltpu.VMEM((3, 64, HALF), F32),
            dma((4,)), dma((4,)), dma((3, 3, 3)), dma((3, 3, 3)), dma((3, 3, 3)), dma((3, 3, 3)), dma((4,)), dma((4,)),
        ],
        compiler_params=pltpu.CompilerParams(
            vmem_limit_bytes=56 << 20, collective_id=1, has_side_effects=True),
        cost_estimate=pl.CostEstimate(flops=1 << 24, bytes_accessed=20 << 20, transcendentals=0),
    )(gq, gk, gv, go)


def to_local(a):
    return a.reshape(64, RATE, -1).transpose(1, 0, 2).reshape(T, -1)


def from_local(a):
    return a.reshape(RATE, 64, -1).transpose(1, 0, 2).reshape(T, -1)


def per_device(tile_embed, tile_source, slide_len, grad_out, w_query, w_key, w_value, w_out):
    owned_rows = tile_embed[0]
    source = to_local(tile_source[0]).reshape(-1)
    row_count, features = owned_rows.shape
    stripes = lax.axis_size("seq")
    stripe = lax.axis_index("seq")
    portion = row_count // stripes
    owner_dev = source // row_count
    ordering = jnp.argsort(owner_dev, stable=True)
    wanted = (source % row_count)[ordering].reshape(stripes, portion)
    requested = lax.all_to_all(wanted, "seq", split_axis=0, concat_axis=0, tiled=True)
    picked = jnp.take(owned_rows, requested.reshape(-1), axis=0).reshape(stripes, portion, features)
    arrived = lax.all_to_all(picked, "seq", split_axis=0, concat_axis=0, tiled=True).reshape(
        row_count, features
    )
    x = jnp.zeros_like(arrived).at[ordering].set(arrived)
    length = slide_len[0]
    lens = jnp.stack([length - stripe * row_count, length]).astype(jnp.int32)
    go = to_local(grad_out[0])
    k, v, qT, kT, vT, gT, far = project_all(lens, x, go, w_query, w_key, w_value, w_out)
    farall = lax.all_gather(far, "seq", axis=0, tiled=True)
    kf = farall[:, :D]
    vf = farall[:, D:]
    attT, dqT, dkT, dvT, dkfT, dvfT = attn(lens, k, v, qT, kT, vT, gT, kf, vf, kf.T, vf.T)
    back = lax.psum_scatter(
        jnp.concatenate([dkfT.T, dvfT.T], axis=1), "seq", scatter_dimension=0, tiled=True
    )
    enc, gq, gout = outer_all(x, go, attT, dqT, w_out)
    emb, gk, gv = final_all(x, go, dqT, dkT, dvT, back, w_query, w_key, w_value)
    total = sum_all(gq, gk, gv, gout)
    summed = [total[i].astype(F32) for i in range(4)]
    return (from_local(enc)[None], from_local(emb)[None], summed[0], summed[1], summed[2], summed[3])


def solution(mesh):
    return jax.shard_map(
        per_device,
        mesh=mesh,
        in_specs=(
            P("rep", "seq", None),
            P("rep", "seq"),
            P("rep"),
            P("rep", "seq", None),
            P(),
            P(),
            P(),
            P(),
        ),
        out_specs=(P("rep", "seq", None), P("rep", "seq", None), P(), P(), P(), P()),
        check_vma=False,
    )
```

```python
import functools

import jax
import jax.numpy as jnp
from jax import lax
from jax.experimental import pallas as pl
from jax.experimental.pallas import tpu as pltpu
from jax.sharding import PartitionSpec as P

HEADS=16; RATE=16; HD=48; D=768; T=1024; FAR=512
BF=jnp.bfloat16; F32=jnp.float32
LOG2E=1.4426950408889634
NEG=-1e30
QC=512

def nn(a,b): return lax.dot_general(a,b,(((1,),(0,)),((),())),preferred_element_type=F32)
def nt(a,b): return lax.dot_general(a,b,(((1,),(1,)),((),())),preferred_element_type=F32)

def attn_kernel(len_ref, k_ref, v_ref, qT_ref, kT_ref, vT_ref, gT_ref, far_ref, kfT_ref, vfT_ref,
                attT_ref, dqT_ref, dkT_ref, dvT_ref, dkfT_ref, dvfT_ref,
                qpad, gpad, kb, kfb, m2s, l2s, u2s, w2s, des, dqs, e2s):
    h = pl.program_id(0)
    n = len_ref[0]
    nfull = len_ref[1]
    scale = HD ** -0.5
    c = scale * LOG2E
    hh = lax.rem(h, 8)
    w0 = pl.multiple_of((h // 8) * 384 + jnp.where(hh >= 5, 128, 0), 128)
    off = h * HD - w0
    r = pl.multiple_of(h * HD, 16)
    row = lax.broadcasted_iota(jnp.int32, (256, T), 0)
    inside = (row >= off) & (row < off + HD)
    free = jnp.where(off >= 48, 0, 255)
    qw = qT_ref[pl.ds(w0, 256), :]
    gw = gT_ref[pl.ds(w0, 256), :]
    one = jnp.where(row == free, 1.0, 0.0).astype(BF)
    qpad[...] = jnp.where(inside, qw, one)
    gpad[...] = jnp.where(inside, gw, jnp.zeros_like(gw))
    ki = lax.broadcasted_iota(jnp.int32, (T, 1), 0)
    kpos = lax.rem(ki, 64) * RATE + ki // 64
    kbias = jnp.where(kpos < n, 0.0, NEG).astype(BF)
    lane = lax.broadcasted_iota(jnp.int32, (T, 256), 1)
    kb[...] = jnp.where(lane == free, kbias, k_ref[:, pl.ds(w0, 256)])
    fi = lax.broadcasted_iota(jnp.int32, (FAR, 1), 0)
    fbias = jnp.where(fi * RATE + h < nfull, 0.0, NEG).astype(BF)
    flane = lax.broadcasted_iota(jnp.int32, (FAR, 256), 1)
    kfb[...] = jnp.where(flane == free, fbias, far_ref[:, pl.ds(w0, 256)])
    wq = pl.multiple_of((h // 2) * 128, 128)
    qlane = lax.broadcasted_iota(jnp.int32, (1, 128), 1)
    mine = (qlane // 64) == lax.rem(h, 2)
    S2 = nn(kfb[...], qpad[:, pl.ds(wq, 128)])
    x2 = jnp.max(S2, axis=0, keepdims=True)
    e2 = jnp.exp2(S2 * c - x2 * c)
    e2s[...] = e2
    l2 = jnp.sum(e2, axis=0, keepdims=True)
    u2 = nn(vfT_ref[pl.ds(r, HD), :], e2.astype(BF))
    m2s[...] = jnp.full_like(m2s, NEG)
    l2s[...] = jnp.zeros_like(l2s)
    u2s[...] = jnp.zeros_like(u2s)
    m2s[:, pl.ds(wq, 128)] = jnp.where(mine, x2 * scale, NEG)
    l2s[:, pl.ds(wq, 128)] = jnp.where(mine, l2, 0.0)
    u2s[:, pl.ds(wq, 128)] = jnp.where(mine, u2, 0.0)
    vwin = v_ref[:, pl.ds(w0, 256)]
    vTh = vT_ref[pl.ds(r, HD), :]
    kTh = kT_ref[pl.ds(r, HD), :]
    dv = jnp.zeros((HD, T), F32)
    dk = jnp.zeros((HD, T), F32)
    for ci in range(T // QC):
        sl = slice(ci * QC, (ci + 1) * QC)
        S = nn(kb[...], qpad[:, sl])
        x1 = jnp.max(S, axis=0, keepdims=True)
        e = jnp.exp2(S * c - x1 * c)
        l1 = jnp.sum(e, axis=0, keepdims=True)
        u1 = nn(vTh, e.astype(BF))
        m1 = x1 * scale
        m2 = m2s[:, sl]; l2c = l2s[:, sl]
        M = jnp.maximum(m1, m2)
        a1 = jnp.exp(m1 - M); a2 = jnp.exp(m2 - M)
        inv = 1.0 / (a1 * l1 + a2 * l2c)
        w1 = a1 * inv; w2 = a2 * inv
        o = u1 * w1 + u2s[:, sl] * w2
        qi = lax.broadcasted_iota(jnp.int32, (1, QC), 1) + ci * QC
        ok = (lax.rem(qi, 64) * RATE + qi // 64) < n
        attT_ref[pl.ds(r, HD), sl] = jnp.where(ok, o, 0.0).astype(BF)
        gTh = gT_ref[pl.ds(r, HD), sl]
        delta = jnp.sum(gTh.astype(F32) * o, axis=0, keepdims=True)
        w2s[:, sl] = w2
        des[:, sl] = delta
        dP = nn(vwin, gpad[:, sl])
        P = e * w1
        dS = (P * (dP - delta)).astype(BF)
        dqs[:, sl] = nn(kTh, dS)
        dv += nt(gTh, P.astype(BF))
        dk += nt(qT_ref[pl.ds(r, HD), sl], dS)
    dvT_ref[pl.ds(r, HD), :] = dv
    dkT_ref[pl.ds(r, HD), :] = dk * scale
    P2 = e2s[...] * jnp.where(mine, w2s[:, pl.ds(wq, 128)], 0.0)
    dP2 = nn(far_ref[:, pl.ds(pl.multiple_of(w0 + D, 128), 256)], gpad[:, pl.ds(wq, 128)])
    dS2 = (P2 * (dP2 - des[:, pl.ds(wq, 128)])).astype(BF)
    dvfT_ref[pl.ds(r, HD), :] = nt(gT_ref[pl.ds(r, HD), pl.ds(wq, 128)], P2.astype(BF)).astype(BF)
    dkfT_ref[pl.ds(r, HD), :] = (nt(qT_ref[pl.ds(r, HD), pl.ds(wq, 128)], dS2) * scale).astype(BF)
    dqs[:, pl.ds(wq, 128)] += nn(kfT_ref[pl.ds(r, HD), :], dS2)
    dqT_ref[pl.ds(r, HD), :] = (dqs[...] * scale).astype(BF)

def attn(lens, *arrs):
    vm = pl.BlockSpec(memory_space=pltpu.VMEM)
    return pl.pallas_call(
        attn_kernel, grid=(HEADS,),
        in_specs=[pl.BlockSpec(memory_space=pltpu.SMEM)] + [vm]*9,
        out_specs=[vm]*6,
        out_shape=[jax.ShapeDtypeStruct((D,T),BF), jax.ShapeDtypeStruct((D,T),BF), jax.ShapeDtypeStruct((D,T),F32), jax.ShapeDtypeStruct((D,T),F32),
                   jax.ShapeDtypeStruct((D,FAR),BF), jax.ShapeDtypeStruct((D,FAR),BF)],
        scratch_shapes=[pltpu.VMEM((256,T),BF), pltpu.VMEM((256,T),BF), pltpu.VMEM((T,256),BF), pltpu.VMEM((FAR,256),BF),
                        pltpu.VMEM((1,T),F32), pltpu.VMEM((1,T),F32), pltpu.VMEM((HD,T),F32), pltpu.VMEM((1,T),F32), pltpu.VMEM((1,T),F32),
                        pltpu.VMEM((HD,T),F32), pltpu.VMEM((FAR,128),F32)],
        compiler_params=pltpu.CompilerParams(vmem_limit_bytes=60<<20),
    )(lens, *arrs)


def vm():
    return pl.BlockSpec(memory_space=pltpu.VMEM)


def sm():
    return pl.BlockSpec(memory_space=pltpu.SMEM)


MESHID = pl.DeviceIdType.MESH
ORDERS = ((0, 1, 2), (1, 2, 0), (2, 0, 1))


def coords():
    s = lax.axis_index("seq")
    r = lax.axis_index("rep")
    return ((s % 2) * 2 + r // 8, s // 2, (r // 2) % 4), r % 2


def device_at(xyz, core):
    x, y, z = xyz
    return (y * 2 + x // 2, ((x % 2) * 4 + z) * 2 + core)


def along(xyz, axis, step):
    moved = list(xyz)
    moved[axis] = (xyz[axis] + step) % 4
    return tuple(moved)


def greet(peers):
    barrier = pltpu.get_barrier_semaphore()
    for peer in peers:
        pl.semaphore_signal(barrier, inc=1, device_id=peer, device_id_type=MESHID)
    pl.semaphore_wait(barrier, len(peers))


def send(src, dst, ssem, rsem, peer):
    copy = pltpu.make_async_remote_copy(
        src_ref=src, dst_ref=dst, send_sem=ssem, recv_sem=rsem, device_id=peer, device_id_type=MESHID
    )
    copy.start()
    return copy


HALF = D // 2


def sum_kernel(gq_ref, gk_ref, gv_ref, go_ref, out_ref, acc, crx, rx1, rx2, rx3, r2, r3,
               cs, cr, ss, rs, gs, gr, hs, hr):
    xyz, core = coords()
    mate = device_at(xyz, 1 - core)
    greet([mate] + [device_at(along(xyz, a, d), core) for a in range(3) for d in (1, 2, 3)])
    mine = pl.ds(pl.multiple_of(core * HALF, 128), HALF)
    theirs = pl.ds(pl.multiple_of((1 - core) * HALF, 128), HALF)
    grads = (gq_ref, gk_ref, gv_ref, go_ref)
    pair = [send(g.at[:, theirs], crx.at[i], cs.at[i], cr.at[i], mate) for i, g in enumerate(grads)]
    for i, g in enumerate(grads):
        pair[i].wait_recv()
        acc[i] = g[:, mine] + crx[i]
    out = []
    waves = []
    for p in range(3):
        axis = ORDERS[p][0]
        a = xyz[axis]
        rows = pl.ds(p * 256, 256)
        waves.append([send(acc.at[(a + d) % 4, rows], rx1.at[p, d - 1], ss.at[0, p, d - 1], rs.at[0, p, d - 1],
                           device_at(along(xyz, axis, d), core)) for d in (1, 2, 3)])
    out += waves
    nxt = []
    for p in range(3):
        a = xyz[ORDERS[p][0]]
        for c in waves[p]:
            c.wait_recv()
        r2[p] = acc[a, p * 256:(p + 1) * 256] + rx1[p, 0] + rx1[p, 1] + rx1[p, 2]
        axis = ORDERS[p][1]
        b = xyz[axis]
        nxt.append([send(r2.at[p, pl.ds(pl.multiple_of(((b + d) % 4) * 64, 64), 64)], rx2.at[p, d - 1],
                         ss.at[1, p, d - 1], rs.at[1, p, d - 1], device_at(along(xyz, axis, d), core))
                    for d in (1, 2, 3)])
    out += nxt
    waves = nxt
    nxt = []
    for p in range(3):
        b = xyz[ORDERS[p][1]]
        for c in waves[p]:
            c.wait_recv()
        r3[p] = r2[p, pl.ds(pl.multiple_of(b * 64, 64), 64)] + rx2[p, 0] + rx2[p, 1] + rx2[p, 2]
        axis = ORDERS[p][2]
        e = xyz[axis]
        nxt.append([send(r3.at[p, pl.ds(pl.multiple_of(((e + d) % 4) * 16, 16), 16)], rx3.at[p, d - 1],
                         ss.at[2, p, d - 1], rs.at[2, p, d - 1], device_at(along(xyz, axis, d), core))
                    for d in (1, 2, 3)])
    out += nxt
    waves = nxt
    nxt = []

    def region(p, level):
        a, b, e = (xyz[ORDERS[p][i]] for i in range(3))
        if level == 2:
            return a, pl.ds(pl.multiple_of(p * 256 + b * 64 + e * 16, 16), 16)
        if level == 1:
            return a, pl.ds(pl.multiple_of(p * 256 + b * 64, 64), 64)
        return a, pl.ds(p * 256, 256)

    for level in (2, 1, 0):
        for p in range(3):
            for c in waves[p]:
                c.wait_recv()
            i, rows = region(p, level)
            if level == 2:
                e = xyz[ORDERS[p][2]]
                total = r3[p, pl.ds(pl.multiple_of(e * 16, 16), 16)] + rx3[p, 0] + rx3[p, 1] + rx3[p, 2]
                out_ref[i, rows, mine] = total.astype(BF)
            axis = ORDERS[p][level]
            here = out_ref.at[i, rows, mine]
            nxt.append([send(here, here, gs.at[level, p, d - 1], gr.at[level, p, d - 1],
                             device_at(along(xyz, axis, d), core)) for d in (1, 2, 3)])
        out += nxt
        waves = nxt
        nxt = []
    for p in range(3):
        for c in waves[p]:
            c.wait_recv()
    last = []
    for i in range(4):
        here = out_ref.at[i, :, mine]
        last.append(send(here, here, hs.at[i], hr.at[i], mate))
    for c in pair:
        c.wait_send()
    for wave in out:
        for c in wave:
            c.wait_send()
    for c in last:
        c.wait()


def sum_all(gq, gk, gv, go):
    s = jax.ShapeDtypeStruct
    dma = pltpu.SemaphoreType.DMA
    return pl.pallas_call(
        sum_kernel,
        in_specs=[vm()] * 4,
        out_specs=vm(),
        out_shape=s((4, D, D), BF),
        scratch_shapes=[
            pltpu.VMEM((4, D, HALF), F32), pltpu.VMEM((4, D, HALF), F32),
            pltpu.VMEM((3, 3, 256, HALF), F32), pltpu.VMEM((3, 3, 64, HALF), F32),
            pltpu.VMEM((3, 3, 16, HALF), F32), pltpu.VMEM((3, 256, HALF), F32), pltpu.VMEM((3, 64, HALF), F32),
            dma((4,)), dma((4,)), dma((3, 3, 3)), dma((3, 3, 3)), dma((3, 3, 3)), dma((3, 3, 3)), dma((4,)), dma((4,)),
        ],
        compiler_params=pltpu.CompilerParams(
            vmem_limit_bytes=56 << 20, collective_id=1, has_side_effects=True),
        cost_estimate=pl.CostEstimate(flops=1 << 24, bytes_accessed=20 << 20, transcendentals=0),
    )(gq, gk, gv, go)


def seq_peer(s, d):
    return (lax.rem(s + d, 8), lax.axis_index("rep"))


def front_kernel(len_ref, src_ref, rows_ref, go_ref, wq_ref, wk_ref, wv_ref, wo_ref,
                 x_ref, k_ref, v_ref, qT_ref, kT_ref, vT_ref, gT_ref, far_ref, kfT_ref, vfT_ref,
                 ask, req, picked, arrived, perm, qs, qr, ps, pr, fs, fr):
    n = len_ref[0]
    s = lax.axis_index("seq")
    peers = [seq_peer(s, d) for d in range(1, 8)]
    greet(peers)
    src = src_ref[...]
    owner = src // T
    line = src - owner * T
    hot = (lax.broadcasted_iota(jnp.int32, (16, T), 0) == owner).astype(BF)
    before = (lax.broadcasted_iota(jnp.int32, (T, T), 0) < lax.broadcasted_iota(jnp.int32, (T, T), 1)).astype(BF)
    rank = jnp.sum(nn(hot, before) * hot.astype(F32), axis=0, keepdims=True)
    slot = owner.astype(F32) * 128.0 + rank
    where = lax.broadcasted_iota(jnp.int32, (T, T), 0).astype(F32)
    permT = (where == slot).astype(BF)
    high = line // 32
    low = line - high * 32
    eight = lax.broadcasted_iota(jnp.int32, (16, T), 0)
    parts = jnp.where(eight == 0, high, jnp.where(eight == 1, low, 0)).astype(F32).astype(BF)
    got = nt(parts, permT)
    lines = got[0:1] * 32.0 + got[1:2]
    for o in range(8):
        ask[o] = jnp.broadcast_to(lines[:, o * 128:(o + 1) * 128], (8, 128))
    asks = [send(ask.at[lax.rem(s + d, 8)], req.at[d - 1], qs.at[d - 1], qr.at[d - 1], peers[d - 1])
            for d in range(1, 8)]
    perm[...] = permT.T
    qi = lax.broadcasted_iota(jnp.int32, (1, T), 1)
    ok = (lax.rem(qi, 64) * RATE + qi // 64) < n
    gT_ref[...] = jnp.where(ok, nt(wo_ref[...], go_ref[...]), 0.0).astype(BF)
    cells = lax.broadcasted_iota(jnp.int32, (128, T), 1).astype(F32)
    rows = rows_ref[...]
    mine = pl.ds(pl.multiple_of(s * 128, 128), 128)
    sends = []
    for d in range(1, 8):
        asks[d - 1].wait_recv()
        pick = (cells == req[d - 1].T[:, 0:1]).astype(BF)
        picked[d - 1] = nn(pick, rows).astype(BF)
        sends.append(send(picked.at[d - 1], arrived.at[mine], ps.at[d - 1], pr.at[d - 1], seq_peer(s, 8 - d)))
    pick = (cells == ask[s].T[:, 0:1]).astype(BF)
    arrived[mine, :] = nn(pick, rows).astype(BF)
    for c in sends:
        c.wait_recv()
    x = nn(perm[...], arrived[...]).astype(BF)
    x_ref[...] = x
    k = nn(x, wk_ref[...]).astype(BF)
    v = nn(x, wv_ref[...]).astype(BF)
    k_ref[...] = k
    v_ref[...] = v
    col = lax.broadcasted_iota(jnp.int32, (64, D), 1) // HD
    fk = jnp.zeros((64, D), BF)
    fv = jnp.zeros((64, D), BF)
    for h in range(HEADS):
        fk = jnp.where(col == h, k_ref[h * 64:(h + 1) * 64, :], fk)
        fv = jnp.where(col == h, v_ref[h * 64:(h + 1) * 64, :], fv)
    here = pl.ds(pl.multiple_of(s * 64, 64), 64)
    far_ref[here, 0:D] = fk
    far_ref[here, D:2 * D] = fv
    fars = [send(far_ref.at[here], far_ref.at[here], fs.at[d - 1], fr.at[d - 1], peers[d - 1]) for d in range(1, 8)]
    qT_ref[...] = nn(x, wq_ref[...]).astype(BF).T
    kT_ref[...] = k.T
    vT_ref[...] = v.T
    for c in fars:
        c.wait_recv()
    kfT_ref[...] = far_ref[:, 0:D].T
    vfT_ref[...] = far_ref[:, D:2 * D].T
    for c in asks + sends + fars:
        c.wait_send()


def front_all(lens, src, rows, go, wq, wk, wv, wo):
    s = jax.ShapeDtypeStruct
    dma = pltpu.SemaphoreType.DMA
    return pl.pallas_call(
        front_kernel,
        in_specs=[sm()] + [vm()] * 7,
        out_specs=[vm()] * 10,
        out_shape=[s((T, D), BF)] * 3 + [s((D, T), BF)] * 4 + [s((FAR, 2 * D), BF)] + [s((D, FAR), BF)] * 2,
        scratch_shapes=[
            pltpu.VMEM((8, 8, 128), F32), pltpu.VMEM((7, 8, 128), F32), pltpu.VMEM((7, 128, D), BF),
            pltpu.VMEM((T, D), BF), pltpu.VMEM((T, T), BF),
        ] + [dma((7,))] * 6,
        compiler_params=pltpu.CompilerParams(
            vmem_limit_bytes=60 << 20, collective_id=2, has_side_effects=True),
        cost_estimate=pl.CostEstimate(flops=12 * T * D * D, bytes_accessed=20 << 20, transcendentals=0),
    )(lens, src, rows, go, wq, wk, wv, wo)


def tail_kernel(x_ref, go_ref, attT_ref, dqT_ref, dkT_ref, dvT_ref, dkfT_ref, dvfT_ref, wq_ref, wk_ref, wv_ref, wo_ref,
                enc_ref, emb_ref, gq_ref, gk_ref, gv_ref, gout_ref, part, rx, dk_s, dv_s, ss, rs):
    s = lax.axis_index("seq")
    peers = [seq_peer(s, d) for d in range(1, 8)]
    greet(peers)
    part[:, 0:D] = dkfT_ref[...].T
    part[:, D:2 * D] = dvfT_ref[...].T
    backs = [send(part.at[pl.ds(pl.multiple_of(lax.rem(s + d, 8) * 64, 64), 64)], rx.at[d - 1],
                  ss.at[d - 1], rs.at[d - 1], peers[d - 1]) for d in range(1, 8)]
    xT = x_ref[...].T
    gq_ref[...] = nt(xT, dqT_ref[...])
    gout_ref[...] = nn(attT_ref[...], go_ref[...])
    enc_ref[...] = (x_ref[...].astype(F32) + nn(attT_ref[...].T, wo_ref[...])).astype(BF)
    back = part[pl.ds(pl.multiple_of(s * 64, 64), 64), :].astype(F32)
    for d in range(1, 8):
        backs[d - 1].wait_recv()
        back = back + rx[d - 1].astype(F32)
    bT = back.T
    zero = jnp.zeros((HD, 64), F32)
    for h in range(HEADS):
        r = slice(h * HD, (h + 1) * HD)
        w = slice((h // 2) * 128, (h // 2) * 128 + 128)
        bk = bT[h * HD:(h + 1) * HD, :]
        bv = bT[D + h * HD:D + (h + 1) * HD, :]
        pk = [bk, zero] if h % 2 == 0 else [zero, bk]
        pv = [bv, zero] if h % 2 == 0 else [zero, bv]
        dk_s[r, :] = dkT_ref[r, :].astype(BF)
        dv_s[r, :] = dvT_ref[r, :].astype(BF)
        dk_s[r, w] = (dkT_ref[r, w] + jnp.concatenate(pk, axis=1)).astype(BF)
        dv_s[r, w] = (dvT_ref[r, w] + jnp.concatenate(pv, axis=1)).astype(BF)
    gk_ref[...] = nt(xT, dk_s[...])
    gv_ref[...] = nt(xT, dv_s[...])
    e = nn(wq_ref[...], dqT_ref[...]) + nn(wk_ref[...], dk_s[...]) + nn(wv_ref[...], dv_s[...])
    emb_ref[...] = (go_ref[...].astype(F32) + e.T).astype(BF)
    for c in backs:
        c.wait_send()


def tail_all(*args):
    s = jax.ShapeDtypeStruct
    dma = pltpu.SemaphoreType.DMA
    return pl.pallas_call(
        tail_kernel,
        in_specs=[vm()] * 12,
        out_specs=[vm()] * 6,
        out_shape=[s((T, D), BF)] * 2 + [s((D, D), F32)] * 4,
        scratch_shapes=[
            pltpu.VMEM((FAR, 2 * D), BF), pltpu.VMEM((7, 64, 2 * D), BF),
            pltpu.VMEM((D, T), BF), pltpu.VMEM((D, T), BF), dma((7,)), dma((7,)),
        ],
        compiler_params=pltpu.CompilerParams(
            vmem_limit_bytes=60 << 20, collective_id=3, has_side_effects=True),
        cost_estimate=pl.CostEstimate(flops=16 * T * D * D, bytes_accessed=30 << 20, transcendentals=0),
    )(*args)


def to_local(a):
    return a.reshape(64, RATE, -1).transpose(1, 0, 2).reshape(T, -1)


def from_local(a):
    return a.reshape(RATE, 64, -1).transpose(1, 0, 2).reshape(T, -1)


def per_device(tile_embed, tile_source, slide_len, grad_out, w_query, w_key, w_value, w_out):
    source = to_local(tile_source[0]).reshape(1, T)
    length = slide_len[0]
    lens = jnp.stack([length - lax.axis_index("seq") * T, length]).astype(jnp.int32)
    go = to_local(grad_out[0])
    x, k, v, qT, kT, vT, gT, far, kfT, vfT = front_all(
        lens, source, tile_embed[0], go, w_query, w_key, w_value, w_out
    )
    attT, dqT, dkT, dvT, dkfT, dvfT = attn(lens, k, v, qT, kT, vT, gT, far, kfT, vfT)
    enc, emb, gq, gk, gv, gout = tail_all(
        x, go, attT, dqT, dkT, dvT, dkfT, dvfT, w_query, w_key, w_value, w_out
    )
    total = sum_all(gq, gk, gv, gout)
    summed = [total[i].astype(F32) for i in range(4)]
    return (from_local(enc)[None], from_local(emb)[None], summed[0], summed[1], summed[2], summed[3])


def solution(mesh):
    return jax.shard_map(
        per_device,
        mesh=mesh,
        in_specs=(
            P("rep", "seq", None),
            P("rep", "seq"),
            P("rep"),
            P("rep", "seq", None),
            P(),
            P(),
            P(),
            P(),
        ),
        out_specs=(P("rep", "seq", None), P("rep", "seq", None), P(), P(), P(), P()),
        check_vma=False,
    )
```

```python
import functools

import jax
import jax.numpy as jnp
from jax import lax
from jax.experimental import pallas as pl
from jax.experimental.pallas import tpu as pltpu
from jax.sharding import PartitionSpec as P

HEADS=16; RATE=16; HD=48; D=768; T=1024; FAR=512
BF=jnp.bfloat16; F32=jnp.float32
LOG2E=1.4426950408889634
NEG=-1e30
QC=512

def nn(a,b): return lax.dot_general(a,b,(((1,),(0,)),((),())),preferred_element_type=F32)
def nt(a,b): return lax.dot_general(a,b,(((1,),(1,)),((),())),preferred_element_type=F32)

def attn_kernel(len_ref, k_ref, v_ref, qT_ref, kT_ref, vT_ref, gT_ref, far_ref, kfT_ref, vfT_ref, x_ref, go_ref,
                attT_ref, dqT_ref, dk0_ref, dv0_ref, dk32_ref, dv32_ref, dkf_ref, dvf_ref, fin_ref,
                qpad, gpad, kb, kfb, m2s, l2s, u2s, w2s, des, dqs, e2s,
                dk0s, dv0s, dkf0, dvf0, xT, part, rx, bs, br, *scratch):
    red = Reduction(*scratch[:7], fin_ref, *scratch[7:])
    h = pl.program_id(0)

    @pl.when(h == 0)
    def _():
        greet(all_peers())

    @pl.when(h == 8)
    def _():
        part[:, 0:HALF] = dkf0[...].T
        part[:, HALF:D] = dvf0[...].T
        for c in back_copies(part, rx, bs, br):
            c.start()
        xT[...] = x_ref[...].T
        red.columns(0, nt(xT[...], dqT_ref[0:HALF, :]))
        red.pair(0).start()
        red.rows(3, nn(attT_ref[0:HALF, :], go_ref[...]))
        red.pair(3).start()

    @pl.when(h == 10)
    def _():
        add_back(back_copies(part, rx, bs, br), part, rx, 0, dk0s, dv0s, dk0_ref, dv0_ref)
        red.columns(1, nt(xT[...], dk0_ref[...]))
        red.pair(1).start()
        red.columns(2, nt(xT[...], dv0_ref[...]))
        red.pair(2).start()

    @pl.when(h == 11)
    def _():
        red.after_pair()

    @pl.when(h == 13)
    def _():
        red.after_first()

    @pl.when(h == 14)
    def _():
        red.after_second()

    n = len_ref[0]
    nfull = len_ref[1]
    scale = HD ** -0.5
    c = scale * LOG2E
    hh = lax.rem(h, 8)
    w0 = pl.multiple_of((h // 8) * 384 + jnp.where(hh >= 5, 128, 0), 128)
    off = h * HD - w0
    r = pl.multiple_of(h * HD, 16)
    row = lax.broadcasted_iota(jnp.int32, (256, T), 0)
    inside = (row >= off) & (row < off + HD)
    free = jnp.where(off >= 48, 0, 255)
    qw = qT_ref[pl.ds(w0, 256), :]
    gw = gT_ref[pl.ds(w0, 256), :]
    one = jnp.where(row == free, 1.0, 0.0).astype(BF)
    qpad[...] = jnp.where(inside, qw, one)
    gpad[...] = jnp.where(inside, gw, jnp.zeros_like(gw))
    ki = lax.broadcasted_iota(jnp.int32, (T, 1), 0)
    kpos = lax.rem(ki, 64) * RATE + ki // 64
    kbias = jnp.where(kpos < n, 0.0, NEG).astype(BF)
    lane = lax.broadcasted_iota(jnp.int32, (T, 256), 1)
    kb[...] = jnp.where(lane == free, kbias, k_ref[:, pl.ds(w0, 256)])
    fi = lax.broadcasted_iota(jnp.int32, (FAR, 1), 0)
    fbias = jnp.where(fi * RATE + h < nfull, 0.0, NEG).astype(BF)
    flane = lax.broadcasted_iota(jnp.int32, (FAR, 256), 1)
    kfb[...] = jnp.where(flane == free, fbias, far_ref[:, pl.ds(w0, 256)])
    wq = pl.multiple_of((h // 2) * 128, 128)
    qlane = lax.broadcasted_iota(jnp.int32, (1, 128), 1)
    mine = (qlane // 64) == lax.rem(h, 2)
    S2 = nn(kfb[...], qpad[:, pl.ds(wq, 128)])
    x2 = jnp.max(S2, axis=0, keepdims=True)
    e2 = jnp.exp2(S2 * c - x2 * c)
    e2s[...] = e2
    l2 = jnp.sum(e2, axis=0, keepdims=True)
    u2 = nn(vfT_ref[pl.ds(r, HD), :], e2.astype(BF))
    m2s[...] = jnp.full_like(m2s, NEG)
    l2s[...] = jnp.zeros_like(l2s)
    u2s[...] = jnp.zeros_like(u2s)
    m2s[:, pl.ds(wq, 128)] = jnp.where(mine, x2 * scale, NEG)
    l2s[:, pl.ds(wq, 128)] = jnp.where(mine, l2, 0.0)
    u2s[:, pl.ds(wq, 128)] = jnp.where(mine, u2, 0.0)
    vwin = v_ref[:, pl.ds(w0, 256)]
    vTh = vT_ref[pl.ds(r, HD), :]
    kTh = kT_ref[pl.ds(r, HD), :]
    dv = jnp.zeros((HD, T), F32)
    dk = jnp.zeros((HD, T), F32)
    for ci in range(T // QC):
        sl = slice(ci * QC, (ci + 1) * QC)
        S = nn(kb[...], qpad[:, sl])
        x1 = jnp.max(S, axis=0, keepdims=True)
        e = jnp.exp2(S * c - x1 * c)
        l1 = jnp.sum(e, axis=0, keepdims=True)
        u1 = nn(vTh, e.astype(BF))
        m1 = x1 * scale
        m2 = m2s[:, sl]; l2c = l2s[:, sl]
        M = jnp.maximum(m1, m2)
        a1 = jnp.exp(m1 - M); a2 = jnp.exp(m2 - M)
        inv = 1.0 / (a1 * l1 + a2 * l2c)
        w1 = a1 * inv; w2 = a2 * inv
        o = u1 * w1 + u2s[:, sl] * w2
        qi = lax.broadcasted_iota(jnp.int32, (1, QC), 1) + ci * QC
        ok = (lax.rem(qi, 64) * RATE + qi // 64) < n
        attT_ref[pl.ds(r, HD), sl] = jnp.where(ok, o, 0.0).astype(BF)
        gTh = gT_ref[pl.ds(r, HD), sl]
        delta = jnp.sum(gTh.astype(F32) * o, axis=0, keepdims=True)
        w2s[:, sl] = w2
        des[:, sl] = delta
        dP = nn(vwin, gpad[:, sl])
        P = e * w1
        dS = (P * (dP - delta)).astype(BF)
        dqs[:, sl] = nn(kTh, dS)
        dv += nt(gTh, P.astype(BF))
        dk += nt(qT_ref[pl.ds(r, HD), sl], dS)
    r1 = pl.multiple_of(lax.rem(h, 8) * HD, 16)

    @pl.when(h < 8)
    def _():
        dv0s[pl.ds(r1, HD), :] = dv
        dk0s[pl.ds(r1, HD), :] = dk * scale

    @pl.when(h >= 8)
    def _():
        dv32_ref[pl.ds(r1, HD), :] = dv
        dk32_ref[pl.ds(r1, HD), :] = dk * scale

    P2 = e2s[...] * jnp.where(mine, w2s[:, pl.ds(wq, 128)], 0.0)
    dP2 = nn(far_ref[:, pl.ds(pl.multiple_of(w0 + D, 128), 256)], gpad[:, pl.ds(wq, 128)])
    dS2 = (P2 * (dP2 - des[:, pl.ds(wq, 128)])).astype(BF)
    dvf = nt(gT_ref[pl.ds(r, HD), pl.ds(wq, 128)], P2.astype(BF)).astype(BF)
    dkf = (nt(qT_ref[pl.ds(r, HD), pl.ds(wq, 128)], dS2) * scale).astype(BF)

    @pl.when(h < 8)
    def _():
        dvf0[pl.ds(r1, HD), :] = dvf
        dkf0[pl.ds(r1, HD), :] = dkf

    @pl.when(h >= 8)
    def _():
        dvf_ref[pl.ds(r1, HD), :] = dvf
        dkf_ref[pl.ds(r1, HD), :] = dkf

    dqs[:, pl.ds(wq, 128)] += nn(kfT_ref[pl.ds(r, HD), :], dS2)
    dqT_ref[pl.ds(r, HD), :] = (dqs[...] * scale).astype(BF)

    @pl.when(h == HEADS - 1)
    def _():
        red.after_third()
        for c in back_copies(part, rx, bs, br):
            c.wait_send()
        red.finish()

def attn(lens, *arrs):
    s = jax.ShapeDtypeStruct
    dma = pltpu.SemaphoreType.DMA
    return pl.pallas_call(
        attn_kernel,
        grid=(HEADS,),
        in_specs=[sm()] + [vm()] * 11,
        out_specs=[vm()] * 9,
        out_shape=[s((D, T), BF)] * 2 + [s((HALF, T), BF)] * 2 + [s((HALF, T), F32)] * 2 + [s((HALF, FAR), BF)] * 2
        + [s((3, 32, HALF), BF)],
        scratch_shapes=[
            pltpu.VMEM((256, T), BF), pltpu.VMEM((256, T), BF), pltpu.VMEM((T, 256), BF), pltpu.VMEM((FAR, 256), BF),
            pltpu.VMEM((1, T), F32), pltpu.VMEM((1, T), F32), pltpu.VMEM((HD, T), F32), pltpu.VMEM((1, T), F32),
            pltpu.VMEM((1, T), F32), pltpu.VMEM((HD, T), F32), pltpu.VMEM((FAR, 128), F32),
            pltpu.VMEM((HALF, T), F32), pltpu.VMEM((HALF, T), F32), pltpu.VMEM((HALF, FAR), BF),
            pltpu.VMEM((HALF, FAR), BF), pltpu.VMEM((D, T), BF), pltpu.VMEM((FAR, D), BF), pltpu.VMEM((7, 64, D), BF),
            dma((7,)), dma((7,)),
        ] + reduction_scratch(),
        compiler_params=pltpu.CompilerParams(
            vmem_limit_bytes=60 << 20, collective_id=4, has_side_effects=True),
        cost_estimate=pl.CostEstimate(flops=100 * T * D * D, bytes_accessed=30 << 20, transcendentals=0),
    )(lens, *arrs)


def vm():
    return pl.BlockSpec(memory_space=pltpu.VMEM)


def sm():
    return pl.BlockSpec(memory_space=pltpu.SMEM)


MESHID = pl.DeviceIdType.MESH
ORDERS = ((0, 1, 2), (1, 2, 0), (2, 0, 1))


def coords():
    s = lax.axis_index("seq")
    r = lax.axis_index("rep")
    return ((s % 2) * 2 + r // 8, s // 2, (r // 2) % 4), r % 2


def device_at(xyz, core):
    x, y, z = xyz
    return (y * 2 + x // 2, ((x % 2) * 4 + z) * 2 + core)


def along(xyz, axis, step):
    moved = list(xyz)
    moved[axis] = (xyz[axis] + step) % 4
    return tuple(moved)


def greet(peers):
    barrier = pltpu.get_barrier_semaphore()
    for peer in peers:
        pl.semaphore_signal(barrier, inc=1, device_id=peer, device_id_type=MESHID)
    pl.semaphore_wait(barrier, len(peers))


def send(src, dst, ssem, rsem, peer):
    copy = pltpu.make_async_remote_copy(
        src_ref=src, dst_ref=dst, send_sem=ssem, recv_sem=rsem, device_id=peer, device_id_type=MESHID
    )
    copy.start()
    return copy


def seq_peer(s, d):
    return (lax.rem(s + d, 8), lax.axis_index("rep"))


def front_kernel(len_ref, src_ref, rows_ref, go_ref, wq_ref, wk_ref, wv_ref, wo_ref,
                 x_ref, k_ref, v_ref, qT_ref, kT_ref, vT_ref, gT_ref, far_ref, kfT_ref, vfT_ref,
                 ask, req, picked, arrived, perm, qs, qr, ps, pr, fs, fr):
    n = len_ref[0]
    s = lax.axis_index("seq")
    peers = [seq_peer(s, d) for d in range(1, 8)]
    greet(peers)
    src = src_ref[...]
    owner = src // T
    line = src - owner * T
    hot = (lax.broadcasted_iota(jnp.int32, (16, T), 0) == owner).astype(BF)
    before = (lax.broadcasted_iota(jnp.int32, (T, T), 0) < lax.broadcasted_iota(jnp.int32, (T, T), 1)).astype(BF)
    rank = jnp.sum(nn(hot, before) * hot.astype(F32), axis=0, keepdims=True)
    slot = owner.astype(F32) * 128.0 + rank
    where = lax.broadcasted_iota(jnp.int32, (T, T), 0).astype(F32)
    permT = (where == slot).astype(BF)
    high = line // 32
    low = line - high * 32
    eight = lax.broadcasted_iota(jnp.int32, (16, T), 0)
    parts = jnp.where(eight == 0, high, jnp.where(eight == 1, low, 0)).astype(F32).astype(BF)
    got = nt(parts, permT)
    lines = got[0:1] * 32.0 + got[1:2]
    for o in range(8):
        ask[o] = jnp.broadcast_to(lines[:, o * 128:(o + 1) * 128], (8, 128))
    asks = [send(ask.at[lax.rem(s + d, 8)], req.at[d - 1], qs.at[d - 1], qr.at[d - 1], peers[d - 1])
            for d in range(1, 8)]
    perm[...] = permT.T
    qi = lax.broadcasted_iota(jnp.int32, (1, T), 1)
    ok = (lax.rem(qi, 64) * RATE + qi // 64) < n
    gT_ref[...] = jnp.where(ok, nt(wo_ref[...], go_ref[...]), 0.0).astype(BF)
    cells = lax.broadcasted_iota(jnp.int32, (128, T), 1).astype(F32)
    rows = rows_ref[...]
    mine = pl.ds(pl.multiple_of(s * 128, 128), 128)
    sends = []
    for d in range(1, 8):
        asks[d - 1].wait_recv()
        pick = (cells == req[d - 1].T[:, 0:1]).astype(BF)
        picked[d - 1] = nn(pick, rows).astype(BF)
        sends.append(send(picked.at[d - 1], arrived.at[mine], ps.at[d - 1], pr.at[d - 1], seq_peer(s, 8 - d)))
    pick = (cells == ask[s].T[:, 0:1]).astype(BF)
    arrived[mine, :] = nn(pick, rows).astype(BF)
    for c in sends:
        c.wait_recv()
    x = nn(perm[...], arrived[...]).astype(BF)
    x_ref[...] = x
    k = nn(x, wk_ref[...]).astype(BF)
    v = nn(x, wv_ref[...]).astype(BF)
    k_ref[...] = k
    v_ref[...] = v
    col = lax.broadcasted_iota(jnp.int32, (64, D), 1) // HD
    fk = jnp.zeros((64, D), BF)
    fv = jnp.zeros((64, D), BF)
    for h in range(HEADS):
        fk = jnp.where(col == h, k_ref[h * 64:(h + 1) * 64, :], fk)
        fv = jnp.where(col == h, v_ref[h * 64:(h + 1) * 64, :], fv)
    here = pl.ds(pl.multiple_of(s * 64, 64), 64)
    far_ref[here, 0:D] = fk
    far_ref[here, D:2 * D] = fv
    fars = [send(far_ref.at[here], far_ref.at[here], fs.at[d - 1], fr.at[d - 1], peers[d - 1]) for d in range(1, 8)]
    qT_ref[...] = nn(x, wq_ref[...]).astype(BF).T
    kT_ref[...] = k.T
    vT_ref[...] = v.T
    for c in fars:
        c.wait_recv()
    kfT_ref[...] = far_ref[:, 0:D].T
    vfT_ref[...] = far_ref[:, D:2 * D].T
    for c in asks + sends + fars:
        c.wait_send()


def front_all(lens, src, rows, go, wq, wk, wv, wo):
    s = jax.ShapeDtypeStruct
    dma = pltpu.SemaphoreType.DMA
    return pl.pallas_call(
        front_kernel,
        in_specs=[sm()] + [vm()] * 7,
        out_specs=[vm()] * 10,
        out_shape=[s((T, D), BF)] * 3 + [s((D, T), BF)] * 4 + [s((FAR, 2 * D), BF)] + [s((D, FAR), BF)] * 2,
        scratch_shapes=[
            pltpu.VMEM((8, 8, 128), F32), pltpu.VMEM((7, 8, 128), F32), pltpu.VMEM((7, 128, D), BF),
            pltpu.VMEM((T, D), BF), pltpu.VMEM((T, T), BF),
        ] + [dma((7,))] * 6,
        compiler_params=pltpu.CompilerParams(
            vmem_limit_bytes=60 << 20, collective_id=2, has_side_effects=True),
        cost_estimate=pl.CostEstimate(flops=12 * T * D * D, bytes_accessed=20 << 20, transcendentals=0),
    )(lens, src, rows, go, wq, wk, wv, wo)


HALF = D // 2
GH = HEADS // 2


def copy_to(src, dst, ssem, rsem, peer):
    return pltpu.make_async_remote_copy(
        src_ref=src, dst_ref=dst, send_sem=ssem, recv_sem=rsem, device_id=peer, device_id_type=MESHID
    )


def all_peers():
    xyz, core = coords()
    s = lax.axis_index("seq")
    near = [device_at(along(xyz, 0, d), core) for d in (1, 3)] + [device_at(along(xyz, 2, d), core) for d in (1, 2, 3)]
    return [seq_peer(s, d) for d in range(1, 8)] + near + [device_at(xyz, 1 - core)]


class Reduction:
    def __init__(self, grads, crx, acc, rx1, rx2, rx3, r2, fin, cs, cr, ss, rs):
        self.xyz, self.core = coords()
        self.grads, self.crx, self.acc = grads, crx, acc
        self.rx1, self.rx2, self.rx3, self.r2, self.fin = rx1, rx2, rx3, r2, fin
        self.cs, self.cr, self.ss, self.rs = cs, cr, ss, rs

    def at(self, p, level):
        return self.xyz[ORDERS[p][level]]

    def peer(self, p, level, d):
        return device_at(along(self.xyz, ORDERS[p][level], d), self.core)

    def pair(self, i):
        return copy_to(self.grads.at[i, 1 - self.core], self.crx.at[i], self.cs.at[i], self.cr.at[i],
                       device_at(self.xyz, 1 - self.core))

    def wave(self, level, parts=(0, 1, 2)):
        made = []
        for p in parts:
            for d in (1, 2, 3):
                other = (self.at(p, level) + d) % 4
                if level == 0:
                    src, dst = self.acc.at[other, pl.ds(p * 128, 128)], self.rx1.at[p, d - 1]
                elif level == 1:
                    src, dst = self.r2.at[p, pl.ds(pl.multiple_of(other * 32, 32), 32)], self.rx2.at[p, d - 1]
                else:
                    own = self.rx3.at[p, self.at(p, 2)]
                    src, dst = own, own
                made.append(copy_to(src, dst, self.ss.at[level, p, d - 1], self.rs.at[level, p, d - 1],
                                    self.peer(p, level, d)))
        return made

    def start(self, copies):
        for c in copies:
            c.start()

    def columns(self, i, value):
        self.grads[i, 0] = value[:HALF]
        self.grads[i, 1] = value[HALF:]

    def rows(self, i, value):
        self.grads[i, 0] = value[:, :HALF]
        self.grads[i, 1] = value[:, HALF:]

    def after_pair(self):
        for i in (0, 3, 1, 2):
            self.pair(i).wait_recv()
            self.acc[i] = self.grads[i, self.core] + self.crx[i]
        self.start(self.wave(0))

    def after_first(self):
        copies = self.wave(0)
        for p in range(3):
            for c in copies[3 * p:3 * p + 3]:
                c.wait_recv()
            self.r2[p] = self.acc[self.at(p, 0), p * 128:(p + 1) * 128] + self.rx1[p, 0] + self.rx1[p, 1] + self.rx1[p, 2]
            self.start(self.wave(1, (p,)))

    def after_second(self):
        copies = self.wave(1)
        for p in range(3):
            for c in copies[3 * p:3 * p + 3]:
                c.wait_recv()
            own = self.r2[p, pl.ds(pl.multiple_of(self.at(p, 1) * 32, 32), 32)]
            self.rx3[p, self.at(p, 2)] = own + self.rx2[p, 0] + self.rx2[p, 1] + self.rx2[p, 2]
            self.start(self.wave(2, (p,)))

    def after_third(self):
        copies = self.wave(2)
        for p in range(3):
            for c in copies[3 * p:3 * p + 3]:
                c.wait_recv()
            self.fin[p] = (self.rx3[p, 0] + self.rx3[p, 1] + self.rx3[p, 2] + self.rx3[p, 3]).astype(BF)

    def finish(self):
        for i in range(4):
            self.pair(i).wait_send()
        for level in range(3):
            for c in self.wave(level):
                c.wait_send()


def reduction_scratch():
    dma = pltpu.SemaphoreType.DMA
    return [
        pltpu.VMEM((4, 2, HALF, HALF), F32), pltpu.VMEM((4, HALF, HALF), F32), pltpu.VMEM((4, HALF, HALF), F32),
        pltpu.VMEM((3, 3, 128, HALF), F32), pltpu.VMEM((3, 3, 32, HALF), F32), pltpu.VMEM((3, 4, 32, HALF), F32),
        pltpu.VMEM((3, 128, HALF), F32), dma((4,)), dma((4,)), dma((3, 3, 3)), dma((3, 3, 3)),
    ]


class Spread:
    def __init__(self, red, fin, out, gs, gr, hs, hr):
        self.red, self.fin, self.out, self.gs, self.gr, self.hs, self.hr = red, fin, out, gs, gr, hs, hr

    def wave(self, level, parts=(0, 1, 2)):
        made = []
        for p in parts:
            a, b = self.red.at(p, 0), self.red.at(p, 1)
            rows = pl.ds(pl.multiple_of(p * 128 + b * 32, 32), 32) if level == 1 else pl.ds(p * 128, 128)
            here = self.out.at[self.red.core, a, rows]
            for d in (1, 2, 3):
                made.append(copy_to(here, here, self.gs.at[level, p, d - 1], self.gr.at[level, p, d - 1],
                                    self.red.peer(p, level, d)))
        return made

    def mate(self):
        here = self.out.at[self.red.core]
        return copy_to(here, here, self.hs, self.hr, device_at(self.red.xyz, 1 - self.red.core))

    def begin(self):
        for p in range(3):
            rows = pl.ds(pl.multiple_of(p * 128 + self.red.at(p, 1) * 32, 32), 32)
            self.out[self.red.core, self.red.at(p, 0), rows] = self.fin[p]
        for c in self.wave(1):
            c.start()

    def middle(self):
        for p in range(3):
            for c in self.wave(1, (p,)):
                c.wait_recv()
            for c in self.wave(0, (p,)):
                c.start()

    def end(self):
        for c in self.wave(0):
            c.wait_recv()
        self.mate().start()

    def finish(self):
        for level in range(2):
            for c in self.wave(level):
                c.wait_send()
        self.mate().wait()


def back_copies(part, rx, ss, rs):
    s = lax.axis_index("seq")
    return [copy_to(part.at[pl.ds(pl.multiple_of(lax.rem(s + d, 8) * 64, 64), 64)], rx.at[d - 1],
                    ss.at[d - 1], rs.at[d - 1], seq_peer(s, d)) for d in range(1, 8)]


def add_back(copies, part, rx, group, dk32, dv32, dk, dv):
    s = lax.axis_index("seq")
    back = part[pl.ds(pl.multiple_of(s * 64, 64), 64), :].astype(F32)
    for d in range(1, 8):
        copies[d - 1].wait_recv()
        back = back + rx[d - 1].astype(F32)
    bT = back.T
    zero = jnp.zeros((HD, 64), F32)
    for i in range(GH):
        h = group * GH + i
        r = slice(i * HD, (i + 1) * HD)
        w = slice((h // 2) * 128, (h // 2) * 128 + 128)
        bk = bT[i * HD:(i + 1) * HD, :]
        bv = bT[HALF + i * HD:HALF + (i + 1) * HD, :]
        pk = [bk, zero] if h % 2 == 0 else [zero, bk]
        pv = [bv, zero] if h % 2 == 0 else [zero, bv]
        dk[r, :] = dk32[r, :].astype(BF)
        dv[r, :] = dv32[r, :].astype(BF)
        dk[r, w] = (dk32[r, w] + jnp.concatenate(pk, axis=1)).astype(BF)
        dv[r, w] = (dv32[r, w] + jnp.concatenate(pv, axis=1)).astype(BF)


def tail_kernel(x_ref, go_ref, attT_ref, dqT_ref, dk0_ref, dv0_ref, dk32_ref, dv32_ref, dkf_ref, dvf_ref, fin0_ref,
                wq_ref, wk_ref, wv_ref, wo_ref, enc_ref, emb_ref, out0_ref, out1_ref,
                part, rx, dk, dv, fin1, bs, br, g0s, g0r, h0s, h0r, g1s, g1r, h1s, h1r, *scratch):
    greet(all_peers())
    red = Reduction(*scratch[:7], fin1, *scratch[7:])
    first = Spread(red, fin0_ref, out0_ref, g0s, g0r, h0s, h0r)
    second = Spread(red, fin1, out1_ref, g1s, g1r, h1s, h1r)
    part[:, 0:HALF] = dkf_ref[...].T
    part[:, HALF:D] = dvf_ref[...].T
    backs = back_copies(part, rx, bs, br)
    for c in backs:
        c.start()
    first.begin()
    xT = x_ref[...].T
    red.columns(0, nt(xT, dqT_ref[HALF:, :]))
    red.pair(0).start()
    red.rows(3, nn(attT_ref[HALF:, :], go_ref[...]))
    red.pair(3).start()
    first.middle()
    enc_ref[...] = (x_ref[...].astype(F32) + nn(attT_ref[...].T, wo_ref[...])).astype(BF)
    add_back(backs, part, rx, 1, dk32_ref, dv32_ref, dk, dv)
    red.columns(1, nt(xT, dk[...]))
    red.pair(1).start()
    red.columns(2, nt(xT, dv[...]))
    red.pair(2).start()
    first.end()
    red.after_pair()
    e = nn(wq_ref[...], dqT_ref[...])
    e = e + nn(wk_ref[:, 0:HALF], dk0_ref[...]) + nn(wk_ref[:, HALF:D], dk[...])
    e = e + nn(wv_ref[:, 0:HALF], dv0_ref[...]) + nn(wv_ref[:, HALF:D], dv[...])
    emb_ref[...] = (go_ref[...].astype(F32) + e.T).astype(BF)
    red.after_first()
    red.after_second()
    red.after_third()
    second.begin()
    second.middle()
    second.end()
    for c in backs:
        c.wait_send()
    red.finish()
    first.finish()
    second.finish()


def tail_all(*args):
    s = jax.ShapeDtypeStruct
    dma = pltpu.SemaphoreType.DMA
    return pl.pallas_call(
        tail_kernel,
        in_specs=[vm()] * 15,
        out_specs=[vm()] * 4,
        out_shape=[s((T, D), BF)] * 2 + [s((2, 4, HALF, HALF), BF)] * 2,
        scratch_shapes=[
            pltpu.VMEM((FAR, D), BF), pltpu.VMEM((7, 64, D), BF),
            pltpu.VMEM((HALF, T), BF), pltpu.VMEM((HALF, T), BF), pltpu.VMEM((3, 32, HALF), BF), dma((7,)), dma((7,)),
        ] + [dma((2, 3, 3)), dma((2, 3, 3)), dma(()), dma(())] * 2 + reduction_scratch(),
        compiler_params=pltpu.CompilerParams(
            vmem_limit_bytes=60 << 20, collective_id=3, has_side_effects=True),
        cost_estimate=pl.CostEstimate(flops=16 * T * D * D, bytes_accessed=30 << 20, transcendentals=0),
    )(*args)


def to_local(a):
    return a.reshape(64, RATE, -1).transpose(1, 0, 2).reshape(T, -1)


def from_local(a):
    return a.reshape(RATE, 64, -1).transpose(1, 0, 2).reshape(T, -1)


def per_device(tile_embed, tile_source, slide_len, grad_out, w_query, w_key, w_value, w_out):
    source = to_local(tile_source[0]).reshape(1, T)
    length = slide_len[0]
    lens = jnp.stack([length - lax.axis_index("seq") * T, length]).astype(jnp.int32)
    go = to_local(grad_out[0])
    x, k, v, qT, kT, vT, gT, far, kfT, vfT = front_all(
        lens, source, tile_embed[0], go, w_query, w_key, w_value, w_out
    )
    attT, dqT, dk0, dv0, dk32, dv32, dkf, dvf, fin0 = attn(lens, k, v, qT, kT, vT, gT, far, kfT, vfT, x, go)
    enc, emb, out0, out1 = tail_all(
        x, go, attT, dqT, dk0, dv0, dk32, dv32, dkf, dvf, fin0, w_query, w_key, w_value, w_out
    )
    summed = []
    for i in range(4):
        along_rows = [jnp.concatenate([o[0, i], o[1, i]], axis=0 if i < 3 else 1) for o in (out0, out1)]
        summed.append(jnp.concatenate(along_rows, axis=1 if i < 3 else 0).astype(F32))
    return (from_local(enc)[None], from_local(emb)[None], summed[0], summed[1], summed[2], summed[3])


def solution(mesh):
    return jax.shard_map(
        per_device,
        mesh=mesh,
        in_specs=(
            P("rep", "seq", None),
            P("rep", "seq"),
            P("rep"),
            P("rep", "seq", None),
            P(),
            P(),
            P(),
            P(),
        ),
        out_specs=(P("rep", "seq", None), P("rep", "seq", None), P(), P(), P(), P()),
        check_vma=False,
    )
```

```python
import functools

import jax
import jax.numpy as jnp
from jax import lax
from jax.experimental import pallas as pl
from jax.experimental.pallas import tpu as pltpu
from jax.sharding import PartitionSpec as P

HEADS=16; RATE=16; HD=48; D=768; T=1024; FAR=512
BF=jnp.bfloat16; F32=jnp.float32
LOG2E=1.4426950408889634
NEG=-1e30
QC=512

def nn(a,b): return lax.dot_general(a,b,(((1,),(0,)),((),())),preferred_element_type=F32)
def nt(a,b): return lax.dot_general(a,b,(((1,),(1,)),((),())),preferred_element_type=F32)

def attn_kernel(len_ref, k_ref, v_ref, qT_ref, kT_ref, vT_ref, gT_ref, far_ref, kfT_ref, vfT_ref, top_ref, x_ref, go_ref,
                attT_ref, dqT_ref, dk0_ref, dv0_ref, dk32_ref, dv32_ref, dkf_ref, dvf_ref, fin_ref,
                qpad, gpad, kb, kfb, m2s, l2s, u2s, w2s, des, dqs, e2s,
                dk0s, dv0s, dkf0, dvf0, xT, part, rx, bs, br, *scratch):
    red = Reduction(*scratch[:7], fin_ref, *scratch[7:])
    h = pl.program_id(0)

    @pl.when(h == 0)
    def _():
        greet(all_peers())

    @pl.when(h == 8)
    def _():
        part[:, 0:HALF] = dkf0[...].T
        part[:, HALF:D] = dvf0[...].T
        for c in back_copies(part, rx, bs, br):
            c.start()
        xT[...] = x_ref[...].T
        red.columns(0, nt(xT[...], dqT_ref[0:HALF, :]))
        red.pair(0).start()
        red.rows(3, nn(attT_ref[0:HALF, :], go_ref[...]))
        red.pair(3).start()

    @pl.when(h == 10)
    def _():
        add_back(back_copies(part, rx, bs, br), part, rx, 0, dk0s, dv0s, dk0_ref, dv0_ref)
        red.columns(1, nt(xT[...], dk0_ref[...]))
        red.pair(1).start()
        red.columns(2, nt(xT[...], dv0_ref[...]))
        red.pair(2).start()

    @pl.when(h == 11)
    def _():
        red.after_pair()

    @pl.when(h == 13)
    def _():
        red.after_first()

    @pl.when(h == 14)
    def _():
        red.after_second()

    n = len_ref[0]
    nfull = len_ref[1]
    scale = HD ** -0.5
    c = scale * LOG2E
    w0, off, free = window(h)
    r = pl.multiple_of(h * HD, 16)
    row = lax.broadcasted_iota(jnp.int32, (256, T), 0)
    qpad[...] = pad_rows(qT_ref, w0, off, row, jnp.where(row == free, 1.0, 0.0).astype(BF))
    gpad[...] = pad_rows(gT_ref, w0, off, row, jnp.zeros((256, T), BF))
    lane = lax.broadcasted_iota(jnp.int32, (T, 256), 1)
    kb[...] = jnp.where(lane == free, key_bias(n), k_ref[:, pl.ds(w0, 256)])
    fi = lax.broadcasted_iota(jnp.int32, (FAR, 1), 0)
    fbias = jnp.where(fi * RATE + h < nfull, 0.0, NEG).astype(BF)
    flane = lax.broadcasted_iota(jnp.int32, (FAR, 256), 1)
    kfb[...] = jnp.where(flane == free, fbias, far_ref[:, pl.ds(w0, 256)])
    wq = pl.multiple_of((h // 2) * 128, 128)
    qlane = lax.broadcasted_iota(jnp.int32, (1, 128), 1)
    mine = (qlane // 64) == lax.rem(h, 2)
    S2 = nn(kfb[...], qpad[:, pl.ds(wq, 128)])
    x2 = jnp.max(S2, axis=0, keepdims=True)
    e2 = jnp.exp2(S2 * c - x2 * c)
    e2s[...] = e2
    l2 = jnp.sum(e2, axis=0, keepdims=True)
    u2 = nn(vfT_ref[pl.ds(r, HD), :], e2.astype(BF))
    m2s[...] = jnp.full_like(m2s, NEG)
    l2s[...] = jnp.zeros_like(l2s)
    u2s[...] = jnp.zeros_like(u2s)
    m2s[:, pl.ds(wq, 128)] = jnp.where(mine, x2 * scale, NEG)
    l2s[:, pl.ds(wq, 128)] = jnp.where(mine, l2, 0.0)
    u2s[:, pl.ds(wq, 128)] = jnp.where(mine, u2, 0.0)
    vwin = v_ref[:, pl.ds(w0, 256)]
    vTh = vT_ref[pl.ds(r, HD), :]
    kTh = kT_ref[pl.ds(r, HD), :]
    dv = jnp.zeros((HD, T), F32)
    dk = jnp.zeros((HD, T), F32)
    for ci in range(T // QC):
        sl = slice(ci * QC, (ci + 1) * QC)
        S = nn(kb[...], qpad[:, sl])
        x1 = top_ref[h, :, sl]
        e = jnp.exp2(S * c - x1 * c)
        l1 = jnp.sum(e, axis=0, keepdims=True)
        u1 = nn(vTh, e.astype(BF))
        m1 = x1 * scale
        m2 = m2s[:, sl]; l2c = l2s[:, sl]
        M = jnp.maximum(m1, m2)
        a1 = jnp.exp(m1 - M); a2 = jnp.exp(m2 - M)
        inv = 1.0 / (a1 * l1 + a2 * l2c)
        w1 = a1 * inv; w2 = a2 * inv
        o = u1 * w1 + u2s[:, sl] * w2
        qi = lax.broadcasted_iota(jnp.int32, (1, QC), 1) + ci * QC
        ok = (lax.rem(qi, 64) * RATE + qi // 64) < n
        attT_ref[pl.ds(r, HD), sl] = jnp.where(ok, o, 0.0).astype(BF)
        gTh = gT_ref[pl.ds(r, HD), sl]
        delta = jnp.sum(gTh.astype(F32) * o, axis=0, keepdims=True)
        w2s[:, sl] = w2
        des[:, sl] = delta
        dP = nn(vwin, gpad[:, sl])
        P = e * w1
        dS = (P * (dP - delta)).astype(BF)
        dqs[:, sl] = nn(kTh, dS)
        dv += nt(gTh, P.astype(BF))
        dk += nt(qT_ref[pl.ds(r, HD), sl], dS)
    r1 = pl.multiple_of(lax.rem(h, 8) * HD, 16)

    @pl.when(h < 8)
    def _():
        dv0s[pl.ds(r1, HD), :] = dv
        dk0s[pl.ds(r1, HD), :] = dk * scale

    @pl.when(h >= 8)
    def _():
        dv32_ref[pl.ds(r1, HD), :] = dv
        dk32_ref[pl.ds(r1, HD), :] = dk * scale

    P2 = e2s[...] * jnp.where(mine, w2s[:, pl.ds(wq, 128)], 0.0)
    dP2 = nn(far_ref[:, pl.ds(pl.multiple_of(w0 + D, 128), 256)], gpad[:, pl.ds(wq, 128)])
    dS2 = (P2 * (dP2 - des[:, pl.ds(wq, 128)])).astype(BF)
    dvf = nt(gT_ref[pl.ds(r, HD), pl.ds(wq, 128)], P2.astype(BF)).astype(BF)
    dkf = (nt(qT_ref[pl.ds(r, HD), pl.ds(wq, 128)], dS2) * scale).astype(BF)

    @pl.when(h < 8)
    def _():
        dvf0[pl.ds(r1, HD), :] = dvf
        dkf0[pl.ds(r1, HD), :] = dkf

    @pl.when(h >= 8)
    def _():
        dvf_ref[pl.ds(r1, HD), :] = dvf
        dkf_ref[pl.ds(r1, HD), :] = dkf

    dqs[:, pl.ds(wq, 128)] += nn(kfT_ref[pl.ds(r, HD), :], dS2)
    dqT_ref[pl.ds(r, HD), :] = (dqs[...] * scale).astype(BF)

    @pl.when(h == HEADS - 1)
    def _():
        red.after_third()
        for c in back_copies(part, rx, bs, br):
            c.wait_send()
        red.finish()

def attn(lens, *arrs):
    s = jax.ShapeDtypeStruct
    dma = pltpu.SemaphoreType.DMA
    return pl.pallas_call(
        attn_kernel,
        grid=(HEADS,),
        in_specs=[sm()] + [vm()] * 12,
        out_specs=[vm()] * 9,
        out_shape=[s((D, T), BF)] * 2 + [s((HALF, T), BF)] * 2 + [s((HALF, T), F32)] * 2 + [s((HALF, FAR), BF)] * 2
        + [s((3, 32, HALF), BF)],
        scratch_shapes=[
            pltpu.VMEM((256, T), BF), pltpu.VMEM((256, T), BF), pltpu.VMEM((T, 256), BF), pltpu.VMEM((FAR, 256), BF),
            pltpu.VMEM((1, T), F32), pltpu.VMEM((1, T), F32), pltpu.VMEM((HD, T), F32), pltpu.VMEM((1, T), F32),
            pltpu.VMEM((1, T), F32), pltpu.VMEM((HD, T), F32), pltpu.VMEM((FAR, 128), F32),
            pltpu.VMEM((HALF, T), F32), pltpu.VMEM((HALF, T), F32), pltpu.VMEM((HALF, FAR), BF),
            pltpu.VMEM((HALF, FAR), BF), pltpu.VMEM((D, T), BF), pltpu.VMEM((FAR, D), BF), pltpu.VMEM((7, 64, D), BF),
            dma((7,)), dma((7,)),
        ] + reduction_scratch(),
        compiler_params=pltpu.CompilerParams(
            vmem_limit_bytes=60 << 20, collective_id=4, has_side_effects=True),
        cost_estimate=pl.CostEstimate(flops=100 * T * D * D, bytes_accessed=30 << 20, transcendentals=0),
    )(lens, *arrs)


def vm():
    return pl.BlockSpec(memory_space=pltpu.VMEM)


def sm():
    return pl.BlockSpec(memory_space=pltpu.SMEM)


MESHID = pl.DeviceIdType.MESH
ORDERS = ((0, 1, 2), (1, 2, 0), (2, 0, 1))


def coords():
    s = lax.axis_index("seq")
    r = lax.axis_index("rep")
    return ((s % 2) * 2 + r // 8, s // 2, (r // 2) % 4), r % 2


def device_at(xyz, core):
    x, y, z = xyz
    return (y * 2 + x // 2, ((x % 2) * 4 + z) * 2 + core)


def along(xyz, axis, step):
    moved = list(xyz)
    moved[axis] = (xyz[axis] + step) % 4
    return tuple(moved)


def greet(peers):
    barrier = pltpu.get_barrier_semaphore()
    for peer in peers:
        pl.semaphore_signal(barrier, inc=1, device_id=peer, device_id_type=MESHID)
    pl.semaphore_wait(barrier, len(peers))


def send(src, dst, ssem, rsem, peer):
    copy = pltpu.make_async_remote_copy(
        src_ref=src, dst_ref=dst, send_sem=ssem, recv_sem=rsem, device_id=peer, device_id_type=MESHID
    )
    copy.start()
    return copy


def seq_peer(s, d):
    return (lax.rem(s + d, 8), lax.axis_index("rep"))


def window(h):
    hh = lax.rem(h, 8)
    w0 = pl.multiple_of((h // 8) * 384 + jnp.where(hh >= 5, 128, 0), 128)
    off = h * HD - w0
    return w0, off, jnp.where(off >= 48, 0, 255)


def pad_rows(ref, w0, off, rows_in, filler):
    return jnp.where((rows_in >= off) & (rows_in < off + HD), ref[pl.ds(w0, 256), :], filler)


def key_bias(n):
    ki = lax.broadcasted_iota(jnp.int32, (T, 1), 0)
    return jnp.where(lax.rem(ki, 64) * RATE + ki // 64 < n, 0.0, NEG).astype(BF)


def front_kernel(len_ref, src_ref, rows_ref, grad_ref, wq_ref, wk_ref, wv_ref, wo_ref,
                 x_ref, go_ref, k_ref, v_ref, qT_ref, kT_ref, vT_ref, gT_ref, far_ref, kfT_ref, vfT_ref, top_ref,
                 ask, req, picked, arrived, perm, qpad, kb, qs, qr, ps, pr, fs, fr):
    n = len_ref[0]
    s = lax.axis_index("seq")
    peers = [seq_peer(s, d) for d in range(1, 8)]
    greet(peers)
    src = src_ref[...]
    sixteen = lax.broadcasted_iota(jnp.int32, (16, T), 0)
    line = lax.rem(src, T)
    parts = jnp.where(sixteen == 0, line // 32, jnp.where(sixteen == 1, lax.rem(line, 32), src // T))
    spot = lax.broadcasted_iota(jnp.int32, (T, T), 0)
    reorder = (lax.broadcasted_iota(jnp.int32, (T, T), 1) == lax.rem(spot, 64) * RATE + spot // 64).astype(BF)
    parts = nt(parts.astype(F32).astype(BF), reorder)
    owner = parts[2:3].astype(jnp.int32)
    hot = (lax.broadcasted_iota(jnp.int32, (16, T), 0) == owner).astype(BF)
    before = (lax.broadcasted_iota(jnp.int32, (T, T), 0) < lax.broadcasted_iota(jnp.int32, (T, T), 1)).astype(BF)
    rank = jnp.sum(nn(hot, before) * hot.astype(F32), axis=0, keepdims=True)
    slot = owner.astype(F32) * 128.0 + rank
    where = lax.broadcasted_iota(jnp.int32, (T, T), 0).astype(F32)
    permT = (where == slot).astype(BF)
    got = nt(parts.astype(BF), permT)
    lines = got[0:1] * 32.0 + got[1:2]
    for o in range(8):
        ask[o] = jnp.broadcast_to(lines[:, o * 128:(o + 1) * 128], (8, 128))
    asks = [send(ask.at[lax.rem(s + d, 8)], req.at[d - 1], qs.at[d - 1], qr.at[d - 1], peers[d - 1])
            for d in range(1, 8)]
    perm[...] = permT.T
    qi = lax.broadcasted_iota(jnp.int32, (1, T), 1)
    ok = (lax.rem(qi, 64) * RATE + qi // 64) < n
    go_ref[...] = nn(reorder, grad_ref[...]).astype(BF)
    gT_ref[...] = jnp.where(ok, nt(wo_ref[...], go_ref[...]), 0.0).astype(BF)
    cells = lax.broadcasted_iota(jnp.int32, (128, T), 1).astype(F32)
    rows = rows_ref[...]
    mine = pl.ds(pl.multiple_of(s * 128, 128), 128)
    sends = []
    for d in range(1, 8):
        asks[d - 1].wait_recv()
        pick = (cells == req[d - 1].T[:, 0:1]).astype(BF)
        picked[d - 1] = nn(pick, rows).astype(BF)
        sends.append(send(picked.at[d - 1], arrived.at[mine], ps.at[d - 1], pr.at[d - 1], seq_peer(s, 8 - d)))
    pick = (cells == ask[s].T[:, 0:1]).astype(BF)
    arrived[mine, :] = nn(pick, rows).astype(BF)
    for c in sends:
        c.wait_recv()
    x = nn(perm[...], arrived[...]).astype(BF)
    x_ref[...] = x
    k = nn(x, wk_ref[...]).astype(BF)
    v = nn(x, wv_ref[...]).astype(BF)
    k_ref[...] = k
    v_ref[...] = v
    col = lax.broadcasted_iota(jnp.int32, (64, D), 1) // HD
    fk = jnp.zeros((64, D), BF)
    fv = jnp.zeros((64, D), BF)
    for h in range(HEADS):
        fk = jnp.where(col == h, k_ref[h * 64:(h + 1) * 64, :], fk)
        fv = jnp.where(col == h, v_ref[h * 64:(h + 1) * 64, :], fv)
    here = pl.ds(pl.multiple_of(s * 64, 64), 64)
    far_ref[here, 0:D] = fk
    far_ref[here, D:2 * D] = fv
    fars = [send(far_ref.at[here], far_ref.at[here], fs.at[d - 1], fr.at[d - 1], peers[d - 1]) for d in range(1, 8)]
    qT_ref[...] = nn(x, wq_ref[...]).astype(BF).T
    kT_ref[...] = k.T
    vT_ref[...] = v.T
    rows_in = lax.broadcasted_iota(jnp.int32, (256, T), 0)
    cols_in = lax.broadcasted_iota(jnp.int32, (T, 256), 1)
    kbias = key_bias(n)

    @pl.loop(0, HEADS)
    def _(h):
        w0, off, free = window(h)
        qpad[...] = pad_rows(qT_ref, w0, off, rows_in, jnp.where(rows_in == free, 1.0, 0.0).astype(BF))
        kb[...] = jnp.where(cols_in == free, kbias, k_ref[:, pl.ds(w0, 256)])
        for ci in range(T // QC):
            sl = slice(ci * QC, (ci + 1) * QC)
            top_ref[h, :, sl] = jnp.max(nn(kb[...], qpad[:, sl]), axis=0, keepdims=True)

    for c in fars:
        c.wait_recv()
    kfT_ref[...] = far_ref[:, 0:D].T
    vfT_ref[...] = far_ref[:, D:2 * D].T
    for c in asks + sends + fars:
        c.wait_send()


def front_all(lens, src, rows, go, wq, wk, wv, wo):
    s = jax.ShapeDtypeStruct
    dma = pltpu.SemaphoreType.DMA
    return pl.pallas_call(
        front_kernel,
        in_specs=[sm()] + [vm()] * 7,
        out_specs=[vm()] * 12,
        out_shape=[s((T, D), BF)] * 4 + [s((D, T), BF)] * 4 + [s((FAR, 2 * D), BF)] + [s((D, FAR), BF)] * 2
        + [s((HEADS, 1, T), F32)],
        scratch_shapes=[
            pltpu.VMEM((8, 8, 128), F32), pltpu.VMEM((7, 8, 128), F32), pltpu.VMEM((7, 128, D), BF),
            pltpu.VMEM((T, D), BF), pltpu.VMEM((T, T), BF), pltpu.VMEM((256, T), BF), pltpu.VMEM((T, 256), BF),
        ] + [dma((7,))] * 6,
        compiler_params=pltpu.CompilerParams(
            vmem_limit_bytes=60 << 20, collective_id=2, has_side_effects=True),
        cost_estimate=pl.CostEstimate(flops=12 * T * D * D, bytes_accessed=20 << 20, transcendentals=0),
    )(lens, src, rows, go, wq, wk, wv, wo)


HALF = D // 2
GH = HEADS // 2


def copy_to(src, dst, ssem, rsem, peer):
    return pltpu.make_async_remote_copy(
        src_ref=src, dst_ref=dst, send_sem=ssem, recv_sem=rsem, device_id=peer, device_id_type=MESHID
    )


def all_peers():
    xyz, core = coords()
    s = lax.axis_index("seq")
    near = [device_at(along(xyz, 0, d), core) for d in (1, 3)] + [device_at(along(xyz, 2, d), core) for d in (1, 2, 3)]
    return [seq_peer(s, d) for d in range(1, 8)] + near + [device_at(xyz, 1 - core)]


class Reduction:
    def __init__(self, grads, crx, acc, rx1, rx2, rx3, r2, fin, cs, cr, ss, rs):
        self.xyz, self.core = coords()
        self.grads, self.crx, self.acc = grads, crx, acc
        self.rx1, self.rx2, self.rx3, self.r2, self.fin = rx1, rx2, rx3, r2, fin
        self.cs, self.cr, self.ss, self.rs = cs, cr, ss, rs

    def at(self, p, level):
        return self.xyz[ORDERS[p][level]]

    def peer(self, p, level, d):
        return device_at(along(self.xyz, ORDERS[p][level], d), self.core)

    def pair(self, i):
        return copy_to(self.grads.at[i, 1 - self.core], self.crx.at[i], self.cs.at[i], self.cr.at[i],
                       device_at(self.xyz, 1 - self.core))

    def wave(self, level, parts=(0, 1, 2)):
        made = []
        for p in parts:
            for d in (1, 2, 3):
                other = (self.at(p, level) + d) % 4
                if level == 0:
                    src, dst = self.acc.at[other, pl.ds(p * 128, 128)], self.rx1.at[p, d - 1]
                elif level == 1:
                    src, dst = self.r2.at[p, pl.ds(pl.multiple_of(other * 32, 32), 32)], self.rx2.at[p, d - 1]
                else:
                    own = self.rx3.at[p, self.at(p, 2)]
                    src, dst = own, own
                made.append(copy_to(src, dst, self.ss.at[level, p, d - 1], self.rs.at[level, p, d - 1],
                                    self.peer(p, level, d)))
        return made

    def start(self, copies):
        for c in copies:
            c.start()

    def columns(self, i, value):
        self.grads[i, 0] = value[:HALF]
        self.grads[i, 1] = value[HALF:]

    def rows(self, i, value):
        self.grads[i, 0] = value[:, :HALF]
        self.grads[i, 1] = value[:, HALF:]

    def after_pair(self):
        for i in (0, 3, 1, 2):
            self.pair(i).wait_recv()
            self.acc[i] = self.grads[i, self.core] + self.crx[i]
        self.start(self.wave(0))

    def after_first(self):
        copies = self.wave(0)
        for p in range(3):
            for c in copies[3 * p:3 * p + 3]:
                c.wait_recv()
            self.r2[p] = self.acc[self.at(p, 0), p * 128:(p + 1) * 128] + self.rx1[p, 0] + self.rx1[p, 1] + self.rx1[p, 2]
            self.start(self.wave(1, (p,)))

    def after_second(self):
        copies = self.wave(1)
        for p in range(3):
            for c in copies[3 * p:3 * p + 3]:
                c.wait_recv()
            own = self.r2[p, pl.ds(pl.multiple_of(self.at(p, 1) * 32, 32), 32)]
            self.rx3[p, self.at(p, 2)] = own + self.rx2[p, 0] + self.rx2[p, 1] + self.rx2[p, 2]
            self.start(self.wave(2, (p,)))

    def after_third(self):
        copies = self.wave(2)
        for p in range(3):
            for c in copies[3 * p:3 * p + 3]:
                c.wait_recv()
            self.fin[p] = (self.rx3[p, 0] + self.rx3[p, 1] + self.rx3[p, 2] + self.rx3[p, 3]).astype(BF)

    def finish(self):
        for i in range(4):
            self.pair(i).wait_send()
        for level in range(3):
            for c in self.wave(level):
                c.wait_send()


def reduction_scratch():
    dma = pltpu.SemaphoreType.DMA
    return [
        pltpu.VMEM((4, 2, HALF, HALF), F32), pltpu.VMEM((4, HALF, HALF), F32), pltpu.VMEM((4, HALF, HALF), F32),
        pltpu.VMEM((3, 3, 128, HALF), F32), pltpu.VMEM((3, 3, 32, HALF), F32), pltpu.VMEM((3, 4, 32, HALF), F32),
        pltpu.VMEM((3, 128, HALF), F32), dma((4,)), dma((4,)), dma((3, 3, 3)), dma((3, 3, 3)),
    ]


class Spread:
    def __init__(self, red, fin, out, gs, gr, hs, hr):
        self.red, self.fin, self.out, self.gs, self.gr, self.hs, self.hr = red, fin, out, gs, gr, hs, hr

    def wave(self, level, parts=(0, 1, 2)):
        made = []
        for p in parts:
            a, b = self.red.at(p, 0), self.red.at(p, 1)
            rows = pl.ds(pl.multiple_of(p * 128 + b * 32, 32), 32) if level == 1 else pl.ds(p * 128, 128)
            here = self.out.at[self.red.core, a, rows]
            for d in (1, 2, 3):
                made.append(copy_to(here, here, self.gs.at[level, p, d - 1], self.gr.at[level, p, d - 1],
                                    self.red.peer(p, level, d)))
        return made

    def mate(self):
        here = self.out.at[self.red.core]
        return copy_to(here, here, self.hs, self.hr, device_at(self.red.xyz, 1 - self.red.core))

    def begin(self):
        for p in range(3):
            rows = pl.ds(pl.multiple_of(p * 128 + self.red.at(p, 1) * 32, 32), 32)
            self.out[self.red.core, self.red.at(p, 0), rows] = self.fin[p]
        for c in self.wave(1):
            c.start()

    def middle(self):
        for p in range(3):
            for c in self.wave(1, (p,)):
                c.wait_recv()
            for c in self.wave(0, (p,)):
                c.start()

    def end(self):
        for c in self.wave(0):
            c.wait_recv()
        self.mate().start()

    def finish(self):
        for level in range(2):
            for c in self.wave(level):
                c.wait_send()
        self.mate().wait()


def back_copies(part, rx, ss, rs):
    s = lax.axis_index("seq")
    return [copy_to(part.at[pl.ds(pl.multiple_of(lax.rem(s + d, 8) * 64, 64), 64)], rx.at[d - 1],
                    ss.at[d - 1], rs.at[d - 1], seq_peer(s, d)) for d in range(1, 8)]


def add_back(copies, part, rx, group, dk32, dv32, dk, dv):
    s = lax.axis_index("seq")
    back = part[pl.ds(pl.multiple_of(s * 64, 64), 64), :].astype(F32)
    for d in range(1, 8):
        copies[d - 1].wait_recv()
        back = back + rx[d - 1].astype(F32)
    bT = back.T
    zero = jnp.zeros((HD, 64), F32)
    for i in range(GH):
        h = group * GH + i
        r = slice(i * HD, (i + 1) * HD)
        w = slice((h // 2) * 128, (h // 2) * 128 + 128)
        bk = bT[i * HD:(i + 1) * HD, :]
        bv = bT[HALF + i * HD:HALF + (i + 1) * HD, :]
        pk = [bk, zero] if h % 2 == 0 else [zero, bk]
        pv = [bv, zero] if h % 2 == 0 else [zero, bv]
        dk[r, :] = dk32[r, :].astype(BF)
        dv[r, :] = dv32[r, :].astype(BF)
        dk[r, w] = (dk32[r, w] + jnp.concatenate(pk, axis=1)).astype(BF)
        dv[r, w] = (dv32[r, w] + jnp.concatenate(pv, axis=1)).astype(BF)


def tail_kernel(x_ref, go_ref, attT_ref, dqT_ref, dk0_ref, dv0_ref, dk32_ref, dv32_ref, dkf_ref, dvf_ref, fin0_ref,
                wq_ref, wk_ref, wv_ref, wo_ref, enc_ref, emb_ref, out0_ref, out1_ref,
                part, rx, dk, dv, fin1, home, bs, br, g0s, g0r, h0s, h0r, g1s, g1r, h1s, h1r, *scratch):
    greet(all_peers())
    red = Reduction(*scratch[:7], fin1, *scratch[7:])
    first = Spread(red, fin0_ref, out0_ref, g0s, g0r, h0s, h0r)
    second = Spread(red, fin1, out1_ref, g1s, g1r, h1s, h1r)
    part[:, 0:HALF] = dkf_ref[...].T
    part[:, HALF:D] = dvf_ref[...].T
    backs = back_copies(part, rx, bs, br)
    for c in backs:
        c.start()
    first.begin()
    xT = x_ref[...].T
    red.columns(0, nt(xT, dqT_ref[HALF:, :]))
    red.pair(0).start()
    red.rows(3, nn(attT_ref[HALF:, :], go_ref[...]))
    red.pair(3).start()
    first.middle()
    enc = (x_ref[...].astype(F32) + nn(attT_ref[...].T, wo_ref[...])).astype(BF)
    spot = lax.broadcasted_iota(jnp.int32, (T, T), 0)
    home[...] = (lax.broadcasted_iota(jnp.int32, (T, T), 1) == lax.rem(spot, RATE) * 64 + spot // RATE).astype(BF)
    enc_ref[...] = nn(home[...], enc).astype(BF)
    add_back(backs, part, rx, 1, dk32_ref, dv32_ref, dk, dv)
    red.columns(1, nt(xT, dk[...]))
    red.pair(1).start()
    red.columns(2, nt(xT, dv[...]))
    red.pair(2).start()
    first.end()
    red.after_pair()
    e = nn(wq_ref[...], dqT_ref[...])
    e = e + nn(wk_ref[:, 0:HALF], dk0_ref[...]) + nn(wk_ref[:, HALF:D], dk[...])
    e = e + nn(wv_ref[:, 0:HALF], dv0_ref[...]) + nn(wv_ref[:, HALF:D], dv[...])
    emb = (go_ref[...].astype(F32) + e.T).astype(BF)
    emb_ref[...] = nn(home[...], emb).astype(BF)
    red.after_first()
    red.after_second()
    red.after_third()
    second.begin()
    second.middle()
    second.end()
    for c in backs:
        c.wait_send()
    red.finish()
    first.finish()
    second.finish()


def tail_all(*args):
    s = jax.ShapeDtypeStruct
    dma = pltpu.SemaphoreType.DMA
    return pl.pallas_call(
        tail_kernel,
        in_specs=[vm()] * 15,
        out_specs=[vm()] * 4,
        out_shape=[s((T, D), BF)] * 2 + [s((2, 4, HALF, HALF), BF)] * 2,
        scratch_shapes=[
            pltpu.VMEM((FAR, D), BF), pltpu.VMEM((7, 64, D), BF),
            pltpu.VMEM((HALF, T), BF), pltpu.VMEM((HALF, T), BF), pltpu.VMEM((3, 32, HALF), BF), pltpu.VMEM((T, T), BF),
            dma((7,)), dma((7,)),
        ] + [dma((2, 3, 3)), dma((2, 3, 3)), dma(()), dma(())] * 2 + reduction_scratch(),
        compiler_params=pltpu.CompilerParams(
            vmem_limit_bytes=60 << 20, collective_id=3, has_side_effects=True),
        cost_estimate=pl.CostEstimate(flops=16 * T * D * D, bytes_accessed=30 << 20, transcendentals=0),
    )(*args)


def per_device(tile_embed, tile_source, slide_len, grad_out, w_query, w_key, w_value, w_out):
    source = tile_source.reshape(1, T)
    length = slide_len[0]
    lens = jnp.stack([length - lax.axis_index("seq") * T, length]).astype(jnp.int32)
    x, go, k, v, qT, kT, vT, gT, far, kfT, vfT, top = front_all(
        lens, source, tile_embed[0], grad_out[0], w_query, w_key, w_value, w_out
    )
    attT, dqT, dk0, dv0, dk32, dv32, dkf, dvf, fin0 = attn(lens, k, v, qT, kT, vT, gT, far, kfT, vfT, top, x, go)
    enc, emb, out0, out1 = tail_all(
        x, go, attT, dqT, dk0, dv0, dk32, dv32, dkf, dvf, fin0, w_query, w_key, w_value, w_out
    )
    summed = []
    for i in range(4):
        along_rows = [jnp.concatenate([o[0, i], o[1, i]], axis=0 if i < 3 else 1) for o in (out0, out1)]
        summed.append(jnp.concatenate(along_rows, axis=1 if i < 3 else 0).astype(F32))
    return (enc[None], emb[None], summed[0], summed[1], summed[2], summed[3])


def solution(mesh):
    return jax.shard_map(
        per_device,
        mesh=mesh,
        in_specs=(
            P("rep", "seq", None),
            P("rep", "seq"),
            P("rep"),
            P("rep", "seq", None),
            P(),
            P(),
            P(),
            P(),
        ),
        out_specs=(P("rep", "seq", None), P("rep", "seq", None), P(), P(), P(), P()),
        check_vma=False,
    )
```

```python
import functools

import jax
import jax.numpy as jnp
from jax import lax
from jax.experimental import pallas as pl
from jax.experimental.pallas import tpu as pltpu
from jax.sharding import PartitionSpec as P

HEADS=16; RATE=16; HD=48; D=768; T=1024; FAR=512
BF=jnp.bfloat16; F32=jnp.float32
LOG2E=1.4426950408889634
NEG=-1e30
QC=512

def nn(a,b): return lax.dot_general(a,b,(((1,),(0,)),((),())),preferred_element_type=F32)
def nt(a,b): return lax.dot_general(a,b,(((1,),(1,)),((),())),preferred_element_type=F32)

def attn_kernel(len_ref, k_ref, v_ref, qT_ref, kT_ref, vT_ref, gT_ref, far_ref, kfT_ref, vfT_ref, top_ref, x_ref, go_ref,
                attT_ref, dqT_ref, dk_ref, dv_ref, dk32_ref, dv32_ref, dkvf_ref, fin_ref, out_ref,
                qpad, gpad, kb, kfb, m2s, l2s, u2s, w2s, des, dqs, e2s,
                dk32, dv32, dkvf, xT, part, rx, sums, bs, br, gs, gr, hs, hr, *scratch):
    h = pl.program_id(0)
    step = lax.rem(h, 4)

    def reduction(g):
        return Reduction(scratch[0], *[ref.at[g] for ref in scratch[1:7]], fin_ref.at[g],
                         *[sem.at[g] for sem in scratch[7:]])

    def spread(g):
        return Spread(reduction(g), fin_ref.at[g], sums.at[g], gs.at[g], gr.at[g], hs.at[g], hr.at[g])

    def backs(g):
        return back_copies(part, rx.at[g], bs.at[g], br.at[g])

    now = jnp.maximum(h // 4 - 1, 0)
    before = jnp.maximum(h // 4 - 2, 0)
    low = pl.ds(pl.multiple_of(now * GR, 64), GR)

    @pl.when(h == 0)
    def _():
        greet(all_peers())

    @pl.when(h == 4)
    def _():
        xT[...] = x_ref[...].T

    @pl.when((step == 0) & (h >= 4))
    def _():
        part[...] = dkvf[lax.rem(now, 2)].T
        for c in backs(now):
            c.start()
        red = reduction(now)
        red.rows(0, nt(dqT_ref[low, :], xT[...]))
        red.pair(0).start()
        red.rows(3, nn(attT_ref[low, :], go_ref[...]))
        red.pair(3).start()

    @pl.when((step == 0) & (h >= 8))
    def _():
        reduction(before).after_second()

    @pl.when((step == 1) & (h >= 4))
    def _():
        slot = lax.rem(now, 2)
        add_back(backs(now), part, rx.at[now], now, dk32.at[slot], dv32.at[slot], dk_ref.at[low], dv_ref.at[low])
        red = reduction(now)
        red.rows(1, nt(dk_ref[low, :], xT[...]))
        red.pair(1).start()
        red.rows(2, nt(dv_ref[low, :], xT[...]))
        red.pair(2).start()

    @pl.when((step == 1) & (h >= 8))
    def _():
        reduction(before).after_third()
        spread(before).begin()

    @pl.when((step == 2) & (h >= 4))
    def _():
        reduction(now).after_pair()

    @pl.when((step == 2) & (h >= 8))
    def _():
        spread(before).middle()

    @pl.when((step == 3) & (h >= 4))
    def _():
        reduction(now).after_first()

    @pl.when((step == 3) & (h >= 8))
    def _():
        spread(before).end()

    n = len_ref[0]
    nfull = len_ref[1]
    scale = HD ** -0.5
    c = scale * LOG2E
    w0, off, free = window(h)
    r = pl.multiple_of(h * HD, 16)
    row = lax.broadcasted_iota(jnp.int32, (256, T), 0)
    qpad[...] = pad_rows(qT_ref, w0, off, row, jnp.where(row == free, 1.0, 0.0).astype(BF))
    gpad[...] = pad_rows(gT_ref, w0, off, row, jnp.zeros((256, T), BF))
    lane = lax.broadcasted_iota(jnp.int32, (T, 256), 1)
    kb[...] = jnp.where(lane == free, key_bias(n), k_ref[:, pl.ds(w0, 256)])
    fi = lax.broadcasted_iota(jnp.int32, (FAR, 1), 0)
    fbias = jnp.where(fi * RATE + h < nfull, 0.0, NEG).astype(BF)
    flane = lax.broadcasted_iota(jnp.int32, (FAR, 256), 1)
    kfb[...] = jnp.where(flane == free, fbias, far_ref[:, pl.ds(w0, 256)])
    wq = pl.multiple_of((h // 2) * 128, 128)
    qlane = lax.broadcasted_iota(jnp.int32, (1, 128), 1)
    mine = (qlane // 64) == lax.rem(h, 2)
    S2 = nn(kfb[...], qpad[:, pl.ds(wq, 128)])
    x2 = jnp.max(S2, axis=0, keepdims=True)
    e2 = jnp.exp2(S2 * c - x2 * c)
    e2s[...] = e2
    l2 = jnp.sum(e2, axis=0, keepdims=True)
    u2 = nn(vfT_ref[pl.ds(r, HD), :], e2.astype(BF))
    m2s[...] = jnp.full_like(m2s, NEG)
    l2s[...] = jnp.zeros_like(l2s)
    u2s[...] = jnp.zeros_like(u2s)
    m2s[:, pl.ds(wq, 128)] = jnp.where(mine, x2 * scale, NEG)
    l2s[:, pl.ds(wq, 128)] = jnp.where(mine, l2, 0.0)
    u2s[:, pl.ds(wq, 128)] = jnp.where(mine, u2, 0.0)
    vwin = v_ref[:, pl.ds(w0, 256)]
    vTh = vT_ref[pl.ds(r, HD), :]
    kTh = kT_ref[pl.ds(r, HD), :]
    dv = jnp.zeros((HD, T), F32)
    dk = jnp.zeros((HD, T), F32)
    for ci in range(T // QC):
        sl = slice(ci * QC, (ci + 1) * QC)
        S = nn(kb[...], qpad[:, sl])
        x1 = top_ref[h, :, sl]
        e = jnp.exp2(S * c - x1 * c)
        l1 = jnp.sum(e, axis=0, keepdims=True)
        u1 = nn(vTh, e.astype(BF))
        m1 = x1 * scale
        m2 = m2s[:, sl]; l2c = l2s[:, sl]
        M = jnp.maximum(m1, m2)
        a1 = jnp.exp(m1 - M); a2 = jnp.exp(m2 - M)
        inv = 1.0 / (a1 * l1 + a2 * l2c)
        w1 = a1 * inv; w2 = a2 * inv
        o = u1 * w1 + u2s[:, sl] * w2
        qi = lax.broadcasted_iota(jnp.int32, (1, QC), 1) + ci * QC
        ok = (lax.rem(qi, 64) * RATE + qi // 64) < n
        attT_ref[pl.ds(r, HD), sl] = jnp.where(ok, o, 0.0).astype(BF)
        gTh = gT_ref[pl.ds(r, HD), sl]
        delta = jnp.sum(gTh.astype(F32) * o, axis=0, keepdims=True)
        w2s[:, sl] = w2
        des[:, sl] = delta
        dP = nn(vwin, gpad[:, sl])
        P = e * w1
        dS = (P * (dP - delta)).astype(BF)
        dqs[:, sl] = nn(kTh, dS)
        dv += nt(gTh, P.astype(BF))
        dk += nt(qT_ref[pl.ds(r, HD), sl], dS)
    r1 = pl.multiple_of(step * HD, 16)
    slot = lax.rem(h // 4, 2)
    dv32[slot, pl.ds(r1, HD), :] = dv
    dk32[slot, pl.ds(r1, HD), :] = dk * scale
    P2 = e2s[...] * jnp.where(mine, w2s[:, pl.ds(wq, 128)], 0.0)
    dP2 = nn(far_ref[:, pl.ds(pl.multiple_of(w0 + D, 128), 256)], gpad[:, pl.ds(wq, 128)])
    dS2 = (P2 * (dP2 - des[:, pl.ds(wq, 128)])).astype(BF)
    dvf = nt(gT_ref[pl.ds(r, HD), pl.ds(wq, 128)], P2.astype(BF)).astype(BF)
    dkf = (nt(qT_ref[pl.ds(r, HD), pl.ds(wq, 128)], dS2) * scale).astype(BF)

    dkvf[slot, pl.ds(r1, HD), :] = dkf
    dkvf[slot, pl.ds(pl.multiple_of(r1 + GR, 16), HD), :] = dvf
    dqs[:, pl.ds(wq, 128)] += nn(kfT_ref[pl.ds(r, HD), :], dS2)
    dqT_ref[pl.ds(r, HD), :] = (dqs[...] * scale).astype(BF)

    @pl.when(h == HEADS - 1)
    def _():
        reduction(2).after_second()
        dk32_ref[...] = dk32[1]
        dv32_ref[...] = dv32[1]
        dkvf_ref[...] = dkvf[1]
        reduction(2).after_third()
        for g in range(3):
            reduction(g).finish()
        for g in range(2):
            spread(g).finish()
        out_ref[...] = sums[...]


def attn(lens, *arrs):
    s = jax.ShapeDtypeStruct
    dma = pltpu.SemaphoreType.DMA
    return pl.pallas_call(
        attn_kernel,
        grid=(HEADS,),
        in_specs=[sm()] + [vm()] * 12,
        out_specs=[vm()] * 9,
        out_shape=[s((D, T), BF)] * 2 + [s((3 * GR, T), BF)] * 2 + [s((GR, T), F32)] * 2 + [s((2 * GR, FAR), BF)]
        + [s((3, 3, 16, HALF), BF), s((2, 2, 4, GR, HALF), BF)],
        scratch_shapes=[
            pltpu.VMEM((256, T), BF), pltpu.VMEM((256, T), BF), pltpu.VMEM((T, 256), BF), pltpu.VMEM((FAR, 256), BF),
            pltpu.VMEM((1, T), F32), pltpu.VMEM((1, T), F32), pltpu.VMEM((HD, T), F32), pltpu.VMEM((1, T), F32),
            pltpu.VMEM((1, T), F32), pltpu.VMEM((HD, T), F32), pltpu.VMEM((FAR, 128), F32),
            pltpu.VMEM((2, GR, T), F32), pltpu.VMEM((2, GR, T), F32), pltpu.VMEM((2, 2 * GR, FAR), BF),
            pltpu.VMEM((D, T), BF), pltpu.VMEM((FAR, 2 * GR), BF), pltpu.VMEM((3, 7, 64, 2 * GR), BF),
            pltpu.VMEM((2, 2, 4, GR, HALF), BF), dma((3, 7)), dma((3, 7)), dma((2, 2, 3, 3)), dma((2, 2, 3, 3)), dma((2,)), dma((2,)),
        ] + reduction_scratch(3),
        compiler_params=pltpu.CompilerParams(
            vmem_limit_bytes=60 << 20, collective_id=4, has_side_effects=True),
        cost_estimate=pl.CostEstimate(flops=100 * T * D * D, bytes_accessed=30 << 20, transcendentals=0),
    )(lens, *arrs)


def vm():
    return pl.BlockSpec(memory_space=pltpu.VMEM)


def sm():
    return pl.BlockSpec(memory_space=pltpu.SMEM)


MESHID = pl.DeviceIdType.MESH
ORDERS = ((0, 1, 2), (1, 2, 0), (2, 0, 1))


def coords():
    s = lax.axis_index("seq")
    r = lax.axis_index("rep")
    return ((s % 2) * 2 + r // 8, s // 2, (r // 2) % 4), r % 2


def device_at(xyz, core):
    x, y, z = xyz
    return (y * 2 + x // 2, ((x % 2) * 4 + z) * 2 + core)


def along(xyz, axis, step):
    moved = list(xyz)
    moved[axis] = (xyz[axis] + step) % 4
    return tuple(moved)


def greet(peers):
    barrier = pltpu.get_barrier_semaphore()
    for peer in peers:
        pl.semaphore_signal(barrier, inc=1, device_id=peer, device_id_type=MESHID)
    pl.semaphore_wait(barrier, len(peers))


def send(src, dst, ssem, rsem, peer):
    copy = pltpu.make_async_remote_copy(
        src_ref=src, dst_ref=dst, send_sem=ssem, recv_sem=rsem, device_id=peer, device_id_type=MESHID
    )
    copy.start()
    return copy


def seq_peer(s, d):
    return (lax.rem(s + d, 8), lax.axis_index("rep"))


def window(h):
    hh = lax.rem(h, 8)
    w0 = pl.multiple_of((h // 8) * 384 + jnp.where(hh >= 5, 128, 0), 128)
    off = h * HD - w0
    return w0, off, jnp.where(off >= 48, 0, 255)


def pad_rows(ref, w0, off, rows_in, filler):
    return jnp.where((rows_in >= off) & (rows_in < off + HD), ref[pl.ds(w0, 256), :], filler)


def key_bias(n):
    ki = lax.broadcasted_iota(jnp.int32, (T, 1), 0)
    return jnp.where(lax.rem(ki, 64) * RATE + ki // 64 < n, 0.0, NEG).astype(BF)


def front_kernel(len_ref, src_ref, rows_ref, grad_ref, wq_ref, wk_ref, wv_ref, wo_ref,
                 x_ref, go_ref, k_ref, v_ref, qT_ref, kT_ref, vT_ref, gT_ref, far_ref, kfT_ref, vfT_ref, top_ref,
                 ask, req, picked, arrived, perm, qpad, kb, qs, qr, ps, pr, fs, fr):
    n = len_ref[0]
    s = lax.axis_index("seq")
    peers = [seq_peer(s, d) for d in range(1, 8)]
    greet(peers)
    src = src_ref[...]
    sixteen = lax.broadcasted_iota(jnp.int32, (16, T), 0)
    line = lax.rem(src, T)
    parts = jnp.where(sixteen == 0, line // 32, jnp.where(sixteen == 1, lax.rem(line, 32), src // T))
    spot = lax.broadcasted_iota(jnp.int32, (T, T), 0)
    reorder = (lax.broadcasted_iota(jnp.int32, (T, T), 1) == lax.rem(spot, 64) * RATE + spot // 64).astype(BF)
    parts = nt(parts.astype(F32).astype(BF), reorder)
    owner = parts[2:3].astype(jnp.int32)
    hot = (lax.broadcasted_iota(jnp.int32, (16, T), 0) == owner).astype(BF)
    before = (lax.broadcasted_iota(jnp.int32, (T, T), 0) < lax.broadcasted_iota(jnp.int32, (T, T), 1)).astype(BF)
    rank = jnp.sum(nn(hot, before) * hot.astype(F32), axis=0, keepdims=True)
    slot = owner.astype(F32) * 128.0 + rank
    where = lax.broadcasted_iota(jnp.int32, (T, T), 0).astype(F32)
    permT = (where == slot).astype(BF)
    got = nt(parts.astype(BF), permT)
    lines = got[0:1] * 32.0 + got[1:2]
    for o in range(8):
        ask[o] = jnp.broadcast_to(lines[:, o * 128:(o + 1) * 128], (8, 128))
    asks = [send(ask.at[lax.rem(s + d, 8)], req.at[d - 1], qs.at[d - 1], qr.at[d - 1], peers[d - 1])
            for d in range(1, 8)]
    perm[...] = permT.T
    qi = lax.broadcasted_iota(jnp.int32, (1, T), 1)
    ok = (lax.rem(qi, 64) * RATE + qi // 64) < n
    go_ref[...] = nn(reorder, grad_ref[...]).astype(BF)
    gT_ref[...] = jnp.where(ok, nt(wo_ref[...], go_ref[...]), 0.0).astype(BF)
    cells = lax.broadcasted_iota(jnp.int32, (128, T), 1).astype(F32)
    rows = rows_ref[...]
    mine = pl.ds(pl.multiple_of(s * 128, 128), 128)
    sends = []
    for d in range(1, 8):
        asks[d - 1].wait_recv()
        pick = (cells == req[d - 1].T[:, 0:1]).astype(BF)
        picked[d - 1] = nn(pick, rows).astype(BF)
        sends.append(send(picked.at[d - 1], arrived.at[mine], ps.at[d - 1], pr.at[d - 1], seq_peer(s, 8 - d)))
    pick = (cells == ask[s].T[:, 0:1]).astype(BF)
    arrived[mine, :] = nn(pick, rows).astype(BF)
    for c in sends:
        c.wait_recv()
    x = nn(perm[...], arrived[...]).astype(BF)
    x_ref[...] = x
    k = nn(x, wk_ref[...]).astype(BF)
    v = nn(x, wv_ref[...]).astype(BF)
    k_ref[...] = k
    v_ref[...] = v
    col = lax.broadcasted_iota(jnp.int32, (64, D), 1) // HD
    fk = jnp.zeros((64, D), BF)
    fv = jnp.zeros((64, D), BF)
    for h in range(HEADS):
        fk = jnp.where(col == h, k_ref[h * 64:(h + 1) * 64, :], fk)
        fv = jnp.where(col == h, v_ref[h * 64:(h + 1) * 64, :], fv)
    here = pl.ds(pl.multiple_of(s * 64, 64), 64)
    far_ref[here, 0:D] = fk
    far_ref[here, D:2 * D] = fv
    fars = [send(far_ref.at[here], far_ref.at[here], fs.at[d - 1], fr.at[d - 1], peers[d - 1]) for d in range(1, 8)]
    qT_ref[...] = nn(x, wq_ref[...]).astype(BF).T
    kT_ref[...] = k.T
    vT_ref[...] = v.T
    rows_in = lax.broadcasted_iota(jnp.int32, (256, T), 0)
    cols_in = lax.broadcasted_iota(jnp.int32, (T, 256), 1)
    kbias = key_bias(n)

    @pl.loop(0, HEADS)
    def _(h):
        w0, off, free = window(h)
        qpad[...] = pad_rows(qT_ref, w0, off, rows_in, jnp.where(rows_in == free, 1.0, 0.0).astype(BF))
        kb[...] = jnp.where(cols_in == free, kbias, k_ref[:, pl.ds(w0, 256)])
        for ci in range(T // QC):
            sl = slice(ci * QC, (ci + 1) * QC)
            top_ref[h, :, sl] = jnp.max(nn(kb[...], qpad[:, sl]), axis=0, keepdims=True)

    for c in fars:
        c.wait_recv()
    kfT_ref[...] = far_ref[:, 0:D].T
    vfT_ref[...] = far_ref[:, D:2 * D].T
    for c in asks + sends + fars:
        c.wait_send()


def front_all(lens, src, rows, go, wq, wk, wv, wo):
    s = jax.ShapeDtypeStruct
    dma = pltpu.SemaphoreType.DMA
    return pl.pallas_call(
        front_kernel,
        in_specs=[sm()] + [vm()] * 7,
        out_specs=[vm()] * 12,
        out_shape=[s((T, D), BF)] * 4 + [s((D, T), BF)] * 4 + [s((FAR, 2 * D), BF)] + [s((D, FAR), BF)] * 2
        + [s((HEADS, 1, T), F32)],
        scratch_shapes=[
            pltpu.VMEM((8, 8, 128), F32), pltpu.VMEM((7, 8, 128), F32), pltpu.VMEM((7, 128, D), BF),
            pltpu.VMEM((T, D), BF), pltpu.VMEM((T, T), BF), pltpu.VMEM((256, T), BF), pltpu.VMEM((T, 256), BF),
        ] + [dma((7,))] * 6,
        compiler_params=pltpu.CompilerParams(
            vmem_limit_bytes=60 << 20, collective_id=2, has_side_effects=True),
        cost_estimate=pl.CostEstimate(flops=12 * T * D * D, bytes_accessed=20 << 20, transcendentals=0),
    )(lens, src, rows, go, wq, wk, wv, wo)


HALF = D // 2
GH = HEADS // 4
GR = GH * HD


def copy_to(src, dst, ssem, rsem, peer):
    return pltpu.make_async_remote_copy(
        src_ref=src, dst_ref=dst, send_sem=ssem, recv_sem=rsem, device_id=peer, device_id_type=MESHID
    )


def all_peers():
    xyz, core = coords()
    s = lax.axis_index("seq")
    near = [device_at(along(xyz, 0, d), core) for d in (1, 3)] + [device_at(along(xyz, 2, d), core) for d in (1, 2, 3)]
    return [seq_peer(s, d) for d in range(1, 8)] + near + [device_at(xyz, 1 - core)]


class Reduction:
    def __init__(self, grads, crx, acc, rx1, rx2, rx3, r2, fin, cs, cr, ss, rs):
        self.xyz, self.core = coords()
        self.grads, self.crx, self.acc = grads, crx, acc
        self.rx1, self.rx2, self.rx3, self.r2, self.fin = rx1, rx2, rx3, r2, fin
        self.cs, self.cr, self.ss, self.rs = cs, cr, ss, rs

    def at(self, p, level):
        return self.xyz[ORDERS[p][level]]

    def peer(self, p, level, d):
        return device_at(along(self.xyz, ORDERS[p][level], d), self.core)

    def pair(self, i):
        return copy_to(self.grads.at[i, 1 - self.core], self.crx.at[i], self.cs.at[i], self.cr.at[i],
                       device_at(self.xyz, 1 - self.core))

    def wave(self, level, parts=(0, 1, 2)):
        made = []
        for p in parts:
            for d in (1, 2, 3):
                other = (self.at(p, level) + d) % 4
                if level == 0:
                    src, dst = self.acc.at[other, pl.ds(p * 64, 64)], self.rx1.at[p, d - 1]
                elif level == 1:
                    src, dst = self.r2.at[p, pl.ds(pl.multiple_of(other * 16, 16), 16)], self.rx2.at[p, d - 1]
                else:
                    own = self.rx3.at[p, self.at(p, 2)]
                    src, dst = own, own
                made.append(copy_to(src, dst, self.ss.at[level, p, d - 1], self.rs.at[level, p, d - 1],
                                    self.peer(p, level, d)))
        return made

    def start(self, copies):
        for c in copies:
            c.start()

    def rows(self, i, value):
        self.grads[i, 0] = value[:, :HALF]
        self.grads[i, 1] = value[:, HALF:]

    def after_pair(self):
        for i in (0, 3, 1, 2):
            self.pair(i).wait_recv()
            self.acc[i] = self.grads[i, self.core] + self.crx[i]
        for i in range(4):
            self.pair(i).wait_send()
        self.start(self.wave(0))

    def after_first(self):
        copies = self.wave(0)
        for p in range(3):
            for c in copies[3 * p:3 * p + 3]:
                c.wait_recv()
            self.r2[p] = self.acc[self.at(p, 0), p * 64:(p + 1) * 64] + self.rx1[p, 0] + self.rx1[p, 1] + self.rx1[p, 2]
            self.start(self.wave(1, (p,)))

    def after_second(self):
        copies = self.wave(1)
        for p in range(3):
            for c in copies[3 * p:3 * p + 3]:
                c.wait_recv()
            own = self.r2[p, pl.ds(pl.multiple_of(self.at(p, 1) * 16, 16), 16)]
            self.rx3[p, self.at(p, 2)] = own + self.rx2[p, 0] + self.rx2[p, 1] + self.rx2[p, 2]
            self.start(self.wave(2, (p,)))

    def after_third(self):
        copies = self.wave(2)
        for p in range(3):
            for c in copies[3 * p:3 * p + 3]:
                c.wait_recv()
            self.fin[p] = (self.rx3[p, 0] + self.rx3[p, 1] + self.rx3[p, 2] + self.rx3[p, 3]).astype(BF)

    def finish(self):
        for level in range(3):
            for c in self.wave(level):
                c.wait_send()


def reduction_scratch(*groups):
    dma = pltpu.SemaphoreType.DMA
    return [
        pltpu.VMEM((4, 2, GR, HALF), F32), pltpu.VMEM(groups + (4, GR, HALF), F32),
        pltpu.VMEM(groups + (4, GR, HALF), F32), pltpu.VMEM(groups + (3, 3, 64, HALF), F32),
        pltpu.VMEM(groups + (3, 3, 16, HALF), F32), pltpu.VMEM(groups + (3, 4, 16, HALF), F32),
        pltpu.VMEM(groups + (3, 64, HALF), F32), dma(groups + (4,)), dma(groups + (4,)),
        dma(groups + (3, 3, 3)), dma(groups + (3, 3, 3)),
    ]


class Spread:
    def __init__(self, red, fin, out, gs, gr, hs, hr):
        self.red, self.fin, self.out, self.gs, self.gr, self.hs, self.hr = red, fin, out, gs, gr, hs, hr

    def wave(self, level, parts=(0, 1, 2)):
        made = []
        for p in parts:
            a, b = self.red.at(p, 0), self.red.at(p, 1)
            rows = pl.ds(pl.multiple_of(p * 64 + b * 16, 16), 16) if level == 1 else pl.ds(p * 64, 64)
            here = self.out.at[self.red.core, a, rows]
            for d in (1, 2, 3):
                made.append(copy_to(here, here, self.gs.at[level, p, d - 1], self.gr.at[level, p, d - 1],
                                    self.red.peer(p, level, d)))
        return made

    def mate(self):
        here = self.out.at[self.red.core]
        return copy_to(here, here, self.hs, self.hr, device_at(self.red.xyz, 1 - self.red.core))

    def begin(self):
        for p in range(3):
            rows = pl.ds(pl.multiple_of(p * 64 + self.red.at(p, 1) * 16, 16), 16)
            self.out[self.red.core, self.red.at(p, 0), rows] = self.fin[p]
        for c in self.wave(1):
            c.start()

    def middle(self):
        for p in range(3):
            for c in self.wave(1, (p,)):
                c.wait_recv()
            for c in self.wave(0, (p,)):
                c.start()

    def end(self):
        for c in self.wave(0):
            c.wait_recv()
        self.mate().start()

    def finish(self):
        for level in range(2):
            for c in self.wave(level):
                c.wait_send()
        self.mate().wait()


def back_copies(part, rx, ss, rs):
    s = lax.axis_index("seq")
    return [copy_to(part.at[pl.ds(pl.multiple_of(lax.rem(s + d, 8) * 64, 64), 64)], rx.at[d - 1],
                    ss.at[d - 1], rs.at[d - 1], seq_peer(s, d)) for d in range(1, 8)]


def add_back(copies, part, rx, group, dk32, dv32, dk, dv):
    s = lax.axis_index("seq")
    back = part[pl.ds(pl.multiple_of(s * 64, 64), 64), :].astype(F32)
    for d in range(1, 8):
        copies[d - 1].wait_recv()
        back = back + rx[d - 1].astype(F32)
    for c in copies:
        c.wait_send()
    bT = back.T
    zero = jnp.zeros((HD, 64), F32)
    for i in range(GH):
        r = slice(i * HD, (i + 1) * HD)
        w = pl.ds(pl.multiple_of((group * 2 + i // 2) * 128, 128), 128)
        bk = bT[i * HD:(i + 1) * HD, :]
        bv = bT[GR + i * HD:GR + (i + 1) * HD, :]
        pk = [bk, zero] if i % 2 == 0 else [zero, bk]
        pv = [bv, zero] if i % 2 == 0 else [zero, bv]
        dk[r, :] = dk32[r, :].astype(BF)
        dv[r, :] = dv32[r, :].astype(BF)
        dk[r, w] = (dk32[r, w] + jnp.concatenate(pk, axis=1)).astype(BF)
        dv[r, w] = (dv32[r, w] + jnp.concatenate(pv, axis=1)).astype(BF)


def tail_kernel(x_ref, go_ref, attT_ref, dqT_ref, dk_ref, dv_ref, dk32_ref, dv32_ref, dkvf_ref, fin_ref,
                wq_ref, wk_ref, wv_ref, wo_ref, enc_ref, emb_ref, out2_ref, out3_ref,
                part, rx, dk, dv, fin3, home, bs, br, g2s, g2r, h2s, h2r, g3s, g3r, h3s, h3r, *scratch):
    greet(all_peers())
    red = Reduction(*scratch[:7], fin3, *scratch[7:])
    first = Spread(red, fin_ref.at[2], out2_ref, g2s, g2r, h2s, h2r)
    second = Spread(red, fin3, out3_ref, g3s, g3r, h3s, h3r)
    part[...] = dkvf_ref[...].T
    backs = back_copies(part, rx, bs, br)
    for c in backs:
        c.start()
    first.begin()
    last = 3 * GR
    xT = x_ref[...].T
    red.rows(0, nt(dqT_ref[last:, :], xT))
    red.pair(0).start()
    red.rows(3, nn(attT_ref[last:, :], go_ref[...]))
    red.pair(3).start()
    first.middle()
    dk[0:last, :] = dk_ref[...]
    dv[0:last, :] = dv_ref[...]
    add_back(backs, part, rx, 3, dk32_ref, dv32_ref, dk.at[last:D], dv.at[last:D])
    red.rows(1, nt(dk[last:D, :], xT))
    red.pair(1).start()
    red.rows(2, nt(dv[last:D, :], xT))
    red.pair(2).start()
    first.end()
    red.after_pair()
    enc = (x_ref[...].astype(F32) + nn(attT_ref[...].T, wo_ref[...])).astype(BF)
    spot = lax.broadcasted_iota(jnp.int32, (T, T), 0)
    home[...] = (lax.broadcasted_iota(jnp.int32, (T, T), 1) == lax.rem(spot, RATE) * 64 + spot // RATE).astype(BF)
    enc_ref[...] = nn(home[...], enc).astype(BF)
    red.after_first()
    e = nn(wq_ref[...], dqT_ref[...]) + nn(wk_ref[...], dk[...])
    red.after_second()
    e = e + nn(wv_ref[...], dv[...])
    emb = (go_ref[...].astype(F32) + e.T).astype(BF)
    red.after_third()
    second.begin()
    emb_ref[...] = nn(home[...], emb).astype(BF)
    second.middle()
    second.end()
    red.finish()
    first.finish()
    second.finish()


def tail_all(*args):
    s = jax.ShapeDtypeStruct
    dma = pltpu.SemaphoreType.DMA
    return pl.pallas_call(
        tail_kernel,
        in_specs=[vm()] * 14,
        out_specs=[vm()] * 4,
        out_shape=[s((T, D), BF)] * 2 + [s((2, 4, GR, HALF), BF)] * 2,
        scratch_shapes=[
            pltpu.VMEM((FAR, 2 * GR), BF), pltpu.VMEM((7, 64, 2 * GR), BF),
            pltpu.VMEM((D, T), BF), pltpu.VMEM((D, T), BF), pltpu.VMEM((3, 16, HALF), BF), pltpu.VMEM((T, T), BF),
            dma((7,)), dma((7,)),
        ] + [dma((2, 3, 3)), dma((2, 3, 3)), dma(()), dma(())] * 2 + reduction_scratch(),
        compiler_params=pltpu.CompilerParams(
            vmem_limit_bytes=60 << 20, collective_id=3, has_side_effects=True),
        cost_estimate=pl.CostEstimate(flops=16 * T * D * D, bytes_accessed=30 << 20, transcendentals=0),
    )(*args)


def lay_kernel(out01_ref, out2_ref, out3_ref, gq_ref, gk_ref, gv_ref, gout_ref, stage, sems):
    copies = []
    for i, to in enumerate((gq_ref, gk_ref, gv_ref, gout_ref)):
        blocks = [out01_ref.at[0], out01_ref.at[1], out2_ref, out3_ref]
        for g, block in enumerate(blocks):
            whole = jnp.concatenate([block[0, i], block[1, i]], axis=1)
            rows = slice(g * GR, (g + 1) * GR)
            if i < 3:
                stage[4, rows, :] = whole.astype(F32)
            else:
                stage[i, rows, :] = whole.astype(F32)
        if i < 3:
            stage[i] = stage[4].T
        copies.append(pltpu.make_async_copy(stage.at[i], to, sems.at[i]))
        copies[-1].start()
    for c in copies:
        c.wait()


def lay_all(out01, out2, out3):
    s = jax.ShapeDtypeStruct
    return pl.pallas_call(
        lay_kernel,
        in_specs=[vm()] * 3,
        out_specs=[pl.BlockSpec(memory_space=pl.ANY)] * 4,
        out_shape=[s((D, D), F32)] * 4,
        scratch_shapes=[pltpu.VMEM((5, D, D), F32), pltpu.SemaphoreType.DMA((4,))],
        compiler_params=pltpu.CompilerParams(vmem_limit_bytes=40 << 20),
        cost_estimate=pl.CostEstimate(flops=4 * D * D, bytes_accessed=24 * D * D, transcendentals=0),
    )(out01, out2, out3)


def per_device(tile_embed, tile_source, slide_len, grad_out, w_query, w_key, w_value, w_out):
    source = tile_source.reshape(1, T)
    length = slide_len[0]
    lens = jnp.stack([length - lax.axis_index("seq") * T, length]).astype(jnp.int32)
    x, go, k, v, qT, kT, vT, gT, far, kfT, vfT, top = front_all(
        lens, source, tile_embed[0], grad_out[0], w_query, w_key, w_value, w_out
    )
    attT, dqT, dk, dv, dk32, dv32, dkvf, fin, out01 = attn(
        lens, k, v, qT, kT, vT, gT, far, kfT, vfT, top, x, go
    )
    enc, emb, out2, out3 = tail_all(
        x, go, attT, dqT, dk, dv, dk32, dv32, dkvf, fin, w_query, w_key, w_value, w_out
    )
    summed = lay_all(out01, out2, out3)
    return (enc[None], emb[None], summed[0], summed[1], summed[2], summed[3])


def solution(mesh):
    return jax.shard_map(
        per_device,
        mesh=mesh,
        in_specs=(
            P("rep", "seq", None),
            P("rep", "seq"),
            P("rep"),
            P("rep", "seq", None),
            P(),
            P(),
            P(),
            P(),
        ),
        out_specs=(P("rep", "seq", None), P("rep", "seq", None), P(), P(), P(), P()),
        check_vma=False,
    )
```

```python
import functools

import jax
import jax.numpy as jnp
from jax import lax
from jax.experimental import pallas as pl
from jax.experimental.pallas import tpu as pltpu
from jax.sharding import PartitionSpec as P

HEADS=16; RATE=16; HD=48; D=768; T=1024; FAR=512
BF=jnp.bfloat16; F32=jnp.float32
LOG2E=1.4426950408889634
NEG=-1e30
QC=512

def nn(a,b): return lax.dot_general(a,b,(((1,),(0,)),((),())),preferred_element_type=F32)
def nt(a,b): return lax.dot_general(a,b,(((1,),(1,)),((),())),preferred_element_type=F32)

def attn_kernel(len_ref, k_ref, v_ref, qT_ref, kT_ref, vT_ref, gT_ref, far_ref, kfT_ref, vfT_ref, top_ref, x_ref, go_ref,
                attT_ref, dqT_ref, dk_ref, dv_ref, dk32_ref, dv32_ref, dkvf_ref, fin_ref, acc_ref, out_ref,
                qpad, gpad, kb, kfb, m2s, l2s, u2s, w2s, des, dqs, e2s,
                dk32, dv32, dkvf, xT, part, rx, sums, bs, br, gs, gr, hs, hr, *scratch):
    h = pl.program_id(0)
    step = lax.rem(h, 4)

    def reduction(g):
        return Reduction(scratch[0], *[ref.at[g] for ref in scratch[1:7]], fin_ref.at[g],
                         *[sem.at[g] for sem in scratch[7:]])

    def spread(g):
        return Spread(reduction(g), fin_ref.at[g], sums, gs, gr, hs, hr)

    def backs(g):
        return back_copies(part, rx.at[g], bs.at[g], br.at[g])

    now = jnp.maximum(h // 4 - 1, 0)
    before = jnp.maximum(h // 4 - 2, 0)
    low = pl.ds(pl.multiple_of(now * GR, 64), GR)

    @pl.when(h == 0)
    def _():
        greet(all_peers())

    @pl.when(h == 4)
    def _():
        xT[...] = x_ref[...].T

    @pl.when((step == 0) & (h >= 4))
    def _():
        part[...] = dkvf[lax.rem(now, 2)].T
        for c in backs(now):
            c.start()
        red = reduction(now)
        red.rows(0, nt(dqT_ref[low, :], xT[...]))
        red.pair(0).start()
        red.rows(3, nn(attT_ref[low, :], go_ref[...]))
        red.pair(3).start()

    @pl.when((step == 2) & (h >= 4))
    def _():
        slot = lax.rem(now, 2)
        add_back(backs(now), part, rx.at[now], now, dk32.at[slot], dv32.at[slot], dk_ref.at[low], dv_ref.at[low])
        red = reduction(now)
        red.rows(1, nt(dk_ref[low, :], xT[...]))
        red.pair(1).start()
        red.rows(2, nt(dv_ref[low, :], xT[...]))
        red.pair(2).start()

    @pl.when((step == 1) & (h >= 8))
    def _():
        reduction(before).after_first()

    @pl.when((step == 2) & (h >= 8))
    def _():
        reduction(before).after_second()

    @pl.when((step == 3) & (h >= 8))
    def _():
        reduction(before).after_third()

    @pl.when((step == 3) & (h >= 4))
    def _():
        reduction(now).add_pairs()

    @pl.when((step == 3) & (h >= 4) & (h < 12))
    def _():
        red = reduction(now)
        red.start(red.wave(0))

    @pl.when(h == 11)
    def _():
        spread(0).begin()

    @pl.when(h == 13)
    def _():
        spread(0).middle()

    @pl.when(h == 14)
    def _():
        spread(0).end()

    n = len_ref[0]
    nfull = len_ref[1]
    scale = HD ** -0.5
    c = scale * LOG2E
    w0, off, free = window(h)
    r = pl.multiple_of(h * HD, 16)
    row = lax.broadcasted_iota(jnp.int32, (256, T), 0)
    qpad[...] = pad_rows(qT_ref, w0, off, row, jnp.where(row == free, 1.0, 0.0).astype(BF))
    gpad[...] = pad_rows(gT_ref, w0, off, row, jnp.zeros((256, T), BF))
    lane = lax.broadcasted_iota(jnp.int32, (T, 256), 1)
    kb[...] = jnp.where(lane == free, key_bias(n), k_ref[:, pl.ds(w0, 256)])
    fi = lax.broadcasted_iota(jnp.int32, (FAR, 1), 0)
    fbias = jnp.where(fi * RATE + h < nfull, 0.0, NEG).astype(BF)
    flane = lax.broadcasted_iota(jnp.int32, (FAR, 256), 1)
    kfb[...] = jnp.where(flane == free, fbias, far_ref[:, pl.ds(w0, 256)])
    wq = pl.multiple_of((h // 2) * 128, 128)
    qlane = lax.broadcasted_iota(jnp.int32, (1, 128), 1)
    mine = (qlane // 64) == lax.rem(h, 2)
    S2 = nn(kfb[...], qpad[:, pl.ds(wq, 128)])
    x2 = jnp.max(S2, axis=0, keepdims=True)
    e2 = jnp.exp2(S2 * c - x2 * c)
    e2s[...] = e2
    l2 = jnp.sum(e2, axis=0, keepdims=True)
    u2 = nn(vfT_ref[pl.ds(r, HD), :], e2.astype(BF))
    m2s[...] = jnp.full_like(m2s, NEG)
    l2s[...] = jnp.zeros_like(l2s)
    u2s[...] = jnp.zeros_like(u2s)
    m2s[:, pl.ds(wq, 128)] = jnp.where(mine, x2 * scale, NEG)
    l2s[:, pl.ds(wq, 128)] = jnp.where(mine, l2, 0.0)
    u2s[:, pl.ds(wq, 128)] = jnp.where(mine, u2, 0.0)
    vwin = v_ref[:, pl.ds(w0, 256)]
    vTh = vT_ref[pl.ds(r, HD), :]
    kTh = kT_ref[pl.ds(r, HD), :]
    dv = jnp.zeros((HD, T), F32)
    dk = jnp.zeros((HD, T), F32)
    for ci in range(T // QC):
        sl = slice(ci * QC, (ci + 1) * QC)
        S = nn(kb[...], qpad[:, sl])
        x1 = top_ref[h, :, sl]
        e = jnp.exp2(S * c - x1 * c)
        l1 = jnp.sum(e, axis=0, keepdims=True)
        u1 = nn(vTh, e.astype(BF))
        m1 = x1 * scale
        m2 = m2s[:, sl]; l2c = l2s[:, sl]
        M = jnp.maximum(m1, m2)
        a1 = jnp.exp(m1 - M); a2 = jnp.exp(m2 - M)
        inv = 1.0 / (a1 * l1 + a2 * l2c)
        w1 = a1 * inv; w2 = a2 * inv
        o = u1 * w1 + u2s[:, sl] * w2
        qi = lax.broadcasted_iota(jnp.int32, (1, QC), 1) + ci * QC
        ok = (lax.rem(qi, 64) * RATE + qi // 64) < n
        attT_ref[pl.ds(r, HD), sl] = jnp.where(ok, o, 0.0).astype(BF)
        gTh = gT_ref[pl.ds(r, HD), sl]
        delta = jnp.sum(gTh.astype(F32) * o, axis=0, keepdims=True)
        w2s[:, sl] = w2
        des[:, sl] = delta
        dP = nn(vwin, gpad[:, sl])
        P = e * w1
        dS = (P * (dP - delta)).astype(BF)
        dqs[:, sl] = nn(kTh, dS)
        dv += nt(gTh, P.astype(BF))
        dk += nt(qT_ref[pl.ds(r, HD), sl], dS)
    r1 = pl.multiple_of(step * HD, 16)
    slot = lax.rem(h // 4, 2)
    dv32[slot, pl.ds(r1, HD), :] = dv
    dk32[slot, pl.ds(r1, HD), :] = dk * scale
    P2 = e2s[...] * jnp.where(mine, w2s[:, pl.ds(wq, 128)], 0.0)
    dP2 = nn(far_ref[:, pl.ds(pl.multiple_of(w0 + D, 128), 256)], gpad[:, pl.ds(wq, 128)])
    dS2 = (P2 * (dP2 - des[:, pl.ds(wq, 128)])).astype(BF)
    dvf = nt(gT_ref[pl.ds(r, HD), pl.ds(wq, 128)], P2.astype(BF)).astype(BF)
    dkf = (nt(qT_ref[pl.ds(r, HD), pl.ds(wq, 128)], dS2) * scale).astype(BF)

    dkvf[slot, pl.ds(r1, HD), :] = dkf
    dkvf[slot, pl.ds(pl.multiple_of(r1 + GR, 16), HD), :] = dvf
    dqs[:, pl.ds(wq, 128)] += nn(kfT_ref[pl.ds(r, HD), :], dS2)
    dqT_ref[pl.ds(r, HD), :] = (dqs[...] * scale).astype(BF)

    @pl.when(h == HEADS - 1)
    def _():
        dk32_ref[...] = dk32[1]
        dv32_ref[...] = dv32[1]
        dkvf_ref[...] = dkvf[1]
        acc_ref[...] = scratch[2][2]
        for g in range(2):
            reduction(g).finish()
        spread(0).finish()
        out_ref[...] = sums[...]


def attn(lens, *arrs):
    s = jax.ShapeDtypeStruct
    dma = pltpu.SemaphoreType.DMA
    return pl.pallas_call(
        attn_kernel,
        grid=(HEADS,),
        in_specs=[sm()] + [vm()] * 12,
        out_specs=[vm()] * 10,
        out_shape=[s((D, T), BF)] * 2 + [s((3 * GR, T), BF)] * 2 + [s((GR, T), F32)] * 2 + [s((2 * GR, FAR), BF)]
        + [s((2, 3, 16, HALF), BF), s((4, GR, HALF), F32), s((2, 4, GR, HALF), BF)],
        scratch_shapes=[
            pltpu.VMEM((256, T), BF), pltpu.VMEM((256, T), BF), pltpu.VMEM((T, 256), BF), pltpu.VMEM((FAR, 256), BF),
            pltpu.VMEM((1, T), F32), pltpu.VMEM((1, T), F32), pltpu.VMEM((HD, T), F32), pltpu.VMEM((1, T), F32),
            pltpu.VMEM((1, T), F32), pltpu.VMEM((HD, T), F32), pltpu.VMEM((FAR, 128), F32),
            pltpu.VMEM((2, GR, T), F32), pltpu.VMEM((2, GR, T), F32), pltpu.VMEM((2, 2 * GR, FAR), BF),
            pltpu.VMEM((D, T), BF), pltpu.VMEM((FAR, 2 * GR), BF), pltpu.VMEM((3, 7, 64, 2 * GR), BF),
            pltpu.VMEM((2, 4, GR, HALF), BF), dma((3, 7)), dma((3, 7)), dma((2, 3, 3)), dma((2, 3, 3)), dma(()), dma(()),
        ] + reduction_scratch(3),
        compiler_params=pltpu.CompilerParams(
            vmem_limit_bytes=60 << 20, collective_id=4, has_side_effects=True),
        cost_estimate=pl.CostEstimate(flops=100 * T * D * D, bytes_accessed=30 << 20, transcendentals=0),
    )(lens, *arrs)


def vm():
    return pl.BlockSpec(memory_space=pltpu.VMEM)


def sm():
    return pl.BlockSpec(memory_space=pltpu.SMEM)


MESHID = pl.DeviceIdType.MESH
ORDERS = ((0, 1, 2), (1, 2, 0), (2, 0, 1))


def coords():
    s = lax.axis_index("seq")
    r = lax.axis_index("rep")
    return ((s % 2) * 2 + r // 8, s // 2, (r // 2) % 4), r % 2


def device_at(xyz, core):
    x, y, z = xyz
    return (y * 2 + x // 2, ((x % 2) * 4 + z) * 2 + core)


def along(xyz, axis, step):
    moved = list(xyz)
    moved[axis] = (xyz[axis] + step) % 4
    return tuple(moved)


def greet(peers):
    barrier = pltpu.get_barrier_semaphore()
    for peer in peers:
        pl.semaphore_signal(barrier, inc=1, device_id=peer, device_id_type=MESHID)
    pl.semaphore_wait(barrier, len(peers))


def send(src, dst, ssem, rsem, peer):
    copy = pltpu.make_async_remote_copy(
        src_ref=src, dst_ref=dst, send_sem=ssem, recv_sem=rsem, device_id=peer, device_id_type=MESHID
    )
    copy.start()
    return copy


def seq_peer(s, d):
    return (lax.rem(s + d, 8), lax.axis_index("rep"))


def window(h):
    hh = lax.rem(h, 8)
    w0 = pl.multiple_of((h // 8) * 384 + jnp.where(hh >= 5, 128, 0), 128)
    off = h * HD - w0
    return w0, off, jnp.where(off >= 48, 0, 255)


def pad_rows(ref, w0, off, rows_in, filler):
    return jnp.where((rows_in >= off) & (rows_in < off + HD), ref[pl.ds(w0, 256), :], filler)


def key_bias(n):
    ki = lax.broadcasted_iota(jnp.int32, (T, 1), 0)
    return jnp.where(lax.rem(ki, 64) * RATE + ki // 64 < n, 0.0, NEG).astype(BF)


def front_kernel(len_ref, src_ref, rows_ref, grad_ref, wq_ref, wk_ref, wv_ref, wo_ref,
                 x_ref, go_ref, k_ref, v_ref, qT_ref, kT_ref, vT_ref, gT_ref, far_ref, kfT_ref, vfT_ref, top_ref,
                 ask, req, picked, arrived, perm, qpad, kb, qs, qr, ps, pr, fs, fr):
    n = len_ref[0]
    s = lax.axis_index("seq")
    peers = [seq_peer(s, d) for d in range(1, 8)]
    greet(peers)
    src = src_ref[...]
    sixteen = lax.broadcasted_iota(jnp.int32, (16, T), 0)
    line = lax.rem(src, T)
    parts = jnp.where(sixteen == 0, line // 32, jnp.where(sixteen == 1, lax.rem(line, 32), src // T))
    spot = lax.broadcasted_iota(jnp.int32, (T, T), 0)
    reorder = (lax.broadcasted_iota(jnp.int32, (T, T), 1) == lax.rem(spot, 64) * RATE + spot // 64).astype(BF)
    parts = nt(parts.astype(F32).astype(BF), reorder)
    owner = parts[2:3].astype(jnp.int32)
    hot = (lax.broadcasted_iota(jnp.int32, (16, T), 0) == owner).astype(BF)
    before = (lax.broadcasted_iota(jnp.int32, (T, T), 0) < lax.broadcasted_iota(jnp.int32, (T, T), 1)).astype(BF)
    rank = jnp.sum(nn(hot, before) * hot.astype(F32), axis=0, keepdims=True)
    slot = owner.astype(F32) * 128.0 + rank
    where = lax.broadcasted_iota(jnp.int32, (T, T), 0).astype(F32)
    permT = (where == slot).astype(BF)
    got = nt(parts.astype(BF), permT)
    lines = got[0:1] * 32.0 + got[1:2]
    for o in range(8):
        ask[o] = jnp.broadcast_to(lines[:, o * 128:(o + 1) * 128], (8, 128))
    asks = [send(ask.at[lax.rem(s + d, 8)], req.at[d - 1], qs.at[d - 1], qr.at[d - 1], peers[d - 1])
            for d in range(1, 8)]
    perm[...] = permT.T
    qi = lax.broadcasted_iota(jnp.int32, (1, T), 1)
    ok = (lax.rem(qi, 64) * RATE + qi // 64) < n
    go_ref[...] = nn(reorder, grad_ref[...]).astype(BF)
    gT_ref[...] = jnp.where(ok, nt(wo_ref[...], go_ref[...]), 0.0).astype(BF)
    cells = lax.broadcasted_iota(jnp.int32, (128, T), 1).astype(F32)
    rows = rows_ref[...]
    mine = pl.ds(pl.multiple_of(s * 128, 128), 128)
    sends = []
    for d in range(1, 8):
        asks[d - 1].wait_recv()
        pick = (cells == req[d - 1].T[:, 0:1]).astype(BF)
        picked[d - 1] = nn(pick, rows).astype(BF)
        sends.append(send(picked.at[d - 1], arrived.at[mine], ps.at[d - 1], pr.at[d - 1], seq_peer(s, 8 - d)))
    pick = (cells == ask[s].T[:, 0:1]).astype(BF)
    arrived[mine, :] = nn(pick, rows).astype(BF)
    for c in sends:
        c.wait_recv()
    x = nn(perm[...], arrived[...]).astype(BF)
    x_ref[...] = x
    k = nn(x, wk_ref[...]).astype(BF)
    v = nn(x, wv_ref[...]).astype(BF)
    k_ref[...] = k
    v_ref[...] = v
    col = lax.broadcasted_iota(jnp.int32, (64, D), 1) // HD
    fk = jnp.zeros((64, D), BF)
    fv = jnp.zeros((64, D), BF)
    for h in range(HEADS):
        fk = jnp.where(col == h, k_ref[h * 64:(h + 1) * 64, :], fk)
        fv = jnp.where(col == h, v_ref[h * 64:(h + 1) * 64, :], fv)
    here = pl.ds(pl.multiple_of(s * 64, 64), 64)
    far_ref[here, 0:D] = fk
    far_ref[here, D:2 * D] = fv
    fars = [send(far_ref.at[here], far_ref.at[here], fs.at[d - 1], fr.at[d - 1], peers[d - 1]) for d in range(1, 8)]
    qT_ref[...] = nn(x, wq_ref[...]).astype(BF).T
    kT_ref[...] = k.T
    vT_ref[...] = v.T
    rows_in = lax.broadcasted_iota(jnp.int32, (256, T), 0)
    cols_in = lax.broadcasted_iota(jnp.int32, (T, 256), 1)
    kbias = key_bias(n)

    @pl.loop(0, HEADS)
    def _(h):
        w0, off, free = window(h)
        qpad[...] = pad_rows(qT_ref, w0, off, rows_in, jnp.where(rows_in == free, 1.0, 0.0).astype(BF))
        kb[...] = jnp.where(cols_in == free, kbias, k_ref[:, pl.ds(w0, 256)])
        for ci in range(T // QC):
            sl = slice(ci * QC, (ci + 1) * QC)
            top_ref[h, :, sl] = jnp.max(nn(kb[...], qpad[:, sl]), axis=0, keepdims=True)

    for c in fars:
        c.wait_recv()
    kfT_ref[...] = far_ref[:, 0:D].T
    vfT_ref[...] = far_ref[:, D:2 * D].T
    for c in asks + sends + fars:
        c.wait_send()


def front_all(lens, src, rows, go, wq, wk, wv, wo):
    s = jax.ShapeDtypeStruct
    dma = pltpu.SemaphoreType.DMA
    return pl.pallas_call(
        front_kernel,
        in_specs=[sm()] + [vm()] * 7,
        out_specs=[vm()] * 12,
        out_shape=[s((T, D), BF)] * 4 + [s((D, T), BF)] * 4 + [s((FAR, 2 * D), BF)] + [s((D, FAR), BF)] * 2
        + [s((HEADS, 1, T), F32)],
        scratch_shapes=[
            pltpu.VMEM((8, 8, 128), F32), pltpu.VMEM((7, 8, 128), F32), pltpu.VMEM((7, 128, D), BF),
            pltpu.VMEM((T, D), BF), pltpu.VMEM((T, T), BF), pltpu.VMEM((256, T), BF), pltpu.VMEM((T, 256), BF),
        ] + [dma((7,))] * 6,
        compiler_params=pltpu.CompilerParams(
            vmem_limit_bytes=60 << 20, collective_id=2, has_side_effects=True),
        cost_estimate=pl.CostEstimate(flops=12 * T * D * D, bytes_accessed=20 << 20, transcendentals=0),
    )(lens, src, rows, go, wq, wk, wv, wo)


HALF = D // 2
GH = HEADS // 4
GR = GH * HD


def copy_to(src, dst, ssem, rsem, peer):
    return pltpu.make_async_remote_copy(
        src_ref=src, dst_ref=dst, send_sem=ssem, recv_sem=rsem, device_id=peer, device_id_type=MESHID
    )


def all_peers():
    xyz, core = coords()
    s = lax.axis_index("seq")
    near = [device_at(along(xyz, 0, d), core) for d in (1, 3)] + [device_at(along(xyz, 2, d), core) for d in (1, 2, 3)]
    return [seq_peer(s, d) for d in range(1, 8)] + near + [device_at(xyz, 1 - core)]


class Reduction:
    def __init__(self, grads, crx, acc, rx1, rx2, rx3, r2, fin, cs, cr, ss, rs):
        self.xyz, self.core = coords()
        self.grads, self.crx, self.acc = grads, crx, acc
        self.rx1, self.rx2, self.rx3, self.r2, self.fin = rx1, rx2, rx3, r2, fin
        self.cs, self.cr, self.ss, self.rs = cs, cr, ss, rs

    def at(self, p, level):
        return self.xyz[ORDERS[p][level]]

    def peer(self, p, level, d):
        return device_at(along(self.xyz, ORDERS[p][level], d), self.core)

    def pair(self, i):
        return copy_to(self.grads.at[i, 1 - self.core], self.crx.at[i], self.cs.at[i], self.cr.at[i],
                       device_at(self.xyz, 1 - self.core))

    def wave(self, level, parts=(0, 1, 2)):
        made = []
        for p in parts:
            for d in (1, 2, 3):
                other = (self.at(p, level) + d) % 4
                if level == 0:
                    src, dst = self.acc.at[other, pl.ds(p * 64, 64)], self.rx1.at[p, d - 1]
                elif level == 1:
                    src, dst = self.r2.at[p, pl.ds(pl.multiple_of(other * 16, 16), 16)], self.rx2.at[p, d - 1]
                else:
                    own = self.rx3.at[p, self.at(p, 2)]
                    src, dst = own, own
                made.append(copy_to(src, dst, self.ss.at[level, p, d - 1], self.rs.at[level, p, d - 1],
                                    self.peer(p, level, d)))
        return made

    def start(self, copies):
        for c in copies:
            c.start()

    def rows(self, i, value):
        self.grads[i, 0] = value[:, :HALF]
        self.grads[i, 1] = value[:, HALF:]

    def add_pairs(self):
        for i in (0, 3, 1, 2):
            self.pair(i).wait_recv()
            self.acc[i] = self.grads[i, self.core] + self.crx[i]
        for i in range(4):
            self.pair(i).wait_send()

    def after_first(self):
        copies = self.wave(0)
        for p in range(3):
            for c in copies[3 * p:3 * p + 3]:
                c.wait_recv()
            self.r2[p] = self.acc[self.at(p, 0), p * 64:(p + 1) * 64] + self.rx1[p, 0] + self.rx1[p, 1] + self.rx1[p, 2]
            self.start(self.wave(1, (p,)))

    def after_second(self):
        copies = self.wave(1)
        for p in range(3):
            for c in copies[3 * p:3 * p + 3]:
                c.wait_recv()
            own = self.r2[p, pl.ds(pl.multiple_of(self.at(p, 1) * 16, 16), 16)]
            self.rx3[p, self.at(p, 2)] = own + self.rx2[p, 0] + self.rx2[p, 1] + self.rx2[p, 2]
            self.start(self.wave(2, (p,)))

    def after_third(self):
        copies = self.wave(2)
        for p in range(3):
            for c in copies[3 * p:3 * p + 3]:
                c.wait_recv()
            self.fin[p] = (self.rx3[p, 0] + self.rx3[p, 1] + self.rx3[p, 2] + self.rx3[p, 3]).astype(BF)

    def finish(self):
        for level in range(3):
            for c in self.wave(level):
                c.wait_send()


def reduction_scratch(*groups):
    dma = pltpu.SemaphoreType.DMA
    return [
        pltpu.VMEM((4, 2, GR, HALF), F32), pltpu.VMEM(groups + (4, GR, HALF), F32),
        pltpu.VMEM(groups + (4, GR, HALF), F32), pltpu.VMEM(groups + (3, 3, 64, HALF), F32),
        pltpu.VMEM(groups + (3, 3, 16, HALF), F32), pltpu.VMEM(groups + (3, 4, 16, HALF), F32),
        pltpu.VMEM(groups + (3, 64, HALF), F32), dma(groups + (4,)), dma(groups + (4,)),
        dma(groups + (3, 3, 3)), dma(groups + (3, 3, 3)),
    ]


class Spread:
    def __init__(self, red, fin, out, gs, gr, hs, hr):
        self.red, self.fin, self.out, self.gs, self.gr, self.hs, self.hr = red, fin, out, gs, gr, hs, hr

    def wave(self, level, parts=(0, 1, 2)):
        made = []
        for p in parts:
            a, b = self.red.at(p, 0), self.red.at(p, 1)
            rows = pl.ds(pl.multiple_of(p * 64 + b * 16, 16), 16) if level == 1 else pl.ds(p * 64, 64)
            here = self.out.at[self.red.core, a, rows]
            for d in (1, 2, 3):
                made.append(copy_to(here, here, self.gs.at[level, p, d - 1], self.gr.at[level, p, d - 1],
                                    self.red.peer(p, level, d)))
        return made

    def mate(self):
        here = self.out.at[self.red.core]
        return copy_to(here, here, self.hs, self.hr, device_at(self.red.xyz, 1 - self.red.core))

    def begin(self):
        for p in range(3):
            rows = pl.ds(pl.multiple_of(p * 64 + self.red.at(p, 1) * 16, 16), 16)
            self.out[self.red.core, self.red.at(p, 0), rows] = self.fin[p]
        for c in self.wave(1):
            c.start()

    def middle(self):
        for p in range(3):
            for c in self.wave(1, (p,)):
                c.wait_recv()
            for c in self.wave(0, (p,)):
                c.start()

    def end(self):
        for c in self.wave(0):
            c.wait_recv()
        self.mate().start()

    def finish(self):
        for level in range(2):
            for c in self.wave(level):
                c.wait_send()
        self.mate().wait()


def back_copies(part, rx, ss, rs):
    s = lax.axis_index("seq")
    return [copy_to(part.at[pl.ds(pl.multiple_of(lax.rem(s + d, 8) * 64, 64), 64)], rx.at[d - 1],
                    ss.at[d - 1], rs.at[d - 1], seq_peer(s, d)) for d in range(1, 8)]


def add_back(copies, part, rx, group, dk32, dv32, dk, dv):
    s = lax.axis_index("seq")
    back = part[pl.ds(pl.multiple_of(s * 64, 64), 64), :].astype(F32)
    for d in range(1, 8):
        copies[d - 1].wait_recv()
        back = back + rx[d - 1].astype(F32)
    for c in copies:
        c.wait_send()
    bT = back.T
    zero = jnp.zeros((HD, 64), F32)
    for i in range(GH):
        r = slice(i * HD, (i + 1) * HD)
        w = pl.ds(pl.multiple_of((group * 2 + i // 2) * 128, 128), 128)
        bk = bT[i * HD:(i + 1) * HD, :]
        bv = bT[GR + i * HD:GR + (i + 1) * HD, :]
        pk = [bk, zero] if i % 2 == 0 else [zero, bk]
        pv = [bv, zero] if i % 2 == 0 else [zero, bv]
        dk[r, :] = dk32[r, :].astype(BF)
        dv[r, :] = dv32[r, :].astype(BF)
        dk[r, w] = (dk32[r, w] + jnp.concatenate(pk, axis=1)).astype(BF)
        dv[r, w] = (dv32[r, w] + jnp.concatenate(pv, axis=1)).astype(BF)


def tail_kernel(x_ref, go_ref, attT_ref, dqT_ref, dk_ref, dv_ref, dk32_ref, dv32_ref, dkvf_ref, fin_ref, acc_ref,
                wq_ref, wk_ref, wv_ref, wo_ref, enc_ref, emb_ref, out1_ref, out2_ref, out3_ref,
                part, rx, dk, dv, fin2, fin3, home, bs, br, *scratch):
    greet(all_peers())
    sems, older, newer = scratch[:12], scratch[12:18], scratch[18:]
    red2 = Reduction(None, None, acc_ref, *older[:4], fin2, None, None, *older[4:])
    red3 = Reduction(*newer[:7], fin3, *newer[7:])
    spread1 = Spread(red2, fin_ref.at[1], out1_ref, *sems[0:4])
    spread2 = Spread(red2, fin2, out2_ref, *sems[4:8])
    spread3 = Spread(red3, fin3, out3_ref, *sems[8:12])
    part[...] = dkvf_ref[...].T
    backs = back_copies(part, rx, bs, br)
    for c in backs:
        c.start()
    spread1.begin()
    red2.start(red2.wave(0))
    last = 3 * GR
    xT = x_ref[...].T
    red3.rows(0, nt(dqT_ref[last:, :], xT))
    red3.pair(0).start()
    red3.rows(3, nn(attT_ref[last:, :], go_ref[...]))
    red3.pair(3).start()
    spread1.middle()
    dk[0:last, :] = dk_ref[...]
    dv[0:last, :] = dv_ref[...]
    spot = lax.broadcasted_iota(jnp.int32, (T, T), 0)
    home[...] = (lax.broadcasted_iota(jnp.int32, (T, T), 1) == lax.rem(spot, RATE) * 64 + spot // RATE).astype(BF)
    red2.after_first()
    add_back(backs, part, rx, 3, dk32_ref, dv32_ref, dk.at[last:D], dv.at[last:D])
    red3.rows(1, nt(dk[last:D, :], xT))
    red3.pair(1).start()
    red3.rows(2, nt(dv[last:D, :], xT))
    red3.pair(2).start()
    spread1.end()
    red2.after_second()
    red3.add_pairs()
    red3.start(red3.wave(0))
    enc = (x_ref[...].astype(F32) + nn(attT_ref[...].T, wo_ref[...])).astype(BF)
    red2.after_third()
    spread2.begin()
    enc_ref[...] = nn(home[...], enc).astype(BF)
    red3.after_first()
    spread2.middle()
    e = nn(wq_ref[...], dqT_ref[...]) + nn(wk_ref[...], dk[...])
    red3.after_second()
    spread2.end()
    e = e + nn(wv_ref[...], dv[...])
    red3.after_third()
    spread3.begin()
    emb = (go_ref[...].astype(F32) + e.T).astype(BF)
    spread3.middle()
    emb_ref[...] = nn(home[...], emb).astype(BF)
    spread3.end()
    red2.finish()
    red3.finish()
    for spread in (spread1, spread2, spread3):
        spread.finish()


def tail_all(*args):
    s = jax.ShapeDtypeStruct
    dma = pltpu.SemaphoreType.DMA
    older = reduction_scratch()
    return pl.pallas_call(
        tail_kernel,
        in_specs=[vm()] * 15,
        out_specs=[vm()] * 5,
        out_shape=[s((T, D), BF)] * 2 + [s((2, 4, GR, HALF), BF)] * 3,
        scratch_shapes=[
            pltpu.VMEM((FAR, 2 * GR), BF), pltpu.VMEM((7, 64, 2 * GR), BF),
            pltpu.VMEM((D, T), BF), pltpu.VMEM((D, T), BF), pltpu.VMEM((3, 16, HALF), BF),
            pltpu.VMEM((3, 16, HALF), BF), pltpu.VMEM((T, T), BF), dma((7,)), dma((7,)),
        ] + [dma((2, 3, 3)), dma((2, 3, 3)), dma(()), dma(())] * 3 + older[3:7] + older[9:] + reduction_scratch(),
        compiler_params=pltpu.CompilerParams(
            vmem_limit_bytes=60 << 20, collective_id=3, has_side_effects=True),
        cost_estimate=pl.CostEstimate(flops=16 * T * D * D, bytes_accessed=30 << 20, transcendentals=0),
    )(*args)


def lay_kernel(out0_ref, out1_ref, out2_ref, out3_ref, gq_ref, gk_ref, gv_ref, gout_ref, stage, sems):
    copies = []
    for i, to in enumerate((gq_ref, gk_ref, gv_ref, gout_ref)):
        blocks = [out0_ref, out1_ref, out2_ref, out3_ref]
        for g, block in enumerate(blocks):
            whole = jnp.concatenate([block[0, i], block[1, i]], axis=1)
            rows = slice(g * GR, (g + 1) * GR)
            if i < 3:
                stage[4, rows, :] = whole.astype(F32)
            else:
                stage[i, rows, :] = whole.astype(F32)
        if i < 3:
            stage[i] = stage[4].T
        copies.append(pltpu.make_async_copy(stage.at[i], to, sems.at[i]))
        copies[-1].start()
    for c in copies:
        c.wait()


def lay_all(out0, out1, out2, out3):
    s = jax.ShapeDtypeStruct
    return pl.pallas_call(
        lay_kernel,
        in_specs=[vm()] * 4,
        out_specs=[pl.BlockSpec(memory_space=pl.ANY)] * 4,
        out_shape=[s((D, D), F32)] * 4,
        scratch_shapes=[pltpu.VMEM((5, D, D), F32), pltpu.SemaphoreType.DMA((4,))],
        compiler_params=pltpu.CompilerParams(vmem_limit_bytes=40 << 20),
        cost_estimate=pl.CostEstimate(flops=4 * D * D, bytes_accessed=24 * D * D, transcendentals=0),
    )(out0, out1, out2, out3)


def per_device(tile_embed, tile_source, slide_len, grad_out, w_query, w_key, w_value, w_out):
    source = tile_source.reshape(1, T)
    length = slide_len[0]
    lens = jnp.stack([length - lax.axis_index("seq") * T, length]).astype(jnp.int32)
    x, go, k, v, qT, kT, vT, gT, far, kfT, vfT, top = front_all(
        lens, source, tile_embed[0], grad_out[0], w_query, w_key, w_value, w_out
    )
    attT, dqT, dk, dv, dk32, dv32, dkvf, fin, acc, out0 = attn(
        lens, k, v, qT, kT, vT, gT, far, kfT, vfT, top, x, go
    )
    enc, emb, out1, out2, out3 = tail_all(
        x, go, attT, dqT, dk, dv, dk32, dv32, dkvf, fin, acc, w_query, w_key, w_value, w_out
    )
    summed = lay_all(out0, out1, out2, out3)
    return (enc[None], emb[None], summed[0], summed[1], summed[2], summed[3])


def solution(mesh):
    return jax.shard_map(
        per_device,
        mesh=mesh,
        in_specs=(
            P("rep", "seq", None),
            P("rep", "seq"),
            P("rep"),
            P("rep", "seq", None),
            P(),
            P(),
            P(),
            P(),
        ),
        out_specs=(P("rep", "seq", None), P("rep", "seq", None), P(), P(), P(), P()),
        check_vma=False,
    )
```

```python
import functools

import jax
import jax.numpy as jnp
from jax import lax
from jax.experimental import pallas as pl
from jax.experimental.pallas import tpu as pltpu
from jax.sharding import PartitionSpec as P

HEADS=16; RATE=16; HD=48; D=768; T=1024; FAR=512
BF=jnp.bfloat16; F32=jnp.float32
LOG2E=1.4426950408889634
NEG=-1e30
QC=512

def nn(a,b): return lax.dot_general(a,b,(((1,),(0,)),((),())),preferred_element_type=F32)
def nt(a,b): return lax.dot_general(a,b,(((1,),(1,)),((),())),preferred_element_type=F32)

def attn_kernel(len_ref, k_ref, v_ref, qT_ref, kT_ref, vT_ref, gT_ref, far_ref, kfT_ref, vfT_ref, top_ref, x_hbm, go_hbm,
                attT_ref, dqT_ref, dk_ref, dv_ref, dk32_ref, dv32_ref, dkvf_ref, fin_ref, acc_ref, out_ref,
                x_ref, go_ref, ins, qpad, gpad, kb, kfb, m2s, l2s, u2s, w2s, des, dqs, e2s,
                dk32, dv32, dkvf, xT, part, rx, sums, bs, br, gs, gr, hs, hr, *scratch):
    h = pl.program_id(0)
    step = lax.rem(h, 4)

    def reduction(g):
        return Reduction(scratch[0], *[ref.at[g] for ref in scratch[1:7]], fin_ref.at[g],
                         *[sem.at[g] for sem in scratch[7:]])

    def spread(g):
        return Spread(reduction(g), fin_ref.at[g], sums, gs, gr, hs, hr)

    def backs(g):
        return back_copies(part, rx.at[g], bs.at[g], br.at[g])

    now = jnp.maximum(h // 4 - 1, 0)
    before = jnp.maximum(h // 4 - 2, 0)
    low = pl.ds(pl.multiple_of(now * GR, 64), GR)

    fetch = [pltpu.make_async_copy(x_hbm, x_ref, ins.at[0]), pltpu.make_async_copy(go_hbm, go_ref, ins.at[1])]

    @pl.when(h == 0)
    def _():
        for c in fetch:
            c.start()
        greet(all_peers())

    @pl.when(h == 4)
    def _():
        for c in fetch:
            c.wait()
        xT[...] = x_ref[...].T

    @pl.when((step == 0) & (h >= 4))
    def _():
        part[...] = dkvf[lax.rem(now, 2)].T
        for c in backs(now):
            c.start()
        red = reduction(now)
        red.rows(0, nt(dqT_ref[low, :], xT[...]))
        red.pair(0).start()
        red.rows(3, nn(attT_ref[low, :], go_ref[...]))
        red.pair(3).start()

    @pl.when((step == 2) & (h >= 4))
    def _():
        slot = lax.rem(now, 2)
        add_back(backs(now), part, rx.at[now], now, dk32.at[slot], dv32.at[slot], dk_ref.at[low], dv_ref.at[low])
        red = reduction(now)
        red.rows(1, nt(dk_ref[low, :], xT[...]))
        red.pair(1).start()
        red.rows(2, nt(dv_ref[low, :], xT[...]))
        red.pair(2).start()

    @pl.when((step == 1) & (h >= 8))
    def _():
        reduction(before).after_first()

    @pl.when((step == 2) & (h >= 8))
    def _():
        reduction(before).after_second()

    @pl.when((step == 3) & (h >= 8))
    def _():
        reduction(before).after_third()

    @pl.when((step == 3) & (h >= 4))
    def _():
        reduction(now).add_pairs()

    @pl.when((step == 3) & (h >= 4) & (h < 12))
    def _():
        red = reduction(now)
        red.start(red.wave(0))

    @pl.when(h == 11)
    def _():
        spread(0).begin()

    @pl.when(h == 13)
    def _():
        spread(0).middle()

    @pl.when(h == 14)
    def _():
        spread(0).end()

    n = len_ref[0]
    nfull = len_ref[1]
    scale = HD ** -0.5
    c = scale * LOG2E
    w0, off, free = window(h)
    r = pl.multiple_of(h * HD, 16)
    row = lax.broadcasted_iota(jnp.int32, (256, T), 0)
    qpad[...] = pad_rows(qT_ref, w0, off, row, jnp.where(row == free, 1.0, 0.0).astype(BF))
    gpad[...] = pad_rows(gT_ref, w0, off, row, jnp.zeros((256, T), BF))
    lane = lax.broadcasted_iota(jnp.int32, (T, 256), 1)
    kb[...] = jnp.where(lane == free, key_bias(n), k_ref[:, pl.ds(w0, 256)])
    fi = lax.broadcasted_iota(jnp.int32, (FAR, 1), 0)
    fbias = jnp.where(fi * RATE + h < nfull, 0.0, NEG).astype(BF)
    flane = lax.broadcasted_iota(jnp.int32, (FAR, 256), 1)
    kfb[...] = jnp.where(flane == free, fbias, far_ref[:, pl.ds(w0, 256)])
    wq = pl.multiple_of((h // 2) * 128, 128)
    qlane = lax.broadcasted_iota(jnp.int32, (1, 128), 1)
    mine = (qlane // 64) == lax.rem(h, 2)
    S2 = nn(kfb[...], qpad[:, pl.ds(wq, 128)])
    x2 = jnp.max(S2, axis=0, keepdims=True)
    e2 = jnp.exp2(S2 * c - x2 * c)
    e2s[...] = e2
    l2 = jnp.sum(e2, axis=0, keepdims=True)
    u2 = nn(vfT_ref[pl.ds(r, HD), :], e2.astype(BF))
    m2s[...] = jnp.full_like(m2s, NEG)
    l2s[...] = jnp.zeros_like(l2s)
    u2s[...] = jnp.zeros_like(u2s)
    m2s[:, pl.ds(wq, 128)] = jnp.where(mine, x2 * scale, NEG)
    l2s[:, pl.ds(wq, 128)] = jnp.where(mine, l2, 0.0)
    u2s[:, pl.ds(wq, 128)] = jnp.where(mine, u2, 0.0)
    vwin = v_ref[:, pl.ds(w0, 256)]
    vTh = vT_ref[pl.ds(r, HD), :]
    kTh = kT_ref[pl.ds(r, HD), :]
    dv = jnp.zeros((HD, T), F32)
    dk = jnp.zeros((HD, T), F32)
    for ci in range(T // QC):
        sl = slice(ci * QC, (ci + 1) * QC)
        S = nn(kb[...], qpad[:, sl])
        x1 = top_ref[h, :, sl]
        e = jnp.exp2(S * c - x1 * c)
        l1 = jnp.sum(e, axis=0, keepdims=True)
        u1 = nn(vTh, e.astype(BF))
        m1 = x1 * scale
        m2 = m2s[:, sl]; l2c = l2s[:, sl]
        M = jnp.maximum(m1, m2)
        a1 = jnp.exp(m1 - M); a2 = jnp.exp(m2 - M)
        inv = 1.0 / (a1 * l1 + a2 * l2c)
        w1 = a1 * inv; w2 = a2 * inv
        o = u1 * w1 + u2s[:, sl] * w2
        qi = lax.broadcasted_iota(jnp.int32, (1, QC), 1) + ci * QC
        ok = (lax.rem(qi, 64) * RATE + qi // 64) < n
        attT_ref[pl.ds(r, HD), sl] = jnp.where(ok, o, 0.0).astype(BF)
        gTh = gT_ref[pl.ds(r, HD), sl]
        delta = jnp.sum(gTh.astype(F32) * o, axis=0, keepdims=True)
        w2s[:, sl] = w2
        des[:, sl] = delta
        dP = nn(vwin, gpad[:, sl])
        P = e * w1
        dS = (P * (dP - delta)).astype(BF)
        dqs[:, sl] = nn(kTh, dS)
        dv += nt(gTh, P.astype(BF))
        dk += nt(qT_ref[pl.ds(r, HD), sl], dS)
    r1 = pl.multiple_of(step * HD, 16)
    slot = lax.rem(h // 4, 2)
    dv32[slot, pl.ds(r1, HD), :] = dv
    dk32[slot, pl.ds(r1, HD), :] = dk * scale
    P2 = e2s[...] * jnp.where(mine, w2s[:, pl.ds(wq, 128)], 0.0)
    dP2 = nn(far_ref[:, pl.ds(pl.multiple_of(w0 + D, 128), 256)], gpad[:, pl.ds(wq, 128)])
    dS2 = (P2 * (dP2 - des[:, pl.ds(wq, 128)])).astype(BF)
    dvf = nt(gT_ref[pl.ds(r, HD), pl.ds(wq, 128)], P2.astype(BF)).astype(BF)
    dkf = (nt(qT_ref[pl.ds(r, HD), pl.ds(wq, 128)], dS2) * scale).astype(BF)

    dkvf[slot, pl.ds(r1, HD), :] = dkf
    dkvf[slot, pl.ds(pl.multiple_of(r1 + GR, 16), HD), :] = dvf
    dqs[:, pl.ds(wq, 128)] += nn(kfT_ref[pl.ds(r, HD), :], dS2)
    dqT_ref[pl.ds(r, HD), :] = (dqs[...] * scale).astype(BF)

    @pl.when(h == HEADS - 1)
    def _():
        dk32_ref[...] = dk32[1]
        dv32_ref[...] = dv32[1]
        dkvf_ref[...] = dkvf[1]
        acc_ref[...] = scratch[2][2]
        for g in range(2):
            reduction(g).finish()
        spread(0).finish()
        out_ref[...] = sums[...]


def attn(lens, *arrs):
    s = jax.ShapeDtypeStruct
    dma = pltpu.SemaphoreType.DMA
    return pl.pallas_call(
        attn_kernel,
        grid=(HEADS,),
        in_specs=[sm()] + [vm()] * 10 + [hbm()] * 2,
        out_specs=[vm()] * 10,
        out_shape=[s((D, T), BF)] * 2 + [s((3 * GR, T), BF)] * 2 + [s((GR, T), F32)] * 2 + [s((2 * GR, FAR), BF)]
        + [s((2, 3, 16, HALF), BF), s((4, GR, HALF), F32), s((2, 4, GR, HALF), BF)],
        scratch_shapes=[
            pltpu.VMEM((T, D), BF), pltpu.VMEM((T, D), BF), dma((2,)),
            pltpu.VMEM((256, T), BF), pltpu.VMEM((256, T), BF), pltpu.VMEM((T, 256), BF), pltpu.VMEM((FAR, 256), BF),
            pltpu.VMEM((1, T), F32), pltpu.VMEM((1, T), F32), pltpu.VMEM((HD, T), F32), pltpu.VMEM((1, T), F32),
            pltpu.VMEM((1, T), F32), pltpu.VMEM((HD, T), F32), pltpu.VMEM((FAR, 128), F32),
            pltpu.VMEM((2, GR, T), F32), pltpu.VMEM((2, GR, T), F32), pltpu.VMEM((2, 2 * GR, FAR), BF),
            pltpu.VMEM((D, T), BF), pltpu.VMEM((FAR, 2 * GR), BF), pltpu.VMEM((3, 7, 64, 2 * GR), BF),
            pltpu.VMEM((2, 4, GR, HALF), BF), dma((3, 7)), dma((3, 7)), dma((2, 3, 3)), dma((2, 3, 3)), dma(()), dma(()),
        ] + reduction_scratch(3),
        compiler_params=pltpu.CompilerParams(
            vmem_limit_bytes=60 << 20, collective_id=4, has_side_effects=True),
        cost_estimate=pl.CostEstimate(flops=100 * T * D * D, bytes_accessed=30 << 20, transcendentals=0),
    )(lens, *arrs)


def vm():
    return pl.BlockSpec(memory_space=pltpu.VMEM)


def hbm():
    return pl.BlockSpec(memory_space=pl.ANY)


def sm():
    return pl.BlockSpec(memory_space=pltpu.SMEM)


MESHID = pl.DeviceIdType.MESH
ORDERS = ((0, 1, 2), (1, 2, 0), (2, 0, 1))


def coords():
    s = lax.axis_index("seq")
    r = lax.axis_index("rep")
    return ((s % 2) * 2 + r // 8, s // 2, (r // 2) % 4), r % 2


def device_at(xyz, core):
    x, y, z = xyz
    return (y * 2 + x // 2, ((x % 2) * 4 + z) * 2 + core)


def along(xyz, axis, step):
    moved = list(xyz)
    moved[axis] = (xyz[axis] + step) % 4
    return tuple(moved)


def greet(peers):
    barrier = pltpu.get_barrier_semaphore()
    for peer in peers:
        pl.semaphore_signal(barrier, inc=1, device_id=peer, device_id_type=MESHID)
    pl.semaphore_wait(barrier, len(peers))


def send(src, dst, ssem, rsem, peer):
    copy = pltpu.make_async_remote_copy(
        src_ref=src, dst_ref=dst, send_sem=ssem, recv_sem=rsem, device_id=peer, device_id_type=MESHID
    )
    copy.start()
    return copy


def seq_peer(s, d):
    return (lax.rem(s + d, 8), lax.axis_index("rep"))


def window(h):
    hh = lax.rem(h, 8)
    w0 = pl.multiple_of((h // 8) * 384 + jnp.where(hh >= 5, 128, 0), 128)
    off = h * HD - w0
    return w0, off, jnp.where(off >= 48, 0, 255)


def pad_rows(ref, w0, off, rows_in, filler):
    return jnp.where((rows_in >= off) & (rows_in < off + HD), ref[pl.ds(w0, 256), :], filler)


def key_bias(n):
    ki = lax.broadcasted_iota(jnp.int32, (T, 1), 0)
    return jnp.where(lax.rem(ki, 64) * RATE + ki // 64 < n, 0.0, NEG).astype(BF)


def front_kernel(len_ref, src_ref, rows_ref, grad_hbm, wq_hbm, wk_hbm, wv_hbm, wo_hbm,
                 x_out, go_out, k_out, v_out, qT_out, kT_out, vT_out, gT_out, far_out, kfT_out, vfT_out, top_out,
                 x_ref, go_ref, k_ref, v_ref, qT_ref, kT_ref, vT_ref, gT_ref, far_ref, kfT_ref, vfT_ref, top_ref,
                 grad_ref, wq_ref, wk_ref, wv_ref, wo_ref,
                 ask, req, picked, arrived, perm, qpad, kb, ins, outs, qs, qr, ps, pr, fs, fr):
    n = len_ref[0]
    fetch = [pltpu.make_async_copy(a, b, ins.at[i]) for i, (a, b) in enumerate((
        (grad_hbm, grad_ref), (wo_hbm, wo_ref), (wk_hbm, wk_ref), (wv_hbm, wv_ref), (wq_hbm, wq_ref)))]
    for c in fetch:
        c.start()
    store = [pltpu.make_async_copy(a, b, outs.at[i]) for i, (a, b) in enumerate((
        (x_ref, x_out), (go_ref, go_out), (k_ref, k_out), (v_ref, v_out), (qT_ref, qT_out), (kT_ref, kT_out),
        (vT_ref, vT_out), (gT_ref, gT_out), (far_ref, far_out), (kfT_ref, kfT_out), (vfT_ref, vfT_out),
        (top_ref, top_out)))]
    s = lax.axis_index("seq")
    peers = [seq_peer(s, d) for d in range(1, 8)]
    greet(peers)
    src = src_ref[...]
    sixteen = lax.broadcasted_iota(jnp.int32, (16, T), 0)
    line = lax.rem(src, T)
    parts = jnp.where(sixteen == 0, line // 32, jnp.where(sixteen == 1, lax.rem(line, 32), src // T))
    spot = lax.broadcasted_iota(jnp.int32, (T, T), 0)
    reorder = (lax.broadcasted_iota(jnp.int32, (T, T), 1) == lax.rem(spot, 64) * RATE + spot // 64).astype(BF)
    parts = nt(parts.astype(F32).astype(BF), reorder)
    owner = parts[2:3].astype(jnp.int32)
    hot = (lax.broadcasted_iota(jnp.int32, (16, T), 0) == owner).astype(BF)
    before = (lax.broadcasted_iota(jnp.int32, (T, T), 0) < lax.broadcasted_iota(jnp.int32, (T, T), 1)).astype(BF)
    rank = jnp.sum(nn(hot, before) * hot.astype(F32), axis=0, keepdims=True)
    slot = owner.astype(F32) * 128.0 + rank
    where = lax.broadcasted_iota(jnp.int32, (T, T), 0).astype(F32)
    permT = (where == slot).astype(BF)
    got = nt(parts.astype(BF), permT)
    lines = got[0:1] * 32.0 + got[1:2]
    for o in range(8):
        ask[o] = jnp.broadcast_to(lines[:, o * 128:(o + 1) * 128], (8, 128))
    asks = [send(ask.at[lax.rem(s + d, 8)], req.at[d - 1], qs.at[d - 1], qr.at[d - 1], peers[d - 1])
            for d in range(1, 8)]
    perm[...] = permT.T
    qi = lax.broadcasted_iota(jnp.int32, (1, T), 1)
    ok = (lax.rem(qi, 64) * RATE + qi // 64) < n
    fetch[0].wait()
    fetch[1].wait()
    go_ref[...] = nn(reorder, grad_ref[...]).astype(BF)
    store[1].start()
    gT_ref[...] = jnp.where(ok, nt(wo_ref[...], go_ref[...]), 0.0).astype(BF)
    store[7].start()
    cells = lax.broadcasted_iota(jnp.int32, (128, T), 1).astype(F32)
    rows = rows_ref[...]
    mine = pl.ds(pl.multiple_of(s * 128, 128), 128)
    sends = []
    for d in range(1, 8):
        asks[d - 1].wait_recv()
        pick = (cells == req[d - 1].T[:, 0:1]).astype(BF)
        picked[d - 1] = nn(pick, rows).astype(BF)
        sends.append(send(picked.at[d - 1], arrived.at[mine], ps.at[d - 1], pr.at[d - 1], seq_peer(s, 8 - d)))
    pick = (cells == ask[s].T[:, 0:1]).astype(BF)
    arrived[mine, :] = nn(pick, rows).astype(BF)
    for c in sends:
        c.wait_recv()
    x = nn(perm[...], arrived[...]).astype(BF)
    x_ref[...] = x
    store[0].start()
    fetch[2].wait()
    fetch[3].wait()
    k = nn(x, wk_ref[...]).astype(BF)
    v = nn(x, wv_ref[...]).astype(BF)
    k_ref[...] = k
    v_ref[...] = v
    store[2].start()
    store[3].start()
    col = lax.broadcasted_iota(jnp.int32, (64, D), 1) // HD
    fk = jnp.zeros((64, D), BF)
    fv = jnp.zeros((64, D), BF)
    for h in range(HEADS):
        fk = jnp.where(col == h, k_ref[h * 64:(h + 1) * 64, :], fk)
        fv = jnp.where(col == h, v_ref[h * 64:(h + 1) * 64, :], fv)
    here = pl.ds(pl.multiple_of(s * 64, 64), 64)
    far_ref[here, 0:D] = fk
    far_ref[here, D:2 * D] = fv
    fars = [send(far_ref.at[here], far_ref.at[here], fs.at[d - 1], fr.at[d - 1], peers[d - 1]) for d in range(1, 8)]
    fetch[4].wait()
    qT_ref[...] = nn(x, wq_ref[...]).astype(BF).T
    store[4].start()
    kT_ref[...] = k.T
    store[5].start()
    vT_ref[...] = v.T
    store[6].start()
    rows_in = lax.broadcasted_iota(jnp.int32, (256, T), 0)
    cols_in = lax.broadcasted_iota(jnp.int32, (T, 256), 1)
    kbias = key_bias(n)

    @pl.loop(0, HEADS)
    def _(h):
        w0, off, free = window(h)
        qpad[...] = pad_rows(qT_ref, w0, off, rows_in, jnp.where(rows_in == free, 1.0, 0.0).astype(BF))
        kb[...] = jnp.where(cols_in == free, kbias, k_ref[:, pl.ds(w0, 256)])
        for ci in range(T // QC):
            sl = slice(ci * QC, (ci + 1) * QC)
            top_ref[h, :, sl] = jnp.max(nn(kb[...], qpad[:, sl]), axis=0, keepdims=True)

    store[11].start()
    for c in fars:
        c.wait_recv()
    store[8].start()
    kfT_ref[...] = far_ref[:, 0:D].T
    vfT_ref[...] = far_ref[:, D:2 * D].T
    store[9].start()
    store[10].start()
    for c in store:
        c.wait()
    for c in asks + sends + fars:
        c.wait_send()


def front_all(lens, src, rows, go, wq, wk, wv, wo):
    s = jax.ShapeDtypeStruct
    dma = pltpu.SemaphoreType.DMA
    return pl.pallas_call(
        front_kernel,
        in_specs=[sm()] + [vm()] * 2 + [hbm()] * 5,
        out_specs=[hbm()] * 12,
        out_shape=[s((T, D), BF)] * 4 + [s((D, T), BF)] * 4 + [s((FAR, 2 * D), BF)] + [s((D, FAR), BF)] * 2
        + [s((HEADS, 1, T), F32)],
        scratch_shapes=[pltpu.VMEM((T, D), BF)] * 4 + [pltpu.VMEM((D, T), BF)] * 4 + [
            pltpu.VMEM((FAR, 2 * D), BF), pltpu.VMEM((D, FAR), BF), pltpu.VMEM((D, FAR), BF),
            pltpu.VMEM((HEADS, 1, T), F32), pltpu.VMEM((T, D), BF), pltpu.VMEM((D, D), BF), pltpu.VMEM((D, D), BF),
            pltpu.VMEM((D, D), BF), pltpu.VMEM((D, D), BF),
            pltpu.VMEM((8, 8, 128), F32), pltpu.VMEM((7, 8, 128), F32), pltpu.VMEM((7, 128, D), BF),
            pltpu.VMEM((T, D), BF), pltpu.VMEM((T, T), BF), pltpu.VMEM((256, T), BF), pltpu.VMEM((T, 256), BF),
        dma((5,)), dma((12,)),
        ] + [dma((7,))] * 6,
        compiler_params=pltpu.CompilerParams(
            vmem_limit_bytes=60 << 20, collective_id=2, has_side_effects=True),
        cost_estimate=pl.CostEstimate(flops=12 * T * D * D, bytes_accessed=20 << 20, transcendentals=0),
    )(lens, src, rows, go, wq, wk, wv, wo)


HALF = D // 2
GH = HEADS // 4
GR = GH * HD


def copy_to(src, dst, ssem, rsem, peer):
    return pltpu.make_async_remote_copy(
        src_ref=src, dst_ref=dst, send_sem=ssem, recv_sem=rsem, device_id=peer, device_id_type=MESHID
    )


def all_peers():
    xyz, core = coords()
    s = lax.axis_index("seq")
    near = [device_at(along(xyz, 0, d), core) for d in (1, 3)] + [device_at(along(xyz, 2, d), core) for d in (1, 2, 3)]
    return [seq_peer(s, d) for d in range(1, 8)] + near + [device_at(xyz, 1 - core)]


class Reduction:
    def __init__(self, grads, crx, acc, rx1, rx2, rx3, r2, fin, cs, cr, ss, rs):
        self.xyz, self.core = coords()
        self.grads, self.crx, self.acc = grads, crx, acc
        self.rx1, self.rx2, self.rx3, self.r2, self.fin = rx1, rx2, rx3, r2, fin
        self.cs, self.cr, self.ss, self.rs = cs, cr, ss, rs

    def at(self, p, level):
        return self.xyz[ORDERS[p][level]]

    def peer(self, p, level, d):
        return device_at(along(self.xyz, ORDERS[p][level], d), self.core)

    def pair(self, i):
        return copy_to(self.grads.at[i, 1 - self.core], self.crx.at[i], self.cs.at[i], self.cr.at[i],
                       device_at(self.xyz, 1 - self.core))

    def wave(self, level, parts=(0, 1, 2)):
        made = []
        for p in parts:
            for d in (1, 2, 3):
                other = (self.at(p, level) + d) % 4
                if level == 0:
                    src, dst = self.acc.at[other, pl.ds(p * 64, 64)], self.rx1.at[p, d - 1]
                elif level == 1:
                    src, dst = self.r2.at[p, pl.ds(pl.multiple_of(other * 16, 16), 16)], self.rx2.at[p, d - 1]
                else:
                    own = self.rx3.at[p, self.at(p, 2)]
                    src, dst = own, own
                made.append(copy_to(src, dst, self.ss.at[level, p, d - 1], self.rs.at[level, p, d - 1],
                                    self.peer(p, level, d)))
        return made

    def start(self, copies):
        for c in copies:
            c.start()

    def rows(self, i, value):
        self.grads[i, 0] = value[:, :HALF]
        self.grads[i, 1] = value[:, HALF:]

    def add_pairs(self):
        for i in (0, 3, 1, 2):
            self.pair(i).wait_recv()
            self.acc[i] = self.grads[i, self.core] + self.crx[i]
        for i in range(4):
            self.pair(i).wait_send()

    def after_first(self):
        copies = self.wave(0)
        for p in range(3):
            for c in copies[3 * p:3 * p + 3]:
                c.wait_recv()
            self.r2[p] = self.acc[self.at(p, 0), p * 64:(p + 1) * 64] + self.rx1[p, 0] + self.rx1[p, 1] + self.rx1[p, 2]
            self.start(self.wave(1, (p,)))

    def after_second(self):
        copies = self.wave(1)
        for p in range(3):
            for c in copies[3 * p:3 * p + 3]:
                c.wait_recv()
            own = self.r2[p, pl.ds(pl.multiple_of(self.at(p, 1) * 16, 16), 16)]
            self.rx3[p, self.at(p, 2)] = own + self.rx2[p, 0] + self.rx2[p, 1] + self.rx2[p, 2]
            self.start(self.wave(2, (p,)))

    def after_third(self):
        copies = self.wave(2)
        for p in range(3):
            for c in copies[3 * p:3 * p + 3]:
                c.wait_recv()
            self.fin[p] = (self.rx3[p, 0] + self.rx3[p, 1] + self.rx3[p, 2] + self.rx3[p, 3]).astype(BF)

    def finish(self):
        for level in range(3):
            for c in self.wave(level):
                c.wait_send()


def reduction_scratch(*groups):
    dma = pltpu.SemaphoreType.DMA
    return [
        pltpu.VMEM((4, 2, GR, HALF), F32), pltpu.VMEM(groups + (4, GR, HALF), F32),
        pltpu.VMEM(groups + (4, GR, HALF), F32), pltpu.VMEM(groups + (3, 3, 64, HALF), F32),
        pltpu.VMEM(groups + (3, 3, 16, HALF), F32), pltpu.VMEM(groups + (3, 4, 16, HALF), F32),
        pltpu.VMEM(groups + (3, 64, HALF), F32), dma(groups + (4,)), dma(groups + (4,)),
        dma(groups + (3, 3, 3)), dma(groups + (3, 3, 3)),
    ]


class Spread:
    def __init__(self, red, fin, out, gs, gr, hs, hr):
        self.red, self.fin, self.out, self.gs, self.gr, self.hs, self.hr = red, fin, out, gs, gr, hs, hr

    def wave(self, level, parts=(0, 1, 2)):
        made = []
        for p in parts:
            a, b = self.red.at(p, 0), self.red.at(p, 1)
            rows = pl.ds(pl.multiple_of(p * 64 + b * 16, 16), 16) if level == 1 else pl.ds(p * 64, 64)
            here = self.out.at[self.red.core, a, rows]
            for d in (1, 2, 3):
                made.append(copy_to(here, here, self.gs.at[level, p, d - 1], self.gr.at[level, p, d - 1],
                                    self.red.peer(p, level, d)))
        return made

    def mate(self):
        here = self.out.at[self.red.core]
        return copy_to(here, here, self.hs, self.hr, device_at(self.red.xyz, 1 - self.red.core))

    def begin(self):
        for p in range(3):
            rows = pl.ds(pl.multiple_of(p * 64 + self.red.at(p, 1) * 16, 16), 16)
            self.out[self.red.core, self.red.at(p, 0), rows] = self.fin[p]
        for c in self.wave(1):
            c.start()

    def middle(self):
        for p in range(3):
            for c in self.wave(1, (p,)):
                c.wait_recv()
            for c in self.wave(0, (p,)):
                c.start()

    def end(self):
        for c in self.wave(0):
            c.wait_recv()
        self.mate().start()

    def finish(self):
        for level in range(2):
            for c in self.wave(level):
                c.wait_send()
        self.mate().wait()


def back_copies(part, rx, ss, rs):
    s = lax.axis_index("seq")
    return [copy_to(part.at[pl.ds(pl.multiple_of(lax.rem(s + d, 8) * 64, 64), 64)], rx.at[d - 1],
                    ss.at[d - 1], rs.at[d - 1], seq_peer(s, d)) for d in range(1, 8)]


def add_back(copies, part, rx, group, dk32, dv32, dk, dv):
    s = lax.axis_index("seq")
    back = part[pl.ds(pl.multiple_of(s * 64, 64), 64), :].astype(F32)
    for d in range(1, 8):
        copies[d - 1].wait_recv()
        back = back + rx[d - 1].astype(F32)
    for c in copies:
        c.wait_send()
    bT = back.T
    zero = jnp.zeros((HD, 64), F32)
    for i in range(GH):
        r = slice(i * HD, (i + 1) * HD)
        w = pl.ds(pl.multiple_of((group * 2 + i // 2) * 128, 128), 128)
        bk = bT[i * HD:(i + 1) * HD, :]
        bv = bT[GR + i * HD:GR + (i + 1) * HD, :]
        pk = [bk, zero] if i % 2 == 0 else [zero, bk]
        pv = [bv, zero] if i % 2 == 0 else [zero, bv]
        dk[r, :] = dk32[r, :].astype(BF)
        dv[r, :] = dv32[r, :].astype(BF)
        dk[r, w] = (dk32[r, w] + jnp.concatenate(pk, axis=1)).astype(BF)
        dv[r, w] = (dv32[r, w] + jnp.concatenate(pv, axis=1)).astype(BF)


def tail_kernel(x_ref, go_ref, attT_ref, dqT_ref, dk_ref, dv_ref, dk32_ref, dv32_ref, dkvf_ref, fin_ref, acc_ref,
                wq_hbm, wk_hbm, wv_hbm, wo_hbm, enc_ref, emb_ref, out1_ref, out2_ref, out3_ref,
                wq_ref, wk_ref, wv_ref, wo_ref, ins, part, rx, dk, dv, fin2, fin3, home, bs, br, *scratch):
    fetch = [pltpu.make_async_copy(a, b, ins.at[i]) for i, (a, b) in enumerate((
        (dk_ref, dk.at[pl.ds(0, 3 * GR)]), (dv_ref, dv.at[pl.ds(0, 3 * GR)]), (wo_hbm, wo_ref), (wq_hbm, wq_ref),
        (wk_hbm, wk_ref), (wv_hbm, wv_ref)))]
    for c in fetch:
        c.start()
    greet(all_peers())
    sems, older, newer = scratch[:12], scratch[12:18], scratch[18:]
    red2 = Reduction(None, None, acc_ref, *older[:4], fin2, None, None, *older[4:])
    red3 = Reduction(*newer[:7], fin3, *newer[7:])
    spread1 = Spread(red2, fin_ref.at[1], out1_ref, *sems[0:4])
    spread2 = Spread(red2, fin2, out2_ref, *sems[4:8])
    spread3 = Spread(red3, fin3, out3_ref, *sems[8:12])
    part[...] = dkvf_ref[...].T
    backs = back_copies(part, rx, bs, br)
    for c in backs:
        c.start()
    spread1.begin()
    red2.start(red2.wave(0))
    last = 3 * GR
    xT = x_ref[...].T
    red3.rows(0, nt(dqT_ref[last:, :], xT))
    red3.pair(0).start()
    red3.rows(3, nn(attT_ref[last:, :], go_ref[...]))
    red3.pair(3).start()
    spread1.middle()
    spot = lax.broadcasted_iota(jnp.int32, (T, T), 0)
    home[...] = (lax.broadcasted_iota(jnp.int32, (T, T), 1) == lax.rem(spot, RATE) * 64 + spot // RATE).astype(BF)
    red2.after_first()
    add_back(backs, part, rx, 3, dk32_ref, dv32_ref, dk.at[last:D], dv.at[last:D])
    red3.rows(1, nt(dk[last:D, :], xT))
    red3.pair(1).start()
    red3.rows(2, nt(dv[last:D, :], xT))
    red3.pair(2).start()
    spread1.end()
    red2.after_second()
    red3.add_pairs()
    red3.start(red3.wave(0))
    for c in fetch:
        c.wait()
    enc = (x_ref[...].astype(F32) + nn(attT_ref[...].T, wo_ref[...])).astype(BF)
    red2.after_third()
    spread2.begin()
    enc_ref[...] = nn(home[...], enc).astype(BF)
    red3.after_first()
    spread2.middle()
    e = nn(wq_ref[...], dqT_ref[...]) + nn(wk_ref[...], dk[...])
    red3.after_second()
    spread2.end()
    e = e + nn(wv_ref[...], dv[...])
    red3.after_third()
    spread3.begin()
    emb = (go_ref[...].astype(F32) + e.T).astype(BF)
    spread3.middle()
    emb_ref[...] = nn(home[...], emb).astype(BF)
    spread3.end()
    red2.finish()
    red3.finish()
    for spread in (spread1, spread2, spread3):
        spread.finish()


def tail_all(*args):
    s = jax.ShapeDtypeStruct
    dma = pltpu.SemaphoreType.DMA
    older = reduction_scratch()
    return pl.pallas_call(
        tail_kernel,
        in_specs=[vm()] * 4 + [hbm()] * 2 + [vm()] * 5 + [hbm()] * 4,
        out_specs=[vm()] * 5,
        out_shape=[s((T, D), BF)] * 2 + [s((2, 4, GR, HALF), BF)] * 3,
        scratch_shapes=[
            pltpu.VMEM((D, D), BF), pltpu.VMEM((D, D), BF), pltpu.VMEM((D, D), BF), pltpu.VMEM((D, D), BF), dma((6,)),
            pltpu.VMEM((FAR, 2 * GR), BF), pltpu.VMEM((7, 64, 2 * GR), BF),
            pltpu.VMEM((D, T), BF), pltpu.VMEM((D, T), BF), pltpu.VMEM((3, 16, HALF), BF),
            pltpu.VMEM((3, 16, HALF), BF), pltpu.VMEM((T, T), BF), dma((7,)), dma((7,)),
        ] + [dma((2, 3, 3)), dma((2, 3, 3)), dma(()), dma(())] * 3 + older[3:7] + older[9:] + reduction_scratch(),
        compiler_params=pltpu.CompilerParams(
            vmem_limit_bytes=60 << 20, collective_id=3, has_side_effects=True),
        cost_estimate=pl.CostEstimate(flops=16 * T * D * D, bytes_accessed=30 << 20, transcendentals=0),
    )(*args)


def lay_kernel(enc_ref, emb_ref, out0_ref, out1_ref, out2_ref, out3_ref,
               enc_out, emb_out, gq_ref, gk_ref, gv_ref, gout_ref, blocks, plain, stage, passing, ins, outs):
    copies = [pltpu.make_async_copy(enc_ref, enc_out, passing.at[0]),
              pltpu.make_async_copy(emb_ref, emb_out, passing.at[1])]
    loads = [pltpu.make_async_copy(o.at[:, i], blocks.at[i, :, g], ins.at[i, g])
             for i in range(4) for g, o in enumerate((out0_ref, out1_ref, out2_ref, out3_ref))]
    for c in loads + copies:
        c.start()
    for i, to in enumerate((gq_ref, gk_ref, gv_ref, gout_ref)):
        for g in range(4):
            loads[4 * i + g].wait()
            rows = slice(g * GR, (g + 1) * GR)
            target = plain if i < 3 else stage.at[i]
            target[rows, 0:HALF] = blocks[i, 0, g].astype(F32)
            target[rows, HALF:D] = blocks[i, 1, g].astype(F32)
        if i < 3:
            stage[i] = plain[...].T
        copies.append(pltpu.make_async_copy(stage.at[i], to, outs.at[i]))
        copies[-1].start()
    for c in copies:
        c.wait()


def lay_all(*args):
    s = jax.ShapeDtypeStruct
    dma = pltpu.SemaphoreType.DMA
    return pl.pallas_call(
        lay_kernel,
        in_specs=[hbm()] * 6,
        out_specs=[hbm()] * 6,
        out_shape=[s((T, D), BF)] * 2 + [s((D, D), F32)] * 4,
        scratch_shapes=[
            pltpu.VMEM((4, 2, 4, GR, HALF), BF), pltpu.VMEM((D, D), F32), pltpu.VMEM((4, D, D), F32),
            dma((2,)), dma((4, 4)), dma((4,)),
        ],
        compiler_params=pltpu.CompilerParams(vmem_limit_bytes=40 << 20),
        cost_estimate=pl.CostEstimate(flops=4 * D * D, bytes_accessed=24 * D * D, transcendentals=0),
    )(*args)


def per_device(tile_embed, tile_source, slide_len, grad_out, w_query, w_key, w_value, w_out):
    source = tile_source.reshape(1, T)
    length = slide_len[0]
    lens = jnp.stack([length - lax.axis_index("seq") * T, length]).astype(jnp.int32)
    x, go, k, v, qT, kT, vT, gT, far, kfT, vfT, top = front_all(
        lens, source, tile_embed[0], grad_out[0], w_query, w_key, w_value, w_out
    )
    attT, dqT, dk, dv, dk32, dv32, dkvf, fin, acc, out0 = attn(
        lens, k, v, qT, kT, vT, gT, far, kfT, vfT, top, x, go
    )
    enc, emb, out1, out2, out3 = tail_all(
        x, go, attT, dqT, dk, dv, dk32, dv32, dkvf, fin, acc, w_query, w_key, w_value, w_out
    )
    enc, emb, *summed = lay_all(enc, emb, out0, out1, out2, out3)
    return (enc[None], emb[None], summed[0], summed[1], summed[2], summed[3])


def solution(mesh):
    return jax.shard_map(
        per_device,
        mesh=mesh,
        in_specs=(
            P("rep", "seq", None),
            P("rep", "seq"),
            P("rep"),
            P("rep", "seq", None),
            P(),
            P(),
            P(),
            P(),
        ),
        out_specs=(P("rep", "seq", None), P("rep", "seq", None), P(), P(), P(), P()),
        check_vma=False,
    )
```

```python
import functools

import jax
import jax.numpy as jnp
from jax import lax
from jax.experimental import pallas as pl
from jax.experimental.pallas import tpu as pltpu
from jax.sharding import PartitionSpec as P

HEADS=16; RATE=16; HD=48; D=768; T=1024; FAR=512
BF=jnp.bfloat16; F32=jnp.float32
LOG2E=1.4426950408889634
NEG=-1e30
QC=512

def nn(a,b): return lax.dot_general(a,b,(((1,),(0,)),((),())),preferred_element_type=F32)
def nt(a,b): return lax.dot_general(a,b,(((1,),(1,)),((),())),preferred_element_type=F32)

def attn_kernel(len_ref, k_ref, v_ref, qT_ref, kT_ref, vT_ref, gT_ref, far_ref, kfT_ref, vfT_ref, top_ref, x_hbm, go_hbm,
                attT_ref, dqT_ref, dk_ref, dv_ref, dk32_ref, dv32_ref, dkvf_ref, fin_ref, acc_ref, out_ref,
                x_ref, go_ref, ins, qpad, gpad, kb, kfb, m2s, l2s, u2s, w2s, des, dqs, e2s,
                dk32, dv32, dkvf, xT, part, rx, sums, bs, br, gs, gr, hs, hr, *scratch):
    h = pl.program_id(0)
    step = lax.rem(h, 4)

    def reduction(g):
        return Reduction(scratch[0], *[ref.at[g] for ref in scratch[1:7]], fin_ref.at[g],
                         *[sem.at[g] for sem in scratch[7:]])

    def spread(g):
        return Spread(reduction(g), fin_ref.at[g], sums, gs, gr, hs, hr)

    def backs(g):
        return back_copies(part, rx.at[g], bs.at[g], br.at[g])

    now = jnp.maximum(h // 4 - 1, 0)
    before = jnp.maximum(h // 4 - 2, 0)
    low = pl.ds(pl.multiple_of(now * GR, 64), GR)

    fetch = [pltpu.make_async_copy(x_hbm, x_ref, ins.at[0]), pltpu.make_async_copy(go_hbm, go_ref, ins.at[1])]

    @pl.when(h == 0)
    def _():
        for c in fetch:
            c.start()
        greet(all_peers())

    @pl.when(h == 4)
    def _():
        for c in fetch:
            c.wait()
        xT[...] = x_ref[...].T

    @pl.when((step == 0) & (h >= 4))
    def _():
        part[...] = dkvf[lax.rem(now, 2)].T
        for c in backs(now):
            c.start()
        red = reduction(now)
        red.rows(0, nt(dqT_ref[low, :], xT[...]))
        red.pair(0).start()
        red.rows(3, nn(attT_ref[low, :], go_ref[...]))
        red.pair(3).start()

    @pl.when((step == 2) & (h >= 4))
    def _():
        slot = lax.rem(now, 2)
        add_back(backs(now), part, rx.at[now], now, dk32.at[slot], dv32.at[slot], dk_ref.at[low], dv_ref.at[low])
        red = reduction(now)
        red.rows(1, nt(dk_ref[low, :], xT[...]))
        red.pair(1).start()
        red.rows(2, nt(dv_ref[low, :], xT[...]))
        red.pair(2).start()

    @pl.when((step == 1) & (h >= 8))
    def _():
        reduction(before).after_first()

    @pl.when((step == 2) & (h >= 8))
    def _():
        reduction(before).after_second()

    @pl.when((step == 3) & (h >= 8))
    def _():
        reduction(before).after_third()

    @pl.when((step == 3) & (h >= 4))
    def _():
        reduction(now).add_pairs()

    @pl.when((step == 3) & (h >= 4) & (h < 12))
    def _():
        red = reduction(now)
        red.start(red.wave(0))

    @pl.when(h == 11)
    def _():
        spread(0).begin()

    @pl.when(h == 13)
    def _():
        spread(0).middle()

    @pl.when(h == 14)
    def _():
        spread(0).end()

    n = len_ref[0]
    nfull = len_ref[1]
    scale = HD ** -0.5
    c = scale * LOG2E
    w0, off, free = window(h)
    r = pl.multiple_of(h * HD, 16)
    row = lax.broadcasted_iota(jnp.int32, (256, T), 0)
    qpad[...] = pad_rows(qT_ref, w0, off, row, jnp.where(row == free, 1.0, 0.0).astype(BF))
    gpad[...] = pad_rows(gT_ref, w0, off, row, jnp.zeros((256, T), BF))
    lane = lax.broadcasted_iota(jnp.int32, (T, 256), 1)
    kb[...] = jnp.where(lane == free, key_bias(n), k_ref[:, pl.ds(w0, 256)])
    fi = lax.broadcasted_iota(jnp.int32, (FAR, 1), 0)
    fbias = jnp.where(fi * RATE + h < nfull, 0.0, NEG).astype(BF)
    flane = lax.broadcasted_iota(jnp.int32, (FAR, 256), 1)
    kfb[...] = jnp.where(flane == free, fbias, far_ref[:, pl.ds(w0, 256)])
    wq = pl.multiple_of((h // 2) * 128, 128)
    qlane = lax.broadcasted_iota(jnp.int32, (1, 128), 1)
    mine = (qlane // 64) == lax.rem(h, 2)
    S2 = nn(kfb[...], qpad[:, pl.ds(wq, 128)])
    x2 = jnp.max(S2, axis=0, keepdims=True)
    e2 = jnp.exp2(S2 * c - x2 * c)
    e2s[...] = e2
    l2 = jnp.sum(e2, axis=0, keepdims=True)
    u2 = nn(vfT_ref[pl.ds(r, HD), :], e2.astype(BF))
    m2s[...] = jnp.full_like(m2s, NEG)
    l2s[...] = jnp.zeros_like(l2s)
    u2s[...] = jnp.zeros_like(u2s)
    m2s[:, pl.ds(wq, 128)] = jnp.where(mine, x2 * scale, NEG)
    l2s[:, pl.ds(wq, 128)] = jnp.where(mine, l2, 0.0)
    u2s[:, pl.ds(wq, 128)] = jnp.where(mine, u2, 0.0)
    vwin = v_ref[:, pl.ds(w0, 256)]
    vTh = vT_ref[pl.ds(r, HD), :]
    kTh = kT_ref[pl.ds(r, HD), :]
    dv = jnp.zeros((HD, T), F32)
    dk = jnp.zeros((HD, T), F32)
    for ci in range(T // QC):
        sl = slice(ci * QC, (ci + 1) * QC)
        S = nn(kb[...], qpad[:, sl])
        x1 = top_ref[h, :, sl]
        e = jnp.exp2(S * c - x1 * c)
        l1 = jnp.sum(e, axis=0, keepdims=True)
        u1 = nn(vTh, e.astype(BF))
        m1 = x1 * scale
        m2 = m2s[:, sl]; l2c = l2s[:, sl]
        M = jnp.maximum(m1, m2)
        a1 = jnp.exp(m1 - M); a2 = jnp.exp(m2 - M)
        inv = 1.0 / (a1 * l1 + a2 * l2c)
        w1 = a1 * inv; w2 = a2 * inv
        o = u1 * w1 + u2s[:, sl] * w2
        qi = lax.broadcasted_iota(jnp.int32, (1, QC), 1) + ci * QC
        ok = (lax.rem(qi, 64) * RATE + qi // 64) < n
        attT_ref[pl.ds(r, HD), sl] = jnp.where(ok, o, 0.0).astype(BF)
        gTh = gT_ref[pl.ds(r, HD), sl]
        delta = jnp.sum(gTh.astype(F32) * o, axis=0, keepdims=True)
        w2s[:, sl] = w2
        des[:, sl] = delta
        dP = nn(vwin, gpad[:, sl])
        P = e * w1
        dS = (P * (dP - delta)).astype(BF)
        dqs[:, sl] = nn(kTh, dS)
        dv += nt(gTh, P.astype(BF))
        dk += nt(qT_ref[pl.ds(r, HD), sl], dS)
    r1 = pl.multiple_of(step * HD, 16)
    slot = lax.rem(h // 4, 2)
    dv32[slot, pl.ds(r1, HD), :] = dv
    dk32[slot, pl.ds(r1, HD), :] = dk * scale
    P2 = e2s[...] * jnp.where(mine, w2s[:, pl.ds(wq, 128)], 0.0)
    dP2 = nn(far_ref[:, pl.ds(pl.multiple_of(w0 + D, 128), 256)], gpad[:, pl.ds(wq, 128)])
    dS2 = (P2 * (dP2 - des[:, pl.ds(wq, 128)])).astype(BF)
    dvf = nt(gT_ref[pl.ds(r, HD), pl.ds(wq, 128)], P2.astype(BF)).astype(BF)
    dkf = (nt(qT_ref[pl.ds(r, HD), pl.ds(wq, 128)], dS2) * scale).astype(BF)

    dkvf[slot, pl.ds(r1, HD), :] = dkf
    dkvf[slot, pl.ds(pl.multiple_of(r1 + GR, 16), HD), :] = dvf
    dqs[:, pl.ds(wq, 128)] += nn(kfT_ref[pl.ds(r, HD), :], dS2)
    dqT_ref[pl.ds(r, HD), :] = (dqs[...] * scale).astype(BF)

    @pl.when(h == HEADS - 1)
    def _():
        dk32_ref[...] = dk32[1]
        dv32_ref[...] = dv32[1]
        dkvf_ref[...] = dkvf[1]
        acc_ref[...] = scratch[2][2]
        for g in range(2):
            reduction(g).finish()
        spread(0).finish()
        out_ref[...] = sums[...]


def attn(lens, *arrs):
    s = jax.ShapeDtypeStruct
    dma = pltpu.SemaphoreType.DMA
    return pl.pallas_call(
        attn_kernel,
        grid=(HEADS,),
        in_specs=[sm()] + [vm()] * 10 + [hbm()] * 2,
        out_specs=[vm()] * 10,
        out_shape=[s((D, T), BF)] * 2 + [s((3 * GR, T), BF)] * 2 + [s((GR, T), F32)] * 2 + [s((2 * GR, FAR), BF)]
        + [s((2, 3, 16, HALF), BF), s((4, GR, HALF), F32), s((2, 4, GR, HALF), BF)],
        scratch_shapes=[
            pltpu.VMEM((T, D), BF), pltpu.VMEM((T, D), BF), dma((2,)),
            pltpu.VMEM((256, T), BF), pltpu.VMEM((256, T), BF), pltpu.VMEM((T, 256), BF), pltpu.VMEM((FAR, 256), BF),
            pltpu.VMEM((1, T), F32), pltpu.VMEM((1, T), F32), pltpu.VMEM((HD, T), F32), pltpu.VMEM((1, T), F32),
            pltpu.VMEM((1, T), F32), pltpu.VMEM((HD, T), F32), pltpu.VMEM((FAR, 128), F32),
            pltpu.VMEM((2, GR, T), F32), pltpu.VMEM((2, GR, T), F32), pltpu.VMEM((2, 2 * GR, FAR), BF),
            pltpu.VMEM((D, T), BF), pltpu.VMEM((FAR, 2 * GR), BF), pltpu.VMEM((3, 7, 64, 2 * GR), BF),
            pltpu.VMEM((2, 4, GR, HALF), BF), dma((3, 7)), dma((3, 7)), dma((2, 3, 3)), dma((2, 3, 3)), dma(()), dma(()),
        ] + reduction_scratch(3),
        compiler_params=pltpu.CompilerParams(
            vmem_limit_bytes=60 << 20, collective_id=4, has_side_effects=True),
        cost_estimate=pl.CostEstimate(flops=100 * T * D * D, bytes_accessed=30 << 20, transcendentals=0),
    )(lens, *arrs)


def vm():
    return pl.BlockSpec(memory_space=pltpu.VMEM)


def hbm():
    return pl.BlockSpec(memory_space=pl.ANY)


def sm():
    return pl.BlockSpec(memory_space=pltpu.SMEM)


MESHID = pl.DeviceIdType.MESH
ORDERS = ((0, 1, 2), (1, 2, 0), (2, 0, 1))


def coords():
    s = lax.axis_index("seq")
    r = lax.axis_index("rep")
    return ((s % 2) * 2 + r // 8, s // 2, (r // 2) % 4), r % 2


def device_at(xyz, core):
    x, y, z = xyz
    return (y * 2 + x // 2, ((x % 2) * 4 + z) * 2 + core)


def along(xyz, axis, step):
    moved = list(xyz)
    moved[axis] = (xyz[axis] + step) % 4
    return tuple(moved)


def greet(peers):
    barrier = pltpu.get_barrier_semaphore()
    for peer in peers:
        pl.semaphore_signal(barrier, inc=1, device_id=peer, device_id_type=MESHID)
    pl.semaphore_wait(barrier, len(peers))


def send(src, dst, ssem, rsem, peer):
    copy = pltpu.make_async_remote_copy(
        src_ref=src, dst_ref=dst, send_sem=ssem, recv_sem=rsem, device_id=peer, device_id_type=MESHID
    )
    copy.start()
    return copy


def seq_peer(s, d):
    return (lax.rem(s + d, 8), lax.axis_index("rep"))


def window(h):
    hh = lax.rem(h, 8)
    w0 = pl.multiple_of((h // 8) * 384 + jnp.where(hh >= 5, 128, 0), 128)
    off = h * HD - w0
    return w0, off, jnp.where(off >= 48, 0, 255)


def pad_rows(ref, w0, off, rows_in, filler):
    return jnp.where((rows_in >= off) & (rows_in < off + HD), ref[pl.ds(w0, 256), :], filler)


def key_bias(n):
    ki = lax.broadcasted_iota(jnp.int32, (T, 1), 0)
    return jnp.where(lax.rem(ki, 64) * RATE + ki // 64 < n, 0.0, NEG).astype(BF)


def front_kernel(len_ref, src_ref, rows_ref, grad_hbm, wq_hbm, wk_hbm, wv_hbm, wo_hbm,
                 x_out, go_out, k_out, v_out, qT_out, kT_out, vT_out, gT_out, far_out, kfT_out, vfT_out, top_out,
                 x_ref, go_ref, k_ref, v_ref, qT_ref, kT_ref, vT_ref, gT_ref, far_ref, kfT_ref, vfT_ref, top_ref,
                 grad_ref, wq_ref, wk_ref, wv_ref, wo_ref,
                 ask, req, picked, arrived, perm, qpad, kb, ins, outs, qs, qr, ps, pr, fs, fr):
    n = len_ref[0]
    fetch = [pltpu.make_async_copy(a, b, ins.at[i]) for i, (a, b) in enumerate((
        (grad_hbm, grad_ref), (wo_hbm, wo_ref), (wk_hbm, wk_ref), (wv_hbm, wv_ref), (wq_hbm, wq_ref)))]
    for c in fetch:
        c.start()
    store = [pltpu.make_async_copy(a, b, outs.at[i]) for i, (a, b) in enumerate((
        (x_ref, x_out), (go_ref, go_out), (k_ref, k_out), (v_ref, v_out), (qT_ref, qT_out), (kT_ref, kT_out),
        (vT_ref, vT_out), (gT_ref, gT_out), (far_ref, far_out), (kfT_ref, kfT_out), (vfT_ref, vfT_out),
        (top_ref, top_out)))]
    s = lax.axis_index("seq")
    peers = [seq_peer(s, d) for d in range(1, 8)]
    greet(peers)
    src = src_ref[...]
    sixteen = lax.broadcasted_iota(jnp.int32, (16, T), 0)
    line = lax.rem(src, T)
    parts = jnp.where(sixteen == 0, line // 32, jnp.where(sixteen == 1, lax.rem(line, 32), src // T))
    spot = lax.broadcasted_iota(jnp.int32, (T, T), 0)
    reorder = (lax.broadcasted_iota(jnp.int32, (T, T), 1) == lax.rem(spot, 64) * RATE + spot // 64).astype(BF)
    parts = nt(parts.astype(F32).astype(BF), reorder)
    owner = parts[2:3].astype(jnp.int32)
    hot = (lax.broadcasted_iota(jnp.int32, (16, T), 0) == owner).astype(BF)
    before = (lax.broadcasted_iota(jnp.int32, (T, T), 0) < lax.broadcasted_iota(jnp.int32, (T, T), 1)).astype(BF)
    rank = jnp.sum(nn(hot, before) * hot.astype(F32), axis=0, keepdims=True)
    slot = owner.astype(F32) * 128.0 + rank
    where = lax.broadcasted_iota(jnp.int32, (T, T), 0).astype(F32)
    permT = (where == slot).astype(BF)
    got = nt(parts.astype(BF), permT)
    lines = got[0:1] * 32.0 + got[1:2]
    for o in range(8):
        ask[o] = jnp.broadcast_to(lines[:, o * 128:(o + 1) * 128], (8, 128))
    asks = [send(ask.at[lax.rem(s + d, 8)], req.at[d - 1], qs.at[d - 1], qr.at[d - 1], peers[d - 1])
            for d in range(1, 8)]
    perm[...] = permT.T
    qi = lax.broadcasted_iota(jnp.int32, (1, T), 1)
    ok = (lax.rem(qi, 64) * RATE + qi // 64) < n
    fetch[0].wait()
    fetch[1].wait()
    go_ref[...] = nn(reorder, grad_ref[...]).astype(BF)
    store[1].start()
    gT_ref[...] = jnp.where(ok, nt(wo_ref[...], go_ref[...]), 0.0).astype(BF)
    store[7].start()
    cells = lax.broadcasted_iota(jnp.int32, (128, T), 1).astype(F32)
    rows = rows_ref[...]
    mine = pl.ds(pl.multiple_of(s * 128, 128), 128)
    sends = []
    for d in range(1, 8):
        asks[d - 1].wait_recv()
        pick = (cells == req[d - 1].T[:, 0:1]).astype(BF)
        picked[d - 1] = nn(pick, rows).astype(BF)
        sends.append(send(picked.at[d - 1], arrived.at[mine], ps.at[d - 1], pr.at[d - 1], seq_peer(s, 8 - d)))
    pick = (cells == ask[s].T[:, 0:1]).astype(BF)
    arrived[mine, :] = nn(pick, rows).astype(BF)
    for c in sends:
        c.wait_recv()
    x = nn(perm[...], arrived[...]).astype(BF)
    x_ref[...] = x
    store[0].start()
    fetch[2].wait()
    fetch[3].wait()
    k = nn(x, wk_ref[...]).astype(BF)
    v = nn(x, wv_ref[...]).astype(BF)
    k_ref[...] = k
    v_ref[...] = v
    store[2].start()
    store[3].start()
    col = lax.broadcasted_iota(jnp.int32, (64, D), 1) // HD
    fk = jnp.zeros((64, D), BF)
    fv = jnp.zeros((64, D), BF)
    for h in range(HEADS):
        fk = jnp.where(col == h, k_ref[h * 64:(h + 1) * 64, :], fk)
        fv = jnp.where(col == h, v_ref[h * 64:(h + 1) * 64, :], fv)
    here = pl.ds(pl.multiple_of(s * 64, 64), 64)
    far_ref[here, 0:D] = fk
    far_ref[here, D:2 * D] = fv
    fars = [send(far_ref.at[here], far_ref.at[here], fs.at[d - 1], fr.at[d - 1], peers[d - 1]) for d in range(1, 8)]
    fetch[4].wait()
    qT_ref[...] = nn(x, wq_ref[...]).astype(BF).T
    store[4].start()
    kT_ref[...] = k.T
    store[5].start()
    vT_ref[...] = v.T
    store[6].start()
    rows_in = lax.broadcasted_iota(jnp.int32, (256, T), 0)
    cols_in = lax.broadcasted_iota(jnp.int32, (T, 256), 1)
    kbias = key_bias(n)

    @pl.loop(0, HEADS)
    def _(h):
        w0, off, free = window(h)
        qpad[...] = pad_rows(qT_ref, w0, off, rows_in, jnp.where(rows_in == free, 1.0, 0.0).astype(BF))
        kb[...] = jnp.where(cols_in == free, kbias, k_ref[:, pl.ds(w0, 256)])
        for ci in range(T // QC):
            sl = slice(ci * QC, (ci + 1) * QC)
            top_ref[h, :, sl] = jnp.max(nn(kb[...], qpad[:, sl]), axis=0, keepdims=True)

    store[11].start()
    for c in fars:
        c.wait_recv()
    store[8].start()
    kfT_ref[...] = far_ref[:, 0:D].T
    vfT_ref[...] = far_ref[:, D:2 * D].T
    store[9].start()
    store[10].start()
    for c in store:
        c.wait()
    for c in asks + sends + fars:
        c.wait_send()


def front_all(lens, src, rows, go, wq, wk, wv, wo):
    s = jax.ShapeDtypeStruct
    dma = pltpu.SemaphoreType.DMA
    return pl.pallas_call(
        front_kernel,
        in_specs=[sm()] + [vm()] * 2 + [hbm()] * 5,
        out_specs=[hbm()] * 12,
        out_shape=[s((T, D), BF)] * 4 + [s((D, T), BF)] * 4 + [s((FAR, 2 * D), BF)] + [s((D, FAR), BF)] * 2
        + [s((HEADS, 1, T), F32)],
        scratch_shapes=[pltpu.VMEM((T, D), BF)] * 4 + [pltpu.VMEM((D, T), BF)] * 4 + [
            pltpu.VMEM((FAR, 2 * D), BF), pltpu.VMEM((D, FAR), BF), pltpu.VMEM((D, FAR), BF),
            pltpu.VMEM((HEADS, 1, T), F32), pltpu.VMEM((T, D), BF), pltpu.VMEM((D, D), BF), pltpu.VMEM((D, D), BF),
            pltpu.VMEM((D, D), BF), pltpu.VMEM((D, D), BF),
            pltpu.VMEM((8, 8, 128), F32), pltpu.VMEM((7, 8, 128), F32), pltpu.VMEM((7, 128, D), BF),
            pltpu.VMEM((T, D), BF), pltpu.VMEM((T, T), BF), pltpu.VMEM((256, T), BF), pltpu.VMEM((T, 256), BF),
        dma((5,)), dma((12,)),
        ] + [dma((7,))] * 6,
        compiler_params=pltpu.CompilerParams(
            vmem_limit_bytes=60 << 20, collective_id=2, has_side_effects=True),
        cost_estimate=pl.CostEstimate(flops=12 * T * D * D, bytes_accessed=20 << 20, transcendentals=0),
    )(lens, src, rows, go, wq, wk, wv, wo)


HALF = D // 2
GH = HEADS // 4
GR = GH * HD


def copy_to(src, dst, ssem, rsem, peer):
    return pltpu.make_async_remote_copy(
        src_ref=src, dst_ref=dst, send_sem=ssem, recv_sem=rsem, device_id=peer, device_id_type=MESHID
    )


def all_peers():
    xyz, core = coords()
    s = lax.axis_index("seq")
    near = [device_at(along(xyz, 0, d), core) for d in (1, 3)] + [device_at(along(xyz, 2, d), core) for d in (1, 2, 3)]
    return [seq_peer(s, d) for d in range(1, 8)] + near + [device_at(xyz, 1 - core)]


class Reduction:
    def __init__(self, grads, crx, acc, rx1, rx2, rx3, r2, fin, cs, cr, ss, rs):
        self.xyz, self.core = coords()
        self.grads, self.crx, self.acc = grads, crx, acc
        self.rx1, self.rx2, self.rx3, self.r2, self.fin = rx1, rx2, rx3, r2, fin
        self.cs, self.cr, self.ss, self.rs = cs, cr, ss, rs

    def at(self, p, level):
        return self.xyz[ORDERS[p][level]]

    def peer(self, p, level, d):
        return device_at(along(self.xyz, ORDERS[p][level], d), self.core)

    def pair(self, i):
        return copy_to(self.grads.at[i, 1 - self.core], self.crx.at[i], self.cs.at[i], self.cr.at[i],
                       device_at(self.xyz, 1 - self.core))

    def wave(self, level, parts=(0, 1, 2)):
        made = []
        for p in parts:
            for d in (1, 2, 3):
                other = (self.at(p, level) + d) % 4
                if level == 0:
                    src, dst = self.acc.at[other, pl.ds(p * 64, 64)], self.rx1.at[p, d - 1]
                elif level == 1:
                    src, dst = self.r2.at[p, pl.ds(pl.multiple_of(other * 16, 16), 16)], self.rx2.at[p, d - 1]
                else:
                    own = self.rx3.at[p, self.at(p, 2)]
                    src, dst = own, own
                made.append(copy_to(src, dst, self.ss.at[level, p, d - 1], self.rs.at[level, p, d - 1],
                                    self.peer(p, level, d)))
        return made

    def start(self, copies):
        for c in copies:
            c.start()

    def rows(self, i, value):
        self.grads[i, 0] = value[:, :HALF]
        self.grads[i, 1] = value[:, HALF:]

    def add_pairs(self):
        for i in (0, 3, 1, 2):
            self.pair(i).wait_recv()
            self.acc[i] = self.grads[i, self.core] + self.crx[i]
        for i in range(4):
            self.pair(i).wait_send()

    def after_first(self):
        copies = self.wave(0)
        for p in range(3):
            for c in copies[3 * p:3 * p + 3]:
                c.wait_recv()
            self.r2[p] = self.acc[self.at(p, 0), p * 64:(p + 1) * 64] + self.rx1[p, 0] + self.rx1[p, 1] + self.rx1[p, 2]
            self.start(self.wave(1, (p,)))

    def after_second(self):
        copies = self.wave(1)
        for p in range(3):
            for c in copies[3 * p:3 * p + 3]:
                c.wait_recv()
            own = self.r2[p, pl.ds(pl.multiple_of(self.at(p, 1) * 16, 16), 16)]
            self.rx3[p, self.at(p, 2)] = own + self.rx2[p, 0] + self.rx2[p, 1] + self.rx2[p, 2]
            self.start(self.wave(2, (p,)))

    def after_third(self):
        copies = self.wave(2)
        for p in range(3):
            for c in copies[3 * p:3 * p + 3]:
                c.wait_recv()
            self.fin[p] = (self.rx3[p, 0] + self.rx3[p, 1] + self.rx3[p, 2] + self.rx3[p, 3]).astype(BF)

    def finish(self):
        for level in range(3):
            for c in self.wave(level):
                c.wait_send()


def reduction_scratch(*groups):
    dma = pltpu.SemaphoreType.DMA
    return [
        pltpu.VMEM((4, 2, GR, HALF), F32), pltpu.VMEM(groups + (4, GR, HALF), F32),
        pltpu.VMEM(groups + (4, GR, HALF), F32), pltpu.VMEM(groups + (3, 3, 64, HALF), F32),
        pltpu.VMEM(groups + (3, 3, 16, HALF), F32), pltpu.VMEM(groups + (3, 4, 16, HALF), F32),
        pltpu.VMEM(groups + (3, 64, HALF), F32), dma(groups + (4,)), dma(groups + (4,)),
        dma(groups + (3, 3, 3)), dma(groups + (3, 3, 3)),
    ]


class Spread:
    def __init__(self, red, fin, out, gs, gr, hs, hr):
        self.red, self.fin, self.out, self.gs, self.gr, self.hs, self.hr = red, fin, out, gs, gr, hs, hr

    def wave(self, level, parts=(0, 1, 2)):
        made = []
        for p in parts:
            a, b = self.red.at(p, 0), self.red.at(p, 1)
            rows = pl.ds(pl.multiple_of(p * 64 + b * 16, 16), 16) if level == 1 else pl.ds(p * 64, 64)
            here = self.out.at[self.red.core, a, rows]
            for d in (1, 2, 3):
                made.append(copy_to(here, here, self.gs.at[level, p, d - 1], self.gr.at[level, p, d - 1],
                                    self.red.peer(p, level, d)))
        return made

    def mate(self):
        here = self.out.at[self.red.core]
        return copy_to(here, here, self.hs, self.hr, device_at(self.red.xyz, 1 - self.red.core))

    def begin(self):
        for p in range(3):
            rows = pl.ds(pl.multiple_of(p * 64 + self.red.at(p, 1) * 16, 16), 16)
            self.out[self.red.core, self.red.at(p, 0), rows] = self.fin[p]
        for c in self.wave(1):
            c.start()

    def middle(self):
        for p in range(3):
            for c in self.wave(1, (p,)):
                c.wait_recv()
            for c in self.wave(0, (p,)):
                c.start()

    def end(self):
        for c in self.wave(0):
            c.wait_recv()
        self.mate().start()

    def finish(self):
        for level in range(2):
            for c in self.wave(level):
                c.wait_send()
        self.mate().wait()


def back_copies(part, rx, ss, rs):
    s = lax.axis_index("seq")
    return [copy_to(part.at[pl.ds(pl.multiple_of(lax.rem(s + d, 8) * 64, 64), 64)], rx.at[d - 1],
                    ss.at[d - 1], rs.at[d - 1], seq_peer(s, d)) for d in range(1, 8)]


def add_back(copies, part, rx, group, dk32, dv32, dk, dv):
    s = lax.axis_index("seq")
    back = part[pl.ds(pl.multiple_of(s * 64, 64), 64), :].astype(F32)
    for d in range(1, 8):
        copies[d - 1].wait_recv()
        back = back + rx[d - 1].astype(F32)
    for c in copies:
        c.wait_send()
    bT = back.T
    zero = jnp.zeros((HD, 64), F32)
    for i in range(GH):
        r = slice(i * HD, (i + 1) * HD)
        w = pl.ds(pl.multiple_of((group * 2 + i // 2) * 128, 128), 128)
        bk = bT[i * HD:(i + 1) * HD, :]
        bv = bT[GR + i * HD:GR + (i + 1) * HD, :]
        pk = [bk, zero] if i % 2 == 0 else [zero, bk]
        pv = [bv, zero] if i % 2 == 0 else [zero, bv]
        dk[r, :] = dk32[r, :].astype(BF)
        dv[r, :] = dv32[r, :].astype(BF)
        dk[r, w] = (dk32[r, w] + jnp.concatenate(pk, axis=1)).astype(BF)
        dv[r, w] = (dv32[r, w] + jnp.concatenate(pv, axis=1)).astype(BF)


def tail_kernel(x_ref, go_ref, attT_ref, dqT_ref, dk_ref, dv_ref, dk32_ref, dv32_ref, dkvf_ref, fin_ref, acc_ref,
                wq_hbm, wk_hbm, wv_hbm, wo_hbm, enc_ref, emb_ref, out1_ref, out2_ref, out3_ref,
                wq_ref, wk_ref, wv_ref, wo_ref, ins, part, rx, dk, dv, fin2, fin3, home, mid, bs, br, *scratch):
    fetch = [pltpu.make_async_copy(a, b, ins.at[i]) for i, (a, b) in enumerate((
        (dk_ref, dk.at[pl.ds(0, 3 * GR)]), (dv_ref, dv.at[pl.ds(0, 3 * GR)]), (wo_hbm, wo_ref), (wq_hbm, wq_ref),
        (wk_hbm, wk_ref), (wv_hbm, wv_ref)))]
    for c in fetch:
        c.start()
    greet(all_peers())
    sems, older, newer = scratch[:12], scratch[12:18], scratch[18:]
    red2 = Reduction(None, None, acc_ref, *older[:4], fin2, None, None, *older[4:])
    red3 = Reduction(*newer[:7], fin3, *newer[7:])
    spread1 = Spread(red2, fin_ref.at[1], out1_ref, *sems[0:4])
    spread2 = Spread(red2, fin2, out2_ref, *sems[4:8])
    spread3 = Spread(red3, fin3, out3_ref, *sems[8:12])

    def send_home(to):
        @pl.loop(0, 4)
        def _(i):
            rows = pl.ds(pl.multiple_of(i * 256, 256), 256)
            to[rows, :] = nn(home[rows, :], mid[...]).astype(BF)

    part[...] = dkvf_ref[...].T
    backs = back_copies(part, rx, bs, br)
    for c in backs:
        c.start()
    spread1.begin()
    last = 3 * GR
    xT = x_ref[...].T
    red3.rows(0, nt(dqT_ref[last:, :], xT))
    red3.pair(0).start()
    red3.rows(3, nn(attT_ref[last:, :], go_ref[...]))
    red3.pair(3).start()
    for c in fetch:
        c.wait()
    mid[...] = (x_ref[...].astype(F32) + nn(attT_ref[...].T, wo_ref[...])).astype(BF)
    spot = lax.broadcasted_iota(jnp.int32, (T, T), 0)
    home[...] = (lax.broadcasted_iota(jnp.int32, (T, T), 1) == lax.rem(spot, RATE) * 64 + spot // RATE).astype(BF)
    add_back(backs, part, rx, 3, dk32_ref, dv32_ref, dk.at[last:D], dv.at[last:D])
    red2.start(red2.wave(0))
    red3.rows(1, nt(dk[last:D, :], xT))
    red3.pair(1).start()
    red3.rows(2, nt(dv[last:D, :], xT))
    red3.pair(2).start()
    spread1.middle()
    red3.add_pairs()
    red3.start(red3.wave(0))
    send_home(enc_ref)
    red2.after_first()
    e = nn(wq_ref[...], dqT_ref[...]) + nn(wk_ref[...], dk[...])
    red3.after_first()
    red2.after_second()
    spread1.end()
    e = e + nn(wv_ref[...], dv[...])
    red3.after_second()
    red2.after_third()
    spread2.begin()
    mid[...] = (go_ref[...].astype(F32) + e.T).astype(BF)
    red3.after_third()
    spread3.begin()
    spread2.middle()
    send_home(emb_ref)
    spread3.middle()
    spread2.end()
    spread3.end()
    red2.finish()
    red3.finish()
    for spread in (spread1, spread2, spread3):
        spread.finish()


def tail_all(*args):
    s = jax.ShapeDtypeStruct
    dma = pltpu.SemaphoreType.DMA
    older = reduction_scratch()
    return pl.pallas_call(
        tail_kernel,
        in_specs=[vm()] * 4 + [hbm()] * 2 + [vm()] * 5 + [hbm()] * 4,
        out_specs=[vm()] * 5,
        out_shape=[s((T, D), BF)] * 2 + [s((2, 4, GR, HALF), BF)] * 3,
        scratch_shapes=[
            pltpu.VMEM((D, D), BF), pltpu.VMEM((D, D), BF), pltpu.VMEM((D, D), BF), pltpu.VMEM((D, D), BF), dma((6,)),
            pltpu.VMEM((FAR, 2 * GR), BF), pltpu.VMEM((7, 64, 2 * GR), BF),
            pltpu.VMEM((D, T), BF), pltpu.VMEM((D, T), BF), pltpu.VMEM((3, 16, HALF), BF),
            pltpu.VMEM((3, 16, HALF), BF), pltpu.VMEM((T, T), BF), pltpu.VMEM((T, D), BF), dma((7,)), dma((7,)),
        ] + [dma((2, 3, 3)), dma((2, 3, 3)), dma(()), dma(())] * 3 + older[3:7] + older[9:] + reduction_scratch(),
        compiler_params=pltpu.CompilerParams(
            vmem_limit_bytes=60 << 20, collective_id=3, has_side_effects=True),
        cost_estimate=pl.CostEstimate(flops=16 * T * D * D, bytes_accessed=30 << 20, transcendentals=0),
    )(*args)


def lay_kernel(enc_ref, emb_ref, out0_ref, out1_ref, out2_ref, out3_ref,
               enc_out, emb_out, gq_ref, gk_ref, gv_ref, gout_ref, blocks, plain, stage, passing, ins, outs):
    copies = [pltpu.make_async_copy(enc_ref, enc_out, passing.at[0]),
              pltpu.make_async_copy(emb_ref, emb_out, passing.at[1])]
    loads = [pltpu.make_async_copy(o.at[:, i], blocks.at[i, :, g], ins.at[i, g])
             for i in range(4) for g, o in enumerate((out0_ref, out1_ref, out2_ref, out3_ref))]
    for c in loads + copies:
        c.start()
    for i, to in enumerate((gq_ref, gk_ref, gv_ref, gout_ref)):
        for g in range(4):
            loads[4 * i + g].wait()
            rows = slice(g * GR, (g + 1) * GR)
            target = plain if i < 3 else stage.at[i]
            target[rows, 0:HALF] = blocks[i, 0, g].astype(F32)
            target[rows, HALF:D] = blocks[i, 1, g].astype(F32)
        if i < 3:
            stage[i] = plain[...].T
        copies.append(pltpu.make_async_copy(stage.at[i], to, outs.at[i]))
        copies[-1].start()
    for c in copies:
        c.wait()


def lay_all(*args):
    s = jax.ShapeDtypeStruct
    dma = pltpu.SemaphoreType.DMA
    return pl.pallas_call(
        lay_kernel,
        in_specs=[hbm()] * 6,
        out_specs=[hbm()] * 6,
        out_shape=[s((T, D), BF)] * 2 + [s((D, D), F32)] * 4,
        scratch_shapes=[
            pltpu.VMEM((4, 2, 4, GR, HALF), BF), pltpu.VMEM((D, D), F32), pltpu.VMEM((4, D, D), F32),
            dma((2,)), dma((4, 4)), dma((4,)),
        ],
        compiler_params=pltpu.CompilerParams(vmem_limit_bytes=60 << 20),
        cost_estimate=pl.CostEstimate(flops=4 * D * D, bytes_accessed=24 * D * D, transcendentals=0),
    )(*args)


def per_device(tile_embed, tile_source, slide_len, grad_out, w_query, w_key, w_value, w_out):
    source = tile_source.reshape(1, T)
    length = slide_len[0]
    lens = jnp.stack([length - lax.axis_index("seq") * T, length]).astype(jnp.int32)
    x, go, k, v, qT, kT, vT, gT, far, kfT, vfT, top = front_all(
        lens, source, tile_embed[0], grad_out[0], w_query, w_key, w_value, w_out
    )
    attT, dqT, dk, dv, dk32, dv32, dkvf, fin, acc, out0 = attn(
        lens, k, v, qT, kT, vT, gT, far, kfT, vfT, top, x, go
    )
    enc, emb, out1, out2, out3 = tail_all(
        x, go, attT, dqT, dk, dv, dk32, dv32, dkvf, fin, acc, w_query, w_key, w_value, w_out
    )
    enc, emb, *summed = lay_all(enc, emb, out0, out1, out2, out3)
    return (enc[None], emb[None], summed[0], summed[1], summed[2], summed[3])


def solution(mesh):
    return jax.shard_map(
        per_device,
        mesh=mesh,
        in_specs=(
            P("rep", "seq", None),
            P("rep", "seq"),
            P("rep"),
            P("rep", "seq", None),
            P(),
            P(),
            P(),
            P(),
        ),
        out_specs=(P("rep", "seq", None), P("rep", "seq", None), P(), P(), P(), P()),
        check_vma=False,
    )
```

```python
import functools

import jax
import jax.numpy as jnp
from jax import lax
from jax.experimental import pallas as pl
from jax.experimental.pallas import tpu as pltpu
from jax.sharding import PartitionSpec as P

HEADS=16; RATE=16; HD=48; D=768; T=1024; FAR=512
BF=jnp.bfloat16; F32=jnp.float32
LOG2E=1.4426950408889634
NEG=-1e30
QC=512

def nn(a,b): return lax.dot_general(a,b,(((1,),(0,)),((),())),preferred_element_type=F32)
def nt(a,b): return lax.dot_general(a,b,(((1,),(1,)),((),())),preferred_element_type=F32)

def attn_kernel(len_ref, k_ref, v_ref, qT_ref, kT_ref, vT_ref, gT_ref, far_ref, kfT_ref, vfT_ref, top_ref, x_hbm, go_hbm,
                attT_ref, dqT_ref, dk_ref, dv_ref, dk32_ref, dv32_ref, dkvf_ref, fin_ref, acc_ref, out_ref,
                x_ref, go_ref, ins, qpad, gpad, kb, kfb, m2s, l2s, u2s, w2s, des, dqs, e2s,
                dk32, dv32, dkvf, xT, part, rx, sums, bs, br, gs, gr, hs, hr, *scratch):
    h = pl.program_id(0)
    step = lax.rem(h, 4)

    def reduction(g):
        return Reduction(scratch[0], *[ref.at[g] for ref in scratch[1:7]], fin_ref.at[g],
                         *[sem.at[g] for sem in scratch[7:]])

    def spread(g):
        return Spread(reduction(g), fin_ref.at[g], sums, gs, gr, hs, hr)

    def backs(g):
        return back_copies(part, rx.at[g], bs.at[g], br.at[g])

    now = jnp.maximum(h // 4 - 1, 0)
    before = jnp.maximum(h // 4 - 2, 0)
    low = pl.ds(pl.multiple_of(now * GR, 64), GR)

    fetch = [pltpu.make_async_copy(x_hbm, x_ref, ins.at[0]), pltpu.make_async_copy(go_hbm, go_ref, ins.at[1])]

    @pl.when(h == 0)
    def _():
        for c in fetch:
            c.start()
        greet(all_peers())

    @pl.when(h == 4)
    def _():
        for c in fetch:
            c.wait()
        xT[...] = x_ref[...].T

    @pl.when((step == 0) & (h >= 4))
    def _():
        part[...] = dkvf[lax.rem(now, 2)].T
        for c in backs(now):
            c.start()
        red = reduction(now)
        red.rows(0, nt(dqT_ref[low, :], xT[...]))
        red.pair(0).start()
        red.rows(3, nn(attT_ref[low, :], go_ref[...]))
        red.pair(3).start()

    @pl.when((step == 2) & (h >= 4))
    def _():
        slot = lax.rem(now, 2)
        add_back(backs(now), part, rx.at[now], now, dk32.at[slot], dv32.at[slot], dk_ref.at[low], dv_ref.at[low])
        red = reduction(now)
        red.rows(1, nt(dk_ref[low, :], xT[...]))
        red.pair(1).start()
        red.rows(2, nt(dv_ref[low, :], xT[...]))
        red.pair(2).start()

    @pl.when((step == 1) & (h >= 8))
    def _():
        reduction(before).after_first()

    @pl.when((step == 2) & (h >= 8))
    def _():
        reduction(before).after_second()

    @pl.when((step == 3) & (h >= 8))
    def _():
        reduction(before).after_third()

    @pl.when((step == 3) & (h >= 4))
    def _():
        reduction(now).add_pairs()

    @pl.when((step == 3) & (h >= 4) & (h < 12))
    def _():
        red = reduction(now)
        red.start(red.wave(0))

    @pl.when(h == 11)
    def _():
        spread(0).begin()

    @pl.when(h == 13)
    def _():
        spread(0).middle()

    @pl.when(h == 14)
    def _():
        spread(0).end()

    n = len_ref[0]
    nfull = len_ref[1]
    scale = HD ** -0.5
    c = scale * LOG2E
    w0, off, free = window(h)
    r = pl.multiple_of(h * HD, 16)
    row = lax.broadcasted_iota(jnp.int32, (256, T), 0)
    qpad[...] = pad_rows(qT_ref, w0, off, row, jnp.where(row == free, 1.0, 0.0).astype(BF))
    gpad[...] = pad_rows(gT_ref, w0, off, row, jnp.zeros((256, T), BF))
    lane = lax.broadcasted_iota(jnp.int32, (T, 256), 1)
    kb[...] = jnp.where(lane == free, key_bias(n), k_ref[:, pl.ds(w0, 256)])
    fi = lax.broadcasted_iota(jnp.int32, (FAR, 1), 0)
    fbias = jnp.where(fi * RATE + h < nfull, 0.0, NEG).astype(BF)
    flane = lax.broadcasted_iota(jnp.int32, (FAR, 256), 1)
    kfb[...] = jnp.where(flane == free, fbias, far_ref[:, pl.ds(w0, 256)])
    wq = pl.multiple_of((h // 2) * 128, 128)
    qlane = lax.broadcasted_iota(jnp.int32, (1, 128), 1)
    mine = (qlane // 64) == lax.rem(h, 2)
    S2 = nn(kfb[...], qpad[:, pl.ds(wq, 128)])
    x2 = jnp.max(S2, axis=0, keepdims=True)
    e2 = jnp.exp2(S2 * c - x2 * c)
    e2s[...] = e2
    l2 = jnp.sum(e2, axis=0, keepdims=True)
    u2 = nn(vfT_ref[pl.ds(r, HD), :], e2.astype(BF))
    m2s[...] = jnp.full_like(m2s, NEG)
    l2s[...] = jnp.zeros_like(l2s)
    u2s[...] = jnp.zeros_like(u2s)
    m2s[:, pl.ds(wq, 128)] = jnp.where(mine, x2 * scale, NEG)
    l2s[:, pl.ds(wq, 128)] = jnp.where(mine, l2, 0.0)
    u2s[:, pl.ds(wq, 128)] = jnp.where(mine, u2, 0.0)
    vwin = v_ref[:, pl.ds(w0, 256)]
    vTh = vT_ref[pl.ds(r, HD), :]
    kTh = kT_ref[pl.ds(r, HD), :]
    dv = jnp.zeros((HD, T), F32)
    dk = jnp.zeros((HD, T), F32)
    for ci in range(T // QC):
        sl = slice(ci * QC, (ci + 1) * QC)
        S = nn(kb[...], qpad[:, sl])
        x1 = top_ref[h, :, sl]
        e = jnp.exp2(S * c - x1 * c)
        l1 = jnp.sum(e, axis=0, keepdims=True)
        u1 = nn(vTh, e.astype(BF))
        m1 = x1 * scale
        m2 = m2s[:, sl]; l2c = l2s[:, sl]
        M = jnp.maximum(m1, m2)
        a1 = jnp.exp(m1 - M); a2 = jnp.exp(m2 - M)
        inv = 1.0 / (a1 * l1 + a2 * l2c)
        w1 = a1 * inv; w2 = a2 * inv
        o = u1 * w1 + u2s[:, sl] * w2
        qi = lax.broadcasted_iota(jnp.int32, (1, QC), 1) + ci * QC
        ok = (lax.rem(qi, 64) * RATE + qi // 64) < n
        attT_ref[pl.ds(r, HD), sl] = jnp.where(ok, o, 0.0).astype(BF)
        gTh = gT_ref[pl.ds(r, HD), sl]
        delta = jnp.sum(gTh.astype(F32) * o, axis=0, keepdims=True)
        w2s[:, sl] = w2
        des[:, sl] = delta
        dP = nn(vwin, gpad[:, sl])
        P = e * w1
        dS = (P * (dP - delta)).astype(BF)
        dqs[:, sl] = nn(kTh, dS)
        dv += nt(gTh, P.astype(BF))
        dk += nt(qT_ref[pl.ds(r, HD), sl], dS)
    r1 = pl.multiple_of(step * HD, 16)
    slot = lax.rem(h // 4, 2)
    dv32[slot, pl.ds(r1, HD), :] = dv
    dk32[slot, pl.ds(r1, HD), :] = dk * scale
    P2 = e2s[...] * jnp.where(mine, w2s[:, pl.ds(wq, 128)], 0.0)
    dP2 = nn(far_ref[:, pl.ds(pl.multiple_of(w0 + D, 128), 256)], gpad[:, pl.ds(wq, 128)])
    dS2 = (P2 * (dP2 - des[:, pl.ds(wq, 128)])).astype(BF)
    dvf = nt(gT_ref[pl.ds(r, HD), pl.ds(wq, 128)], P2.astype(BF)).astype(BF)
    dkf = (nt(qT_ref[pl.ds(r, HD), pl.ds(wq, 128)], dS2) * scale).astype(BF)

    dkvf[slot, pl.ds(r1, HD), :] = dkf
    dkvf[slot, pl.ds(pl.multiple_of(r1 + GR, 16), HD), :] = dvf
    dqs[:, pl.ds(wq, 128)] += nn(kfT_ref[pl.ds(r, HD), :], dS2)
    dqT_ref[pl.ds(r, HD), :] = (dqs[...] * scale).astype(BF)

    @pl.when(h == HEADS - 1)
    def _():
        dk32_ref[...] = dk32[1]
        dv32_ref[...] = dv32[1]
        dkvf_ref[...] = dkvf[1]
        acc_ref[...] = scratch[2][2]
        for g in range(2):
            reduction(g).finish()
        spread(0).finish()
        out_ref[...] = sums[...]


def attn(lens, *arrs):
    s = jax.ShapeDtypeStruct
    dma = pltpu.SemaphoreType.DMA
    return pl.pallas_call(
        attn_kernel,
        grid=(HEADS,),
        in_specs=[sm()] + [vm()] * 10 + [hbm()] * 2,
        out_specs=[vm()] * 10,
        out_shape=[s((D, T), BF)] * 2 + [s((3 * GR, T), BF)] * 2 + [s((GR, T), F32)] * 2 + [s((2 * GR, FAR), BF)]
        + [s((2, 3, 16, HALF), BF), s((4, GR, HALF), F32), s((2, 4, GR, HALF), BF)],
        scratch_shapes=[
            pltpu.VMEM((T, D), BF), pltpu.VMEM((T, D), BF), dma((2,)),
            pltpu.VMEM((256, T), BF), pltpu.VMEM((256, T), BF), pltpu.VMEM((T, 256), BF), pltpu.VMEM((FAR, 256), BF),
            pltpu.VMEM((1, T), F32), pltpu.VMEM((1, T), F32), pltpu.VMEM((HD, T), F32), pltpu.VMEM((1, T), F32),
            pltpu.VMEM((1, T), F32), pltpu.VMEM((HD, T), F32), pltpu.VMEM((FAR, 128), F32),
            pltpu.VMEM((2, GR, T), F32), pltpu.VMEM((2, GR, T), F32), pltpu.VMEM((2, 2 * GR, FAR), BF),
            pltpu.VMEM((D, T), BF), pltpu.VMEM((FAR, 2 * GR), BF), pltpu.VMEM((3, 7, 64, 2 * GR), BF),
            pltpu.VMEM((2, 4, GR, HALF), BF), dma((3, 7)), dma((3, 7)), dma((2, 3, 3)), dma((2, 3, 3)), dma(()), dma(()),
        ] + reduction_scratch(3),
        compiler_params=pltpu.CompilerParams(
            vmem_limit_bytes=60 << 20, collective_id=4, has_side_effects=True),
        cost_estimate=pl.CostEstimate(flops=100 * T * D * D, bytes_accessed=30 << 20, transcendentals=0),
    )(lens, *arrs)


def vm():
    return pl.BlockSpec(memory_space=pltpu.VMEM)


def hbm():
    return pl.BlockSpec(memory_space=pl.ANY)


def sm():
    return pl.BlockSpec(memory_space=pltpu.SMEM)


MESHID = pl.DeviceIdType.MESH
ORDERS = ((0, 1, 2), (1, 2, 0), (2, 0, 1))


def coords():
    s = lax.axis_index("seq")
    r = lax.axis_index("rep")
    return ((s % 2) * 2 + r // 8, s // 2, (r // 2) % 4), r % 2


def device_at(xyz, core):
    x, y, z = xyz
    return (y * 2 + x // 2, ((x % 2) * 4 + z) * 2 + core)


def along(xyz, axis, step):
    moved = list(xyz)
    moved[axis] = (xyz[axis] + step) % 4
    return tuple(moved)


def greet(peers):
    barrier = pltpu.get_barrier_semaphore()
    for peer in peers:
        pl.semaphore_signal(barrier, inc=1, device_id=peer, device_id_type=MESHID)
    pl.semaphore_wait(barrier, len(peers))


def send(src, dst, ssem, rsem, peer):
    copy = pltpu.make_async_remote_copy(
        src_ref=src, dst_ref=dst, send_sem=ssem, recv_sem=rsem, device_id=peer, device_id_type=MESHID
    )
    copy.start()
    return copy


def seq_peer(s, d):
    return (lax.rem(s + d, 8), lax.axis_index("rep"))


def window(h):
    hh = lax.rem(h, 8)
    w0 = pl.multiple_of((h // 8) * 384 + jnp.where(hh >= 5, 128, 0), 128)
    off = h * HD - w0
    return w0, off, jnp.where(off >= 48, 0, 255)


def pad_rows(ref, w0, off, rows_in, filler):
    return jnp.where((rows_in >= off) & (rows_in < off + HD), ref[pl.ds(w0, 256), :], filler)


def key_bias(n):
    ki = lax.broadcasted_iota(jnp.int32, (T, 1), 0)
    return jnp.where(lax.rem(ki, 64) * RATE + ki // 64 < n, 0.0, NEG).astype(BF)


def front_kernel(len_ref, src_ref, rows_ref, grad_hbm, wq_hbm, wk_hbm, wv_hbm, wo_hbm,
                 x_out, go_out, k_out, v_out, qT_out, kT_out, vT_out, gT_out, far_out, kfT_out, vfT_out, top_out,
                 x_ref, go_ref, k_ref, v_ref, qT_ref, kT_ref, vT_ref, gT_ref, far_ref, kfT_ref, vfT_ref, top_ref,
                 grad_ref, wq_ref, wk_ref, wv_ref, wo_ref,
                 ask, req, picked, arrived, perm, qpad, kb, ins, outs, qs, qr, ps, pr, fs, fr):
    n = len_ref[0]
    fetch = [pltpu.make_async_copy(a, b, ins.at[i]) for i, (a, b) in enumerate((
        (grad_hbm, grad_ref), (wo_hbm, wo_ref), (wk_hbm, wk_ref), (wv_hbm, wv_ref), (wq_hbm, wq_ref)))]
    for c in fetch:
        c.start()
    store = [pltpu.make_async_copy(a, b, outs.at[i]) for i, (a, b) in enumerate((
        (x_ref, x_out), (go_ref, go_out), (k_ref, k_out), (v_ref, v_out), (qT_ref, qT_out), (kT_ref, kT_out),
        (vT_ref, vT_out), (gT_ref, gT_out), (far_ref, far_out), (kfT_ref, kfT_out), (vfT_ref, vfT_out),
        (top_ref, top_out)))]
    s = lax.axis_index("seq")
    peers = [seq_peer(s, d) for d in range(1, 8)]
    greet(peers)
    src = src_ref[...]
    sixteen = lax.broadcasted_iota(jnp.int32, (16, T), 0)
    line = lax.rem(src, T)
    parts = jnp.where(sixteen == 0, line // 32, jnp.where(sixteen == 1, lax.rem(line, 32), src // T))
    spot = lax.broadcasted_iota(jnp.int32, (T, T), 0)
    reorder = (lax.broadcasted_iota(jnp.int32, (T, T), 1) == lax.rem(spot, 64) * RATE + spot // 64).astype(BF)
    parts = nt(parts.astype(F32).astype(BF), reorder)
    owner = parts[2:3].astype(jnp.int32)
    hot = (lax.broadcasted_iota(jnp.int32, (16, T), 0) == owner).astype(BF)
    before = (lax.broadcasted_iota(jnp.int32, (T, T), 0) < lax.broadcasted_iota(jnp.int32, (T, T), 1)).astype(BF)
    rank = jnp.sum(nn(hot, before) * hot.astype(F32), axis=0, keepdims=True)
    slot = owner.astype(F32) * 128.0 + rank
    where = lax.broadcasted_iota(jnp.int32, (T, T), 0).astype(F32)
    permT = (where == slot).astype(BF)
    got = nt(parts.astype(BF), permT)
    lines = got[0:1] * 32.0 + got[1:2]
    for o in range(8):
        ask[o] = jnp.broadcast_to(lines[:, o * 128:(o + 1) * 128], (8, 128))
    asks = [send(ask.at[lax.rem(s + d, 8)], req.at[d - 1], qs.at[d - 1], qr.at[d - 1], peers[d - 1])
            for d in range(1, 8)]
    perm[...] = permT.T
    qi = lax.broadcasted_iota(jnp.int32, (1, T), 1)
    ok = (lax.rem(qi, 64) * RATE + qi // 64) < n
    fetch[0].wait()
    fetch[1].wait()
    go_ref[...] = nn(reorder, grad_ref[...]).astype(BF)
    store[1].start()
    gT_ref[...] = jnp.where(ok, nt(wo_ref[...], go_ref[...]), 0.0).astype(BF)
    store[7].start()
    cells = lax.broadcasted_iota(jnp.int32, (128, T), 1).astype(F32)
    rows = rows_ref[...]
    mine = pl.ds(pl.multiple_of(s * 128, 128), 128)
    sends = []
    for d in range(1, 8):
        asks[d - 1].wait_recv()
        pick = (cells == req[d - 1].T[:, 0:1]).astype(BF)
        picked[d - 1] = nn(pick, rows).astype(BF)
        sends.append(send(picked.at[d - 1], arrived.at[mine], ps.at[d - 1], pr.at[d - 1], seq_peer(s, 8 - d)))
    pick = (cells == ask[s].T[:, 0:1]).astype(BF)
    arrived[mine, :] = nn(pick, rows).astype(BF)
    for c in sends:
        c.wait_recv()
    x = nn(perm[...], arrived[...]).astype(BF)
    x_ref[...] = x
    store[0].start()
    fetch[2].wait()
    fetch[3].wait()
    k = nn(x, wk_ref[...]).astype(BF)
    v = nn(x, wv_ref[...]).astype(BF)
    k_ref[...] = k
    v_ref[...] = v
    store[2].start()
    store[3].start()
    col = lax.broadcasted_iota(jnp.int32, (64, D), 1) // HD
    fk = jnp.zeros((64, D), BF)
    fv = jnp.zeros((64, D), BF)
    for h in range(HEADS):
        fk = jnp.where(col == h, k_ref[h * 64:(h + 1) * 64, :], fk)
        fv = jnp.where(col == h, v_ref[h * 64:(h + 1) * 64, :], fv)
    here = pl.ds(pl.multiple_of(s * 64, 64), 64)
    far_ref[here, 0:D] = fk
    far_ref[here, D:2 * D] = fv
    fars = [send(far_ref.at[here], far_ref.at[here], fs.at[d - 1], fr.at[d - 1], peers[d - 1]) for d in range(1, 8)]
    fetch[4].wait()
    qT_ref[...] = nn(x, wq_ref[...]).astype(BF).T
    store[4].start()
    kT_ref[...] = k.T
    store[5].start()
    vT_ref[...] = v.T
    store[6].start()
    rows_in = lax.broadcasted_iota(jnp.int32, (256, T), 0)
    cols_in = lax.broadcasted_iota(jnp.int32, (T, 256), 1)
    kbias = key_bias(n)

    @pl.loop(0, HEADS)
    def _(h):
        w0, off, free = window(h)
        qpad[...] = pad_rows(qT_ref, w0, off, rows_in, jnp.where(rows_in == free, 1.0, 0.0).astype(BF))
        kb[...] = jnp.where(cols_in == free, kbias, k_ref[:, pl.ds(w0, 256)])
        for ci in range(T // QC):
            sl = slice(ci * QC, (ci + 1) * QC)
            top_ref[h, :, sl] = jnp.max(nn(kb[...], qpad[:, sl]), axis=0, keepdims=True)

    store[11].start()
    for c in fars:
        c.wait_recv()
    store[8].start()
    kfT_ref[...] = far_ref[:, 0:D].T
    vfT_ref[...] = far_ref[:, D:2 * D].T
    store[9].start()
    store[10].start()
    for c in store:
        c.wait()
    for c in asks + sends + fars:
        c.wait_send()


def front_all(lens, src, rows, go, wq, wk, wv, wo):
    s = jax.ShapeDtypeStruct
    dma = pltpu.SemaphoreType.DMA
    return pl.pallas_call(
        front_kernel,
        in_specs=[sm()] + [vm()] * 2 + [hbm()] * 5,
        out_specs=[hbm()] * 12,
        out_shape=[s((T, D), BF)] * 4 + [s((D, T), BF)] * 4 + [s((FAR, 2 * D), BF)] + [s((D, FAR), BF)] * 2
        + [s((HEADS, 1, T), F32)],
        scratch_shapes=[pltpu.VMEM((T, D), BF)] * 4 + [pltpu.VMEM((D, T), BF)] * 4 + [
            pltpu.VMEM((FAR, 2 * D), BF), pltpu.VMEM((D, FAR), BF), pltpu.VMEM((D, FAR), BF),
            pltpu.VMEM((HEADS, 1, T), F32), pltpu.VMEM((T, D), BF), pltpu.VMEM((D, D), BF), pltpu.VMEM((D, D), BF),
            pltpu.VMEM((D, D), BF), pltpu.VMEM((D, D), BF),
            pltpu.VMEM((8, 8, 128), F32), pltpu.VMEM((7, 8, 128), F32), pltpu.VMEM((7, 128, D), BF),
            pltpu.VMEM((T, D), BF), pltpu.VMEM((T, T), BF), pltpu.VMEM((256, T), BF), pltpu.VMEM((T, 256), BF),
        dma((5,)), dma((12,)),
        ] + [dma((7,))] * 6,
        compiler_params=pltpu.CompilerParams(
            vmem_limit_bytes=60 << 20, collective_id=2, has_side_effects=True),
        cost_estimate=pl.CostEstimate(flops=12 * T * D * D, bytes_accessed=20 << 20, transcendentals=0),
    )(lens, src, rows, go, wq, wk, wv, wo)


HALF = D // 2
GH = HEADS // 4
GR = GH * HD


def copy_to(src, dst, ssem, rsem, peer):
    return pltpu.make_async_remote_copy(
        src_ref=src, dst_ref=dst, send_sem=ssem, recv_sem=rsem, device_id=peer, device_id_type=MESHID
    )


def all_peers():
    xyz, core = coords()
    s = lax.axis_index("seq")
    near = [device_at(along(xyz, 0, d), core) for d in (1, 3)] + [device_at(along(xyz, 2, d), core) for d in (1, 2, 3)]
    return [seq_peer(s, d) for d in range(1, 8)] + near + [device_at(xyz, 1 - core)]


class Reduction:
    def __init__(self, grads, crx, acc, rx1, rx2, rx3, r2, fin, cs, cr, ss, rs):
        self.xyz, self.core = coords()
        self.grads, self.crx, self.acc = grads, crx, acc
        self.rx1, self.rx2, self.rx3, self.r2, self.fin = rx1, rx2, rx3, r2, fin
        self.cs, self.cr, self.ss, self.rs = cs, cr, ss, rs

    def at(self, p, level):
        return self.xyz[ORDERS[p][level]]

    def peer(self, p, level, d):
        return device_at(along(self.xyz, ORDERS[p][level], d), self.core)

    def pair(self, i):
        return copy_to(self.grads.at[i, 1 - self.core], self.crx.at[i], self.cs.at[i], self.cr.at[i],
                       device_at(self.xyz, 1 - self.core))

    def wave(self, level, parts=(0, 1, 2)):
        made = []
        for p in parts:
            for d in (1, 2, 3):
                other = (self.at(p, level) + d) % 4
                if level == 0:
                    src, dst = self.acc.at[other, pl.ds(p * 64, 64)], self.rx1.at[p, d - 1]
                elif level == 1:
                    src, dst = self.r2.at[p, pl.ds(pl.multiple_of(other * 16, 16), 16)], self.rx2.at[p, d - 1]
                else:
                    own = self.rx3.at[p, self.at(p, 2)]
                    src, dst = own, own
                made.append(copy_to(src, dst, self.ss.at[level, p, d - 1], self.rs.at[level, p, d - 1],
                                    self.peer(p, level, d)))
        return made

    def start(self, copies):
        for c in copies:
            c.start()

    def rows(self, i, value):
        self.grads[i, 0] = value[:, :HALF]
        self.grads[i, 1] = value[:, HALF:]

    def add_pairs(self):
        for i in (0, 3, 1, 2):
            self.pair(i).wait_recv()
            self.acc[i] = self.grads[i, self.core] + self.crx[i]
        for i in range(4):
            self.pair(i).wait_send()

    def after_first(self):
        copies = self.wave(0)
        for p in range(3):
            for c in copies[3 * p:3 * p + 3]:
                c.wait_recv()
            self.r2[p] = self.acc[self.at(p, 0), p * 64:(p + 1) * 64] + self.rx1[p, 0] + self.rx1[p, 1] + self.rx1[p, 2]
            self.start(self.wave(1, (p,)))

    def after_second(self):
        copies = self.wave(1)
        for p in range(3):
            for c in copies[3 * p:3 * p + 3]:
                c.wait_recv()
            own = self.r2[p, pl.ds(pl.multiple_of(self.at(p, 1) * 16, 16), 16)]
            self.rx3[p, self.at(p, 2)] = own + self.rx2[p, 0] + self.rx2[p, 1] + self.rx2[p, 2]
            self.start(self.wave(2, (p,)))

    def after_third(self):
        copies = self.wave(2)
        for p in range(3):
            for c in copies[3 * p:3 * p + 3]:
                c.wait_recv()
            self.fin[p] = (self.rx3[p, 0] + self.rx3[p, 1] + self.rx3[p, 2] + self.rx3[p, 3]).astype(BF)

    def finish(self):
        for level in range(3):
            for c in self.wave(level):
                c.wait_send()


def reduction_scratch(*groups):
    dma = pltpu.SemaphoreType.DMA
    return [
        pltpu.VMEM((4, 2, GR, HALF), F32), pltpu.VMEM(groups + (4, GR, HALF), F32),
        pltpu.VMEM(groups + (4, GR, HALF), F32), pltpu.VMEM(groups + (3, 3, 64, HALF), F32),
        pltpu.VMEM(groups + (3, 3, 16, HALF), F32), pltpu.VMEM(groups + (3, 4, 16, HALF), F32),
        pltpu.VMEM(groups + (3, 64, HALF), F32), dma(groups + (4,)), dma(groups + (4,)),
        dma(groups + (3, 3, 3)), dma(groups + (3, 3, 3)),
    ]


class Spread:
    def __init__(self, red, fin, out, gs, gr, hs, hr):
        self.red, self.fin, self.out, self.gs, self.gr, self.hs, self.hr = red, fin, out, gs, gr, hs, hr

    def wave(self, level, parts=(0, 1, 2)):
        made = []
        for p in parts:
            a, b = self.red.at(p, 0), self.red.at(p, 1)
            rows = pl.ds(pl.multiple_of(p * 64 + b * 16, 16), 16) if level == 1 else pl.ds(p * 64, 64)
            here = self.out.at[self.red.core, a, rows]
            for d in (1, 2, 3):
                made.append(copy_to(here, here, self.gs.at[level, p, d - 1], self.gr.at[level, p, d - 1],
                                    self.red.peer(p, level, d)))
        return made

    def mate(self):
        here = self.out.at[self.red.core]
        return copy_to(here, here, self.hs, self.hr, device_at(self.red.xyz, 1 - self.red.core))

    def begin(self):
        for p in range(3):
            rows = pl.ds(pl.multiple_of(p * 64 + self.red.at(p, 1) * 16, 16), 16)
            self.out[self.red.core, self.red.at(p, 0), rows] = self.fin[p]
        for c in self.wave(1):
            c.start()

    def middle(self):
        for p in range(3):
            for c in self.wave(1, (p,)):
                c.wait_recv()
            for c in self.wave(0, (p,)):
                c.start()

    def end(self):
        for c in self.wave(0):
            c.wait_recv()
        self.mate().start()

    def finish(self):
        for level in range(2):
            for c in self.wave(level):
                c.wait_send()
        self.mate().wait()


def back_copies(part, rx, ss, rs):
    s = lax.axis_index("seq")
    return [copy_to(part.at[pl.ds(pl.multiple_of(lax.rem(s + d, 8) * 64, 64), 64)], rx.at[d - 1],
                    ss.at[d - 1], rs.at[d - 1], seq_peer(s, d)) for d in range(1, 8)]


def add_back(copies, part, rx, group, dk32, dv32, dk, dv):
    s = lax.axis_index("seq")
    back = part[pl.ds(pl.multiple_of(s * 64, 64), 64), :].astype(F32)
    for d in range(1, 8):
        copies[d - 1].wait_recv()
        back = back + rx[d - 1].astype(F32)
    for c in copies:
        c.wait_send()
    bT = back.T
    zero = jnp.zeros((HD, 64), F32)
    for i in range(GH):
        r = slice(i * HD, (i + 1) * HD)
        w = pl.ds(pl.multiple_of((group * 2 + i // 2) * 128, 128), 128)
        bk = bT[i * HD:(i + 1) * HD, :]
        bv = bT[GR + i * HD:GR + (i + 1) * HD, :]
        pk = [bk, zero] if i % 2 == 0 else [zero, bk]
        pv = [bv, zero] if i % 2 == 0 else [zero, bv]
        dk[r, :] = dk32[r, :].astype(BF)
        dv[r, :] = dv32[r, :].astype(BF)
        dk[r, w] = (dk32[r, w] + jnp.concatenate(pk, axis=1)).astype(BF)
        dv[r, w] = (dv32[r, w] + jnp.concatenate(pv, axis=1)).astype(BF)


def tail_kernel(x_ref, go_ref, attT_ref, dqT_ref, dk_ref, dv_ref, dk32_ref, dv32_ref, dkvf_ref, fin_ref, acc_ref,
                wq_hbm, wk_hbm, wv_hbm, wo_hbm, enc_ref, emb_ref, out1_ref, out2_ref, out3_ref,
                wq_ref, wk_ref, wv_ref, wo_ref, ins, part, rx, dk, dv, fin2, fin3, home, mid, bs, br, *scratch):
    fetch = [pltpu.make_async_copy(a, b, ins.at[i]) for i, (a, b) in enumerate((
        (dk_ref, dk.at[pl.ds(0, 3 * GR)]), (dv_ref, dv.at[pl.ds(0, 3 * GR)]), (wo_hbm, wo_ref), (wq_hbm, wq_ref),
        (wk_hbm, wk_ref), (wv_hbm, wv_ref)))]
    for c in fetch:
        c.start()
    greet(all_peers())
    sems, older, newer = scratch[:12], scratch[12:18], scratch[18:]
    red2 = Reduction(None, None, acc_ref, *older[:4], fin2, None, None, *older[4:])
    red3 = Reduction(*newer[:7], fin3, *newer[7:])
    spread1 = Spread(red2, fin_ref.at[1], out1_ref, *sems[0:4])
    spread2 = Spread(red2, fin2, out2_ref, *sems[4:8])
    spread3 = Spread(red3, fin3, out3_ref, *sems[8:12])

    def send_home(to):
        @pl.loop(0, 4)
        def _(i):
            rows = pl.ds(pl.multiple_of(i * 256, 256), 256)
            to[rows, :] = nn(home[rows, :], mid[...]).astype(BF)

    part[...] = dkvf_ref[...].T
    backs = back_copies(part, rx, bs, br)
    for c in backs:
        c.start()
    spread1.begin()
    last = 3 * GR
    xT = x_ref[...].T
    red3.rows(0, nt(dqT_ref[last:, :], xT))
    red3.pair(0).start()
    red3.rows(3, nn(attT_ref[last:, :], go_ref[...]))
    red3.pair(3).start()
    for c in fetch:
        c.wait()
    mid[...] = (x_ref[...].astype(F32) + nn(attT_ref[...].T, wo_ref[...])).astype(BF)
    spot = lax.broadcasted_iota(jnp.int32, (T, T), 0)
    home[...] = (lax.broadcasted_iota(jnp.int32, (T, T), 1) == lax.rem(spot, RATE) * 64 + spot // RATE).astype(BF)
    add_back(backs, part, rx, 3, dk32_ref, dv32_ref, dk.at[last:D], dv.at[last:D])
    red2.start(red2.wave(0))
    red3.rows(1, nt(dk[last:D, :], xT))
    red3.pair(1).start()
    red3.rows(2, nt(dv[last:D, :], xT))
    red3.pair(2).start()
    spread1.middle()
    red3.add_pairs()
    red3.start(red3.wave(0))
    send_home(enc_ref)
    red2.after_first()
    e = nn(wq_ref[...], dqT_ref[...]) + nn(wk_ref[...], dk[...])
    red3.after_first()
    red2.after_second()
    spread1.end()
    e = e + nn(wv_ref[...], dv[...])
    red3.after_second()
    red2.after_third()
    spread2.begin()
    mid[...] = (go_ref[...].astype(F32) + e.T).astype(BF)
    red3.after_third()
    spread3.begin()
    spread2.middle()
    send_home(emb_ref)
    spread3.middle()
    spread2.end()
    spread3.end()
    red2.finish()
    red3.finish()
    for spread in (spread1, spread2, spread3):
        spread.finish()


def tail_all(*args):
    s = jax.ShapeDtypeStruct
    dma = pltpu.SemaphoreType.DMA
    older = reduction_scratch()
    return pl.pallas_call(
        tail_kernel,
        in_specs=[vm()] * 4 + [hbm()] * 2 + [vm()] * 5 + [hbm()] * 4,
        out_specs=[vm()] * 5,
        out_shape=[s((T, D), BF)] * 2 + [s((2, 4, GR, HALF), BF)] * 3,
        scratch_shapes=[
            pltpu.VMEM((D, D), BF), pltpu.VMEM((D, D), BF), pltpu.VMEM((D, D), BF), pltpu.VMEM((D, D), BF), dma((6,)),
            pltpu.VMEM((FAR, 2 * GR), BF), pltpu.VMEM((7, 64, 2 * GR), BF),
            pltpu.VMEM((D, T), BF), pltpu.VMEM((D, T), BF), pltpu.VMEM((3, 16, HALF), BF),
            pltpu.VMEM((3, 16, HALF), BF), pltpu.VMEM((T, T), BF), pltpu.VMEM((T, D), BF), dma((7,)), dma((7,)),
        ] + [dma((2, 3, 3)), dma((2, 3, 3)), dma(()), dma(())] * 3 + older[3:7] + older[9:] + reduction_scratch(),
        compiler_params=pltpu.CompilerParams(
            vmem_limit_bytes=60 << 20, collective_id=3, has_side_effects=True),
        cost_estimate=pl.CostEstimate(flops=16 * T * D * D, bytes_accessed=30 << 20, transcendentals=0),
    )(*args)


def lay_kernel(enc_ref, emb_ref, out0_ref, out1_ref, out2_ref, out3_ref,
               enc_out, emb_out, gq_ref, gk_ref, gv_ref, gout_ref, blocks, plain, stage, held, taking, passing, ins, outs):
    takes = [pltpu.make_async_copy(enc_ref, held.at[0], taking.at[0]),
             pltpu.make_async_copy(emb_ref, held.at[1], taking.at[1])]
    copies = [pltpu.make_async_copy(held.at[0], enc_out, passing.at[0]),
              pltpu.make_async_copy(held.at[1], emb_out, passing.at[1])]
    loads = [pltpu.make_async_copy(o.at[:, i], blocks.at[i, :, g], ins.at[i, g])
             for i in range(4) for g, o in enumerate((out0_ref, out1_ref, out2_ref, out3_ref))]
    for c in loads + takes:
        c.start()
    for i, to in enumerate((gq_ref, gk_ref, gv_ref, gout_ref)):
        for g in range(4):
            loads[4 * i + g].wait()
            rows = slice(g * GR, (g + 1) * GR)
            target = plain if i < 3 else stage.at[i]
            target[rows, 0:HALF] = blocks[i, 0, g].astype(F32)
            target[rows, HALF:D] = blocks[i, 1, g].astype(F32)
        if i < 3:
            stage[i] = plain[...].T
        copies.append(pltpu.make_async_copy(stage.at[i], to, outs.at[i]))
        copies[-1].start()
        if i < 2:
            takes[i].wait()
            copies[i].start()
    for c in copies:
        c.wait()


def lay_all(*args):
    s = jax.ShapeDtypeStruct
    dma = pltpu.SemaphoreType.DMA
    return pl.pallas_call(
        lay_kernel,
        in_specs=[hbm()] * 6,
        out_specs=[hbm()] * 6,
        out_shape=[s((T, D), BF)] * 2 + [s((D, D), F32)] * 4,
        scratch_shapes=[
            pltpu.VMEM((4, 2, 4, GR, HALF), BF), pltpu.VMEM((D, D), F32), pltpu.VMEM((4, D, D), F32),
            pltpu.VMEM((2, T, D), BF), dma((2,)), dma((2,)), dma((4, 4)), dma((4,)),
        ],
        compiler_params=pltpu.CompilerParams(vmem_limit_bytes=60 << 20),
        cost_estimate=pl.CostEstimate(flops=4 * D * D, bytes_accessed=24 * D * D, transcendentals=0),
    )(*args)


def per_device(tile_embed, tile_source, slide_len, grad_out, w_query, w_key, w_value, w_out):
    source = tile_source.reshape(1, T)
    length = slide_len[0]
    lens = jnp.stack([length - lax.axis_index("seq") * T, length]).astype(jnp.int32)
    x, go, k, v, qT, kT, vT, gT, far, kfT, vfT, top = front_all(
        lens, source, tile_embed[0], grad_out[0], w_query, w_key, w_value, w_out
    )
    attT, dqT, dk, dv, dk32, dv32, dkvf, fin, acc, out0 = attn(
        lens, k, v, qT, kT, vT, gT, far, kfT, vfT, top, x, go
    )
    enc, emb, out1, out2, out3 = tail_all(
        x, go, attT, dqT, dk, dv, dk32, dv32, dkvf, fin, acc, w_query, w_key, w_value, w_out
    )
    enc, emb, *summed = lay_all(enc, emb, out0, out1, out2, out3)
    return (enc[None], emb[None], summed[0], summed[1], summed[2], summed[3])


def solution(mesh):
    return jax.shard_map(
        per_device,
        mesh=mesh,
        in_specs=(
            P("rep", "seq", None),
            P("rep", "seq"),
            P("rep"),
            P("rep", "seq", None),
            P(),
            P(),
            P(),
            P(),
        ),
        out_specs=(P("rep", "seq", None), P("rep", "seq", None), P(), P(), P(), P()),
        check_vma=False,
    )
```
